32 devices in a mesh: seg: 4 (over z), pair: 8 (over y, x, core).
Axes of the slice: x: 2, y: 2, z: 4, core: 2. Of those that a mesh axis runs over, the one named last changes fastest.
Arguments:
- spectra: bfloat16 [4, 2, 2048, 2048], P('seg', None, None, 'pair'), may hold values from -6 to 6
- pair_lists: int32 [32, 2], P('pair'), may hold values from 0 to 15
- pair_counts: int32 [8], P('pair'), may hold values from 1 to 4, as said below
Outputs:
- correlations: float32 [2048, 32, 128], P('seg', 'pair')
The draws below stay inside these ranges and needn't reach their ends.
Inputs may be any that keep to these rules, and one draw needn't show every extreme that they name: `pair_counts`: some owner uses exactly 4 slots.
All inputs are finite; a program needn't handle non-finite values.
Results may differ from the reference program's by a relative error of at most 0.0003.
Values may be sent and summed in bfloat16 or wider, within the bound.
No kernel may reach another device: no remote copies, remote signals or barrier semaphores. Data moves between devices by JAX's collectives and lax.ppermute only.
A program may use at most 128 MiB of HBM per device.

```python
import math
import jax
import jax.numpy as jnp
from jax import lax

TILE = 128
F = 2048
LAG = 2048
MOST = 4
SEGS = 4
OWNERS = 8
TILES = 16
CH = 2048
PAIR_SLOTS = 32


def draw_pair_counts(key, part):
    first_key, second_key = jax.random.split(jax.random.fold_in(key, 7))
    base_counts = jax.random.randint(first_key, (OWNERS,), 1, MOST // 2 + 1)
    fullest = jax.random.randint(second_key, (), 0, OWNERS)
    return jnp.where(jnp.arange(OWNERS) == fullest, MOST, base_counts).astype(jnp.int32)


def touch_ends(array, rng, low, largest):
    longest = array.shape.index(max(array.shape))
    spots = []
    for shift in (0, 1):
        where = [jax.random.randint(jax.random.fold_in(rng, axis), (), 0, length) for axis, length in enumerate(array.shape)]
        where[longest] = (where[longest] + shift) % array.shape[longest]
        spots.append(tuple(where))
    return array.at[spots[0]].set(low).at[spots[1]].set(largest)


def shard_levels(rng, extent, shards, low, top_value):
    gain = 1.0
    for dim, blocks in shards:
        steps = jax.random.uniform(jax.random.fold_in(jax.random.fold_in(rng, 6), dim), (blocks,), jnp.float32, low / len(shards), top_value / len(shards))
        gain = gain * jnp.repeat(jnp.exp(steps), extent[dim] // blocks).reshape((-1,) + (1,) * (len(extent) - 1 - dim))
    return gain


def gaussian(rng, shape, spread, reach, cuts=(), held_as=jnp.bfloat16):
    drawn = jax.random.normal(rng, shape, jnp.float32) * spread
    if len(cuts) > 0:
        drawn = shard_levels(rng, shape, cuts, -0.22, 0.18) * drawn
    return jnp.clip(drawn, min=-reach, max=reach).astype(held_as)


def setup_inputs(seed: int = 0) -> dict:
    key_list = jax.random.split(jax.random.key(seed), 4)
    return {
        "spectra": gaussian(key_list[0], (SEGS, 2, F, CH), 1.0, 6.0, ((0, 4), (3, 8))),
        "pair_lists": touch_ends(jax.random.randint(key_list[1], (PAIR_SLOTS, 2), 0, TILES), jax.random.fold_in(key_list[1], 1), 0, TILES - 1).astype(jnp.int32),
        "pair_counts": draw_pair_counts(jax.random.fold_in(key_list[3], 71), 0),
    }


def reference(spectra, pair_lists, pair_counts):
    source_ids = pair_lists[:, 0]
    receiver_ids = pair_lists[:, 1]
    tiled_spec = spectra.reshape(SEGS, 2, F, TILES, TILE)

    def one_segment(totals, segment):
        source_spec = jnp.take(segment, source_ids, axis=2).astype(jnp.float32)
        recv_spec = jnp.take(segment, receiver_ids, axis=2).astype(jnp.float32)
        cross_re = source_spec[0] * recv_spec[0] + source_spec[1] * recv_spec[1]
        cross_im = source_spec[1] * recv_spec[0] - source_spec[0] * recv_spec[1]
        magnitude = jnp.sqrt(cross_re * cross_re + cross_im * cross_im + 1.0)
        return ((totals[0] + cross_re, totals[1] + cross_im, totals[2] + cross_re / magnitude, totals[3] + cross_im / magnitude), None)
    zeros = jnp.zeros((F, PAIR_SLOTS, TILE), jnp.float32)
    sums, _ = lax.scan(one_segment, (zeros, zeros, zeros, zeros), tiled_spec)
    linear_re, linear_im, phase_re, phase_im = sums
    slot_index = jnp.arange(PAIR_SLOTS, dtype=jnp.int32)
    live_mask = (slot_index % MOST < pair_counts[slot_index // MOST]).astype(jnp.float32)
    weight = (phase_re * phase_re + phase_im * phase_im) / float(SEGS * SEGS)
    stack_re = (linear_re * weight * live_mask[None, :, None]).reshape(F, PAIR_SLOTS * TILE)
    stack_im = (linear_im * weight * live_mask[None, :, None]).reshape(F, PAIR_SLOTS * TILE)
    lag_offset = jnp.arange(LAG, dtype=jnp.int32) - LAG // 2
    bin_index = jnp.arange(F, dtype=jnp.int32)
    product = lag_offset[:, None] * bin_index[None, :] % (2 * F)
    angles = product.astype(jnp.float32) * jnp.float32(math.pi / F)
    result = jnp.dot(jnp.cos(angles), stack_re, precision=lax.Precision.HIGHEST, preferred_element_type=jnp.float32)
    result = result - jnp.dot(jnp.sin(angles), stack_im, precision=lax.Precision.HIGHEST, preferred_element_type=jnp.float32)
    result = result * jnp.float32(1.0 / math.sqrt(F))
    return result.reshape(LAG, PAIR_SLOTS, TILE)
```

```python
import functools
import math

import jax
import jax.numpy as jnp
import numpy as np
from jax import lax
from jax.experimental import pallas as pl
from jax.experimental.pallas import tpu as pltpu
from jax.sharding import PartitionSpec as P

TILE = 128
LAG = 2048
GROUPS = 8
CC = TILE // GROUPS


def lane_groups(shape):
    return lax.broadcasted_iota(jnp.int32, shape, len(shape) - 1) // CC


def shift_groups(x, by):
    return pltpu.roll(x, (by * CC) % TILE, x.ndim - 1)


def transpose_groups(vectors):
    v = list(vectors)
    grp = lane_groups(v[0].shape)
    for bit in (4, 2, 1):
        low = (grp & bit) == 0
        for i in range(GROUPS):
            if i & bit:
                continue
            a, b = v[i], v[i | bit]
            v[i] = jnp.where(low, a, shift_groups(b, bit))
            v[i | bit] = jnp.where(low, shift_groups(a, -bit), b)
    return v


def reduce_groups(vectors):
    v = list(vectors)
    grp = lane_groups(v[0].shape)
    low = (grp & 4) == 0
    v = [
        jnp.where(low, v[i], v[i + 4])
        + shift_groups(jnp.where(low, v[i + 4], v[i]), 4)
        for i in range(4)
    ]
    for bit in (2, 1):
        low = (grp & bit) == 0
        v = [
            jnp.where(low, v[i], v[i + bit])
            + jnp.where(low, shift_groups(v[i], -bit), shift_groups(v[i + bit], bit))
            for i in range(bit)
        ]
    return v[0]


def pack_kernel(n_seg, n_pair, x_ref, sel_ref, out_ref, buf_ref):
    freq = x_ref.shape[1]
    tiles = out_ref.shape[2]
    rows = out_ref.shape[4]
    band = freq // n_pair
    wide = sel_ref.shape[1]

    def one(step, _):
        ri, p = step // n_pair, step % n_pair
        block = x_ref[ri, pl.ds(pl.multiple_of(p * band, band), band), :]
        for part in range(wide // TILE):
            buf_ref[...] = jnp.dot(
                block,
                sel_ref[:, part * TILE : (part + 1) * TILE],
                preferred_element_type=jnp.float32,
            )
            v = [buf_ref[pl.ds(fb, rows, stride=GROUPS), :] for fb in range(GROUPS)]
            v = transpose_groups(v)
            for g in range(GROUPS):
                t, z = divmod(part * GROUPS + g, n_seg)
                out_ref[z, p, t, ri] = v[g].astype(jnp.bfloat16)
        return 0

    lax.fori_loop(0, 2 * n_pair, one, 0)


def pack(x, chunk, n_seg, n_pair):
    _, freq, chans = x.shape
    tiles = chans // TILE
    rows = freq // n_pair // GROUPS
    wide = tiles * n_seg * CC
    sel = np.zeros((chans, wide), np.float32)
    for t in range(tiles):
        for z in range(n_seg):
            for c in range(CC):
                src = t * TILE + z * (TILE // n_seg) + chunk * CC + c
                sel[src, (t * n_seg + z) * CC + c] = 1.0
    return pl.pallas_call(
        functools.partial(pack_kernel, n_seg, n_pair),
        out_shape=jax.ShapeDtypeStruct(
            (n_seg, n_pair, tiles, 2, rows, TILE), jnp.bfloat16
        ),
        in_specs=[pl.BlockSpec(memory_space=pltpu.VMEM)] * 2,
        out_specs=pl.BlockSpec(memory_space=pltpu.VMEM),
        scratch_shapes=[pltpu.VMEM((freq // n_pair, TILE), jnp.float32)],
        name="pack",
        cost_estimate=pl.CostEstimate(
            flops=4 * freq * chans * wide,
            bytes_accessed=x.size * 2 + 2 * freq * wide * 2,
            transcendentals=0,
        ),
    )(x, jnp.asarray(sel, jnp.bfloat16))


def stack_kernel(n_seg, n_pair, most, me_ref, table_ref, spec_ref, *out_refs):
    inv = 1.0 / float(n_seg * n_seg)
    for k in range(n_pair):
        owner = jnp.bitwise_xor(me_ref[1], k)
        count = table_ref[owner, 2 * most]
        out_ref = out_refs[k]

        def one(s, _):
            src = table_ref[owner, 2 * s]
            rcv = table_ref[owner, 2 * s + 1]

            @pl.when(s < count)
            def _():
                lr = li = pr = pi = None
                for g in range(n_seg):
                    a0 = spec_ref[g, src, 0].astype(jnp.float32)
                    a1 = spec_ref[g, src, 1].astype(jnp.float32)
                    b0 = spec_ref[g, rcv, 0].astype(jnp.float32)
                    b1 = spec_ref[g, rcv, 1].astype(jnp.float32)
                    cr = a0 * b0 + a1 * b1
                    ci = a1 * b0 - a0 * b1
                    m = lax.rsqrt(cr * cr + ci * ci + 1.0)
                    if g == 0:
                        lr, li, pr, pi = cr, ci, cr * m, ci * m
                    else:
                        lr, li, pr, pi = lr + cr, li + ci, pr + cr * m, pi + ci * m
                w = (pr * pr + pi * pi) * inv
                out_ref[s, 0] = lr * w
                out_ref[s, 1] = li * w

            @pl.when(s >= count)
            def _():
                out_ref[s] = jnp.zeros(out_ref.shape[1:], jnp.float32)

            return 0

        lax.fori_loop(0, most, one, 0)


def stacks(me, table, spec, n_seg, n_pair, most):
    rows = spec.shape[3]
    shape = (most, 2, rows, TILE)
    smem = pl.BlockSpec(memory_space=pltpu.SMEM)
    vmem = pl.BlockSpec(memory_space=pltpu.VMEM)
    return pl.pallas_call(
        functools.partial(stack_kernel, n_seg, n_pair, most),
        out_shape=[jax.ShapeDtypeStruct(shape, jnp.float32)] * n_pair,
        in_specs=[smem, smem, vmem],
        out_specs=[vmem] * n_pair,
        name="stack",
        cost_estimate=pl.CostEstimate(
            flops=n_pair * most * rows * TILE * n_seg * 20,
            bytes_accessed=spec.size * 2 + n_pair * most * 2 * rows * TILE * 4,
            transcendentals=n_pair * most * rows * TILE * n_seg,
        ),
    )(me, table, spec)


def dft_kernel(n_seg, n_pair, most, me_ref, whi_ref, wlo_ref, cos_ref, sin_ref, turn_ref, *refs):
    ins = refs[:n_pair]
    outs = refs[n_pair : n_pair + n_seg]
    s32, shi, slo, y = refs[n_pair + n_seg :]
    rows = ins[0].shape[2]
    half_h = s32.shape[0] // 2
    for k in range(n_pair):
        band = jnp.bitwise_xor(me_ref[1], k)
        for s in range(most):
            for ri in range(2):
                at = pl.multiple_of(ri * half_h + band * rows, rows)
                s32[pl.ds(at, rows), s * TILE : (s + 1) * TILE] = ins[k][s, ri]
    full = s32[...]
    hi = full.astype(jnp.bfloat16)
    shi[...] = hi
    slo[...] = (full - hi.astype(jnp.float32)).astype(jnp.bfloat16)
    for m in range(whi_ref.shape[0]):
        y[m] = (
            jnp.dot(wlo_ref[m], shi[...], preferred_element_type=jnp.float32)
            + jnp.dot(whi_ref[m], slo[...], preferred_element_type=jnp.float32)
        ) + jnp.dot(whi_ref[m], shi[...], preferred_element_type=jnp.float32)
    period = y.shape[1]
    half = outs[0].shape[0]
    step_rows = 16
    for k in range(n_seg):
        dest = jnp.bitwise_xor(me_ref[0], k)
        out_ref = outs[k]

        def one(b, _):
            v = []
            for h in range(2):
                lag = dest * (2 * half) + h * half + b * step_rows
                l0 = pl.multiple_of(lax.rem(lag, period), step_rows)
                c0 = cos_ref[pl.ds(l0, step_rows), :]
                d0 = sin_ref[pl.ds(l0, step_rows), :]
                ct = turn_ref[0, lag // period]
                dt = turn_ref[1, lag // period]
                c = c0 * ct - d0 * dt
                d = d0 * ct + c0 * dt
                for s in range(most):
                    lanes = slice(s * TILE, (s + 1) * TILE)
                    v.append(
                        c * y[0, pl.ds(l0, step_rows), lanes]
                        - d * y[1, pl.ds(l0, step_rows), lanes]
                    )
            at = pl.multiple_of(b * step_rows, step_rows)
            out_ref[pl.ds(at, step_rows), :] = reduce_groups(v)
            return 0

        lax.fori_loop(0, half // step_rows, one, 0)


def dft(me, blocks, freq, n_seg, n_pair, most):
    h = freq // GROUPS
    period = 2 * h
    turn = (np.arange(period)[:, None] * np.arange(h)[None, :]) % period
    angle = turn * (2.0 * math.pi / period)
    w = np.stack(
        [
            np.concatenate([np.cos(angle), -np.sin(angle)], 1),
            np.concatenate([np.sin(angle), np.cos(angle)], 1),
        ]
    ).astype(np.float32)
    whi = w.astype(jnp.bfloat16)
    wlo = (w - whi.astype(np.float32)).astype(jnp.bfloat16)
    fb = np.arange(TILE) // CC
    phase = ((np.arange(period)[:, None] * fb[None, :]) % (2 * freq)) * (math.pi / freq)
    scale = 1.0 / math.sqrt(freq)
    cos = jnp.asarray(np.cos(phase) * scale, jnp.float32)
    sin = jnp.asarray(np.sin(phase) * scale, jnp.float32)
    start = np.arange(LAG // period) * period - LAG // 2
    phase = ((start[:, None] * fb[None, :]) % (2 * freq)) * (math.pi / freq)
    turns = jnp.asarray(np.stack([np.cos(phase), np.sin(phase)])[:, :, None], jnp.float32)
    smem = pl.BlockSpec(memory_space=pltpu.SMEM)
    vmem = pl.BlockSpec(memory_space=pltpu.VMEM)
    half = LAG // n_seg // 2
    wide = most * TILE
    return pl.pallas_call(
        functools.partial(dft_kernel, n_seg, n_pair, most),
        out_shape=[jax.ShapeDtypeStruct((half, TILE), jnp.float32)] * n_seg,
        in_specs=[smem] + [vmem] * (5 + n_pair),
        out_specs=[vmem] * n_seg,
        scratch_shapes=[
            pltpu.VMEM((2 * h, wide), jnp.float32),
            pltpu.VMEM((2 * h, wide), jnp.bfloat16),
            pltpu.VMEM((2 * h, wide), jnp.bfloat16),
            pltpu.VMEM((2, period, wide), jnp.float32),
        ],
        name="dft",
        cost_estimate=pl.CostEstimate(
            flops=3 * 2 * 2 * period * 2 * h * wide,
            bytes_accessed=2 * w.size * 2 + 2 * period * TILE * 4 + 2 * h * wide * 4,
            transcendentals=0,
        ),
    )(me, jnp.asarray(whi), jnp.asarray(wlo), cos, sin, turns, *blocks)


def unpack_kernel(n_seg, chunks, most, me_ref, *refs):
    ins = refs[: n_seg * chunks]
    out_ref, buf = refs[n_seg * chunks :]
    half = ins[0].shape[0]
    for k in range(n_seg):
        z = jnp.bitwise_xor(me_ref[0], k)
        for ch in range(chunks):
            buf[z * chunks + ch] = ins[ch * n_seg + k][...]
    step_rows = 16

    def one(b, _):
        at = pl.multiple_of(b * step_rows, step_rows)
        v = transpose_groups([buf[i, pl.ds(at, step_rows), :] for i in range(GROUPS)])
        for h in range(2):
            for s in range(most):
                out_ref[pl.ds(h * half + at, step_rows), s, :] = v[h * most + s]
        return 0

    lax.fori_loop(0, half // step_rows, one, 0)


def unpack(me, parts, n_seg, chunks, most):
    half = parts[0].shape[0]
    smem = pl.BlockSpec(memory_space=pltpu.SMEM)
    vmem = pl.BlockSpec(memory_space=pltpu.VMEM)
    return pl.pallas_call(
        functools.partial(unpack_kernel, n_seg, chunks, most),
        out_shape=jax.ShapeDtypeStruct((2 * half, most, TILE), jnp.float32),
        in_specs=[smem] + [vmem] * len(parts),
        out_specs=vmem,
        scratch_shapes=[pltpu.VMEM((GROUPS, half, TILE), jnp.float32)],
        name="unpack",
        cost_estimate=pl.CostEstimate(
            flops=half * TILE * GROUPS * 9,
            bytes_accessed=2 * half * TILE * GROUPS * 4,
            transcendentals=0,
        ),
    )(me, *parts)


def exchange(blocks, axis, size):
    return [blocks[0]] + [
        lax.ppermute(blocks[k], axis, [(i, i ^ k) for i in range(size)])
        for k in range(1, size)
    ]


def body(spectra, pair_lists, pair_counts):
    n_pair = lax.axis_size("pair")
    n_seg = lax.axis_size("seg")
    freq = spectra.shape[2]
    most = pair_lists.shape[0]
    tiles = spectra.shape[3] // TILE
    chunks = GROUPS // n_seg
    rows = freq // n_pair // GROUPS
    me = jnp.stack([lax.axis_index("seg"), lax.axis_index("pair")]).astype(jnp.int32)
    x = spectra.reshape(2, freq, spectra.shape[3])
    table = lax.all_gather(
        jnp.concatenate([pair_lists.reshape(-1), pair_counts]), "pair", axis=0
    )
    done = []
    for chunk in range(chunks):
        sent = pack(x, chunk, n_seg, n_pair)
        sent = sent.reshape(n_seg * n_pair, tiles, 2, rows, TILE)
        got = lax.all_to_all(
            sent, ("seg", "pair"), split_axis=0, concat_axis=0, tiled=True
        )
        spec = got.reshape(n_seg, n_pair * tiles, 2, rows, TILE)
        blocks = stacks(me, table, spec, n_seg, n_pair, most)
        blocks = exchange(blocks, "pair", n_pair)
        lags = dft(me, blocks, freq, n_seg, n_pair, most)
        done += exchange(lags, "seg", n_seg)
    return unpack(me, done, n_seg, chunks, most)


def solution(mesh):
    return jax.shard_map(
        body,
        mesh=mesh,
        in_specs=(P("seg", None, None, "pair"), P("pair", None), P("pair")),
        out_specs=P("seg", "pair", None),
        check_vma=False,
    )
```

```python
import functools
import math

import jax
import jax.numpy as jnp
import numpy as np
from jax import lax
from jax.experimental import pallas as pl
from jax.experimental.pallas import tpu as pltpu
from jax.sharding import PartitionSpec as P

TILE = 128
LAG = 2048
GROUPS = 8
CC = TILE // GROUPS


def lane_groups(shape):
    return lax.broadcasted_iota(jnp.int32, shape, len(shape) - 1) // CC


def shift_groups(x, by):
    return pltpu.roll(x, (by * CC) % TILE, x.ndim - 1)


def transpose_groups(vectors):
    v = list(vectors)
    grp = lane_groups(v[0].shape)
    for bit in (4, 2, 1):
        low = (grp & bit) == 0
        for i in range(GROUPS):
            if i & bit:
                continue
            a, b = v[i], v[i | bit]
            v[i] = jnp.where(low, a, shift_groups(b, bit))
            v[i | bit] = jnp.where(low, shift_groups(a, -bit), b)
    return v


def reduce_groups(vectors):
    v = list(vectors)
    grp = lane_groups(v[0].shape)
    low = (grp & 4) == 0
    v = [
        jnp.where(low, v[i], v[i + 4])
        + shift_groups(jnp.where(low, v[i + 4], v[i]), 4)
        for i in range(4)
    ]
    for bit in (2, 1):
        low = (grp & bit) == 0
        v = [
            jnp.where(low, v[i], v[i + bit])
            + jnp.where(low, shift_groups(v[i], -bit), shift_groups(v[i + bit], bit))
            for i in range(bit)
        ]
    return v[0]


def pack_kernel(n_seg, n_pair, x_ref, sel_ref, out_ref, buf_ref):
    freq = x_ref.shape[1]
    tiles = out_ref.shape[2]
    rows = out_ref.shape[4]
    band = freq // n_pair
    wide = sel_ref.shape[1]

    unroll = buf_ref.shape[0]

    def one(step, _):
        ri, p = step // n_pair, step % n_pair
        slot = step % unroll
        block = x_ref[ri, pl.ds(pl.multiple_of(p * band, band), band), :]
        for part in range(wide // TILE):
            buf_ref[slot] = jnp.dot(
                block,
                sel_ref[:, part * TILE : (part + 1) * TILE],
                preferred_element_type=jnp.float32,
            )
            v = [
                buf_ref[slot, pl.ds(fb, rows, stride=GROUPS), :] for fb in range(GROUPS)
            ]
            v = transpose_groups(v)
            for g in range(GROUPS):
                t, z = divmod(part * GROUPS + g, n_seg)
                out_ref[z, p, t, ri] = v[g].astype(jnp.bfloat16)
        return 0

    lax.fori_loop(0, 2 * n_pair, one, 0, unroll=unroll)


def pack(x, chunk, n_seg, n_pair):
    _, freq, chans = x.shape
    tiles = chans // TILE
    rows = freq // n_pair // GROUPS
    wide = tiles * n_seg * CC
    sel = np.zeros((chans, wide), np.float32)
    for t in range(tiles):
        for z in range(n_seg):
            for c in range(CC):
                src = t * TILE + z * (TILE // n_seg) + chunk * CC + c
                sel[src, (t * n_seg + z) * CC + c] = 1.0
    return pl.pallas_call(
        functools.partial(pack_kernel, n_seg, n_pair),
        out_shape=jax.ShapeDtypeStruct(
            (n_seg, n_pair, tiles, 2, rows, TILE), jnp.bfloat16
        ),
        in_specs=[pl.BlockSpec(memory_space=pltpu.VMEM)] * 2,
        out_specs=pl.BlockSpec(memory_space=pltpu.VMEM),
        scratch_shapes=[pltpu.VMEM((8, freq // n_pair, TILE), jnp.float32)],
        name="pack",
        compiler_params=pltpu.CompilerParams(vmem_limit_bytes=16 << 20),
        cost_estimate=pl.CostEstimate(
            flops=4 * freq * chans * wide,
            bytes_accessed=x.size * 2 + 2 * freq * wide * 2,
            transcendentals=0,
        ),
    )(x, jnp.asarray(sel, jnp.bfloat16))


def stack_kernel(n_seg, n_pair, most, me_ref, table_ref, spec_ref, *out_refs):
    inv = 1.0 / float(n_seg * n_seg)
    for k in range(n_pair):
        owner = jnp.bitwise_xor(me_ref[1], k)
        count = table_ref[owner, 2 * most]
        out_ref = out_refs[k]

        def one(s, _):
            src = table_ref[owner, 2 * s]
            rcv = table_ref[owner, 2 * s + 1]

            @pl.when(s < count)
            def _():
                lr = li = pr = pi = None
                for g in range(n_seg):
                    a0 = spec_ref[g, src, 0].astype(jnp.float32)
                    a1 = spec_ref[g, src, 1].astype(jnp.float32)
                    b0 = spec_ref[g, rcv, 0].astype(jnp.float32)
                    b1 = spec_ref[g, rcv, 1].astype(jnp.float32)
                    cr = a0 * b0 + a1 * b1
                    ci = a1 * b0 - a0 * b1
                    m = lax.rsqrt(cr * cr + ci * ci + 1.0)
                    if g == 0:
                        lr, li, pr, pi = cr, ci, cr * m, ci * m
                    else:
                        lr, li, pr, pi = lr + cr, li + ci, pr + cr * m, pi + ci * m
                w = (pr * pr + pi * pi) * inv
                out_ref[s, 0] = lr * w
                out_ref[s, 1] = li * w

            @pl.when(s >= count)
            def _():
                out_ref[s] = jnp.zeros(out_ref.shape[1:], jnp.float32)

            return 0

        lax.fori_loop(0, most, one, 0)


def stacks(me, table, spec, n_seg, n_pair, most):
    rows = spec.shape[3]
    shape = (most, 2, rows, TILE)
    smem = pl.BlockSpec(memory_space=pltpu.SMEM)
    vmem = pl.BlockSpec(memory_space=pltpu.VMEM)
    return pl.pallas_call(
        functools.partial(stack_kernel, n_seg, n_pair, most),
        out_shape=[jax.ShapeDtypeStruct(shape, jnp.float32)] * n_pair,
        in_specs=[smem, smem, vmem],
        out_specs=[vmem] * n_pair,
        name="stack",
        compiler_params=pltpu.CompilerParams(vmem_limit_bytes=12 << 20),
        cost_estimate=pl.CostEstimate(
            flops=n_pair * most * rows * TILE * n_seg * 20,
            bytes_accessed=spec.size * 2 + n_pair * most * 2 * rows * TILE * 4,
            transcendentals=n_pair * most * rows * TILE * n_seg,
        ),
    )(me, table, spec)


def dft_kernel(n_seg, n_pair, most, me_ref, whi_ref, wlo_ref, cos_ref, sin_ref, thi_ref, tlo_ref, *refs):
    ins = refs[:n_pair]
    outs = refs[n_pair : n_pair + n_seg]
    s32, shi, slo, y, zhi, zlo, sums, parts = refs[n_pair + n_seg :]
    rows = ins[0].shape[2]
    half_h = s32.shape[0] // 2
    for k in range(n_pair):
        band = jnp.bitwise_xor(me_ref[1], k)
        for s in range(most):
            for ri in range(2):
                at = pl.multiple_of(ri * half_h + band * rows, rows)
                s32[pl.ds(at, rows), s * TILE : (s + 1) * TILE] = ins[k][s, ri]
    full = s32[...]
    hi = full.astype(jnp.bfloat16)
    shi[...] = hi
    slo[...] = (full - hi.astype(jnp.float32)).astype(jnp.bfloat16)
    for m in range(whi_ref.shape[0]):
        y[m] = (
            jnp.dot(wlo_ref[m], shi[...], preferred_element_type=jnp.float32)
            + jnp.dot(whi_ref[m], slo[...], preferred_element_type=jnp.float32)
        ) + jnp.dot(whi_ref[m], shi[...], preferred_element_type=jnp.float32)
    period = y.shape[1]
    step_rows = 64
    for b in range(period // step_rows):
        at = slice(b * step_rows, (b + 1) * step_rows)
        c = cos_ref[at, :]
        d = sin_ref[at, :]
        for s in range(most):
            lanes = slice(s * TILE, (s + 1) * TILE)
            yr = y[0, at, lanes]
            yi = y[1, at, lanes]
            for ri, z in enumerate((c * yr - d * yi, d * yr + c * yi)):
                to = slice((ri * most + s) * TILE, (ri * most + s + 1) * TILE)
                hi = z.astype(jnp.bfloat16)
                zhi[at, to] = hi
                zlo[at, to] = (z - hi.astype(jnp.float32)).astype(jnp.bfloat16)
    sums[...] = (
        jnp.dot(zhi[...], tlo_ref[...], preferred_element_type=jnp.float32)
        + jnp.dot(zlo[...], thi_ref[...], preferred_element_type=jnp.float32)
    ) + jnp.dot(zhi[...], thi_ref[...], preferred_element_type=jnp.float32)
    half = outs[0].shape[0]
    first = lax.broadcasted_iota(jnp.int32, (half, TILE), 1) < TILE // 2
    for dest in range(n_seg):
        lag = dest * 2 * half
        r, l0 = lag // period, lag % period
        col = slice(r // 2 * TILE, (r // 2 + 1) * TILE)
        low = sums[l0 : l0 + half, col]
        high = sums[l0 + half : l0 + 2 * half, col]
        if r % 2 == 0:
            high = pltpu.roll(high, TILE // 2, 1)
        else:
            low = pltpu.roll(low, TILE // 2, 1)
        parts[dest] = jnp.where(first, low, high)
    for k in range(n_seg):
        outs[k][...] = parts[jnp.bitwise_xor(me_ref[0], k)]


def dft(me, blocks, freq, n_seg, n_pair, most):
    h = freq // GROUPS
    period = 2 * h
    turn = (np.arange(period)[:, None] * np.arange(h)[None, :]) % period
    angle = turn * (2.0 * math.pi / period)
    w = np.stack(
        [
            np.concatenate([np.cos(angle), -np.sin(angle)], 1),
            np.concatenate([np.sin(angle), np.cos(angle)], 1),
        ]
    ).astype(np.float32)
    whi = w.astype(jnp.bfloat16)
    wlo = (w - whi.astype(np.float32)).astype(jnp.bfloat16)
    fb = np.arange(TILE) // CC
    phase = ((np.arange(period)[:, None] * fb[None, :]) % (2 * freq)) * (math.pi / freq)
    scale = 1.0 / math.sqrt(freq)
    cos = jnp.asarray(np.cos(phase) * scale, jnp.float32)
    sin = jnp.asarray(np.sin(phase) * scale, jnp.float32)
    turns = LAG // period
    t = np.zeros((2, most, GROUPS, CC, turns, most, CC), np.float64)
    for r in range(turns):
        for q in range(GROUPS):
            phase = ((r * period - LAG // 2) * q % (2 * freq)) * (math.pi / freq)
            for sl in range(most):
                for ch in range(CC):
                    t[0, sl, q, ch, r, sl, ch] = math.cos(phase)
                    t[1, sl, q, ch, r, sl, ch] = -math.sin(phase)
    t = t.reshape(2 * most * TILE, turns * most * CC).astype(np.float32)
    thi = t.astype(jnp.bfloat16)
    tlo = (t - thi.astype(np.float32)).astype(jnp.bfloat16)
    smem = pl.BlockSpec(memory_space=pltpu.SMEM)
    vmem = pl.BlockSpec(memory_space=pltpu.VMEM)
    half = LAG // n_seg // 2
    wide = most * TILE
    return pl.pallas_call(
        functools.partial(dft_kernel, n_seg, n_pair, most),
        out_shape=[jax.ShapeDtypeStruct((half, TILE), jnp.float32)] * n_seg,
        in_specs=[smem] + [vmem] * (6 + n_pair),
        out_specs=[vmem] * n_seg,
        scratch_shapes=[
            pltpu.VMEM((2 * h, wide), jnp.float32),
            pltpu.VMEM((2 * h, wide), jnp.bfloat16),
            pltpu.VMEM((2 * h, wide), jnp.bfloat16),
            pltpu.VMEM((2, period, wide), jnp.float32),
            pltpu.VMEM((period, 2 * wide), jnp.bfloat16),
            pltpu.VMEM((period, 2 * wide), jnp.bfloat16),
            pltpu.VMEM((period, turns * most * CC), jnp.float32),
            pltpu.VMEM((n_seg, half, TILE), jnp.float32),
        ],
        name="dft",
        compiler_params=pltpu.CompilerParams(vmem_limit_bytes=24 << 20),
        cost_estimate=pl.CostEstimate(
            flops=3 * 2 * 2 * period * 2 * h * wide,
            bytes_accessed=2 * w.size * 2 + 2 * period * TILE * 4 + 2 * h * wide * 4,
            transcendentals=0,
        ),
    )(me, jnp.asarray(whi), jnp.asarray(wlo), cos, sin, jnp.asarray(thi), jnp.asarray(tlo), *blocks)


def unpack_kernel(n_seg, chunks, most, me_ref, *refs):
    ins = refs[: n_seg * chunks]
    out_ref, buf = refs[n_seg * chunks :]
    half = ins[0].shape[0]
    for k in range(n_seg):
        z = jnp.bitwise_xor(me_ref[0], k)
        for ch in range(chunks):
            buf[z * chunks + ch] = ins[ch * n_seg + k][...]
    step_rows = 16

    def one(b, _):
        at = pl.multiple_of(b * step_rows, step_rows)
        v = transpose_groups([buf[i, pl.ds(at, step_rows), :] for i in range(GROUPS)])
        for h in range(2):
            for s in range(most):
                out_ref[pl.ds(h * half + at, step_rows), s, :] = v[h * most + s]
        return 0

    lax.fori_loop(0, half // step_rows, one, 0, unroll=4)


def unpack(me, parts, n_seg, chunks, most):
    half = parts[0].shape[0]
    smem = pl.BlockSpec(memory_space=pltpu.SMEM)
    vmem = pl.BlockSpec(memory_space=pltpu.VMEM)
    return pl.pallas_call(
        functools.partial(unpack_kernel, n_seg, chunks, most),
        out_shape=jax.ShapeDtypeStruct((2 * half, most, TILE), jnp.float32),
        in_specs=[smem] + [vmem] * len(parts),
        out_specs=vmem,
        scratch_shapes=[pltpu.VMEM((GROUPS, half, TILE), jnp.float32)],
        name="unpack",
        compiler_params=pltpu.CompilerParams(vmem_limit_bytes=12 << 20),
        cost_estimate=pl.CostEstimate(
            flops=half * TILE * GROUPS * 9,
            bytes_accessed=2 * half * TILE * GROUPS * 4,
            transcendentals=0,
        ),
    )(me, *parts)


def exchange(blocks, axis, size):
    return [blocks[0]] + [
        lax.ppermute(blocks[k], axis, [(i, i ^ k) for i in range(size)])
        for k in range(1, size)
    ]


def body(spectra, pair_lists, pair_counts):
    n_pair = lax.axis_size("pair")
    n_seg = lax.axis_size("seg")
    freq = spectra.shape[2]
    most = pair_lists.shape[0]
    tiles = spectra.shape[3] // TILE
    chunks = GROUPS // n_seg
    rows = freq // n_pair // GROUPS
    me = jnp.stack([lax.axis_index("seg"), lax.axis_index("pair")]).astype(jnp.int32)
    x = spectra.reshape(2, freq, spectra.shape[3])
    lists = jnp.concatenate([pair_lists.reshape(-1), pair_counts])
    packed = [pack(x, chunk, n_seg, n_pair) for chunk in range(chunks)]
    lists, packed[-1] = lax.optimization_barrier((lists, packed[-1]))
    table = lax.all_gather(lists, "pair", axis=0)
    if chunks > 1:
        table, packed[1] = lax.optimization_barrier((table, packed[1]))
    done = []
    lags = None
    for sent in packed:
        got = lax.all_to_all(
            sent.reshape(n_seg * n_pair, tiles, 2, rows, TILE),
            ("seg", "pair"),
            split_axis=0,
            concat_axis=0,
            tiled=True,
        )
        if lags is not None:
            got, lags = lax.optimization_barrier((got, lags))
            done += exchange(lags, "seg", n_seg)
        spec = got.reshape(n_seg, n_pair * tiles, 2, rows, TILE)
        blocks = stacks(me, table, spec, n_seg, n_pair, most)
        blocks = exchange(blocks, "pair", n_pair)
        lags = dft(me, blocks, freq, n_seg, n_pair, most)
    done += exchange(lags, "seg", n_seg)
    return unpack(me, done, n_seg, chunks, most)


def solution(mesh):
    return jax.shard_map(
        body,
        mesh=mesh,
        in_specs=(P("seg", None, None, "pair"), P("pair", None), P("pair")),
        out_specs=P("seg", "pair", None),
        check_vma=False,
    )
```

```python
import functools
import math

import jax
import jax.numpy as jnp
import numpy as np
from jax import lax
from jax.experimental import pallas as pl
from jax.experimental.pallas import tpu as pltpu
from jax.sharding import PartitionSpec as P

TILE = 128
LAG = 2048
GROUPS = 8
SMALL = pl.CostEstimate(flops=1, bytes_accessed=1, transcendentals=0)
LARGE = pl.CostEstimate(flops=10**11, bytes_accessed=1, transcendentals=0)
CC = TILE // GROUPS


def lane_groups(shape):
    return lax.broadcasted_iota(jnp.int32, shape, len(shape) - 1) // CC


def shift_groups(x, by):
    return pltpu.roll(x, (by * CC) % TILE, x.ndim - 1)


def transpose_groups(vectors):
    v = list(vectors)
    grp = lane_groups(v[0].shape)
    for bit in (4, 2, 1):
        low = (grp & bit) == 0
        for i in range(GROUPS):
            if i & bit:
                continue
            a, b = v[i], v[i | bit]
            v[i] = jnp.where(low, a, shift_groups(b, bit))
            v[i | bit] = jnp.where(low, shift_groups(a, -bit), b)
    return v


def reduce_groups(vectors):
    v = list(vectors)
    grp = lane_groups(v[0].shape)
    low = (grp & 4) == 0
    v = [
        jnp.where(low, v[i], v[i + 4])
        + shift_groups(jnp.where(low, v[i + 4], v[i]), 4)
        for i in range(4)
    ]
    for bit in (2, 1):
        low = (grp & bit) == 0
        v = [
            jnp.where(low, v[i], v[i + bit])
            + jnp.where(low, shift_groups(v[i], -bit), shift_groups(v[i + bit], bit))
            for i in range(bit)
        ]
    return v[0]


def selection(n_seg, chunk, chans):
    wide = chans // TILE * n_seg * CC
    row = lax.broadcasted_iota(jnp.int32, (chans, wide), 0)
    col = lax.broadcasted_iota(jnp.int32, (chans, wide), 1)
    group = col // CC
    want = (
        group // n_seg * TILE
        + group % n_seg * (TILE // n_seg)
        + chunk * CC
        + col % CC
    )
    return (row == want).astype(jnp.bfloat16)


def pack_band(n_seg, band, sel, buf_ref, store):
    rows = band.shape[0] // GROUPS
    for part in range(sel.shape[1] // TILE):
        lanes = slice(part * TILE, (part + 1) * TILE)
        buf_ref[...] = jnp.dot(
            band, sel[:, lanes], preferred_element_type=jnp.float32
        )
        v = [buf_ref[pl.ds(fb, rows, stride=GROUPS), :] for fb in range(GROUPS)]
        v = transpose_groups(v)
        for g in range(GROUPS):
            t, z = divmod(part * GROUPS + g, n_seg)
            store(t, z, v[g].astype(jnp.bfloat16))


def pack_kernel(n_seg, chunk, x_ref, out_ref, buf_ref):
    sel = selection(n_seg, chunk, x_ref.shape[2])
    for ri in range(2):

        def store(t, z, value, ri=ri):
            out_ref[z, 0, t, ri] = value

        pack_band(n_seg, x_ref[ri], sel, buf_ref.at[ri], store)


def pack(x, chunk, n_seg, n_pair):
    _, freq, chans = x.shape
    tiles = chans // TILE
    band = freq // n_pair
    rows = band // GROUPS
    return pl.pallas_call(
        functools.partial(pack_kernel, n_seg, chunk),
        out_shape=jax.ShapeDtypeStruct(
            (n_seg, n_pair, tiles, 2, rows, TILE), jnp.bfloat16
        ),
        grid=(n_pair,),
        in_specs=[pl.BlockSpec((2, band, chans), lambda p: (0, p, 0))],
        out_specs=pl.BlockSpec(
            (n_seg, 1, tiles, 2, rows, TILE), lambda p: (0, p, 0, 0, 0, 0)
        ),
        scratch_shapes=[pltpu.VMEM((2, band, TILE), jnp.float32)],
        name="pack",
        cost_estimate=SMALL,
    )(x)


def pack_near_kernel(n_seg, n_pair, chunk, me_ref, x_ref, *refs):
    outs, buf_ref = refs[:-1], refs[-1]
    band = x_ref.shape[1] // n_pair
    sel = selection(n_seg, chunk, x_ref.shape[2])
    for k in range(n_pair):
        p = jnp.bitwise_xor(me_ref[1], k)
        at = pl.ds(pl.multiple_of(p * band, band), band)
        for ri in range(2):

            def store(t, z, value, ri=ri, k=k):
                outs[k // 2][k % 2, z, t, ri] = value

            pack_band(n_seg, x_ref[ri, at, :], sel, buf_ref.at[ri], store)


def pack_near(me, x, chunk, n_seg, n_pair):
    _, freq, chans = x.shape
    tiles = chans // TILE
    band = freq // n_pair
    rows = band // GROUPS
    shape = (2, n_seg, tiles, 2, rows, TILE)
    vmem = pl.BlockSpec(memory_space=pltpu.VMEM)
    return pl.pallas_call(
        functools.partial(pack_near_kernel, n_seg, n_pair, chunk),
        out_shape=[jax.ShapeDtypeStruct(shape, jnp.bfloat16)] * (n_pair // 2),
        in_specs=[pl.BlockSpec(memory_space=pltpu.SMEM), vmem],
        out_specs=[vmem] * (n_pair // 2),
        scratch_shapes=[pltpu.VMEM((2, band, TILE), jnp.float32)],
        name="pack_near",
        cost_estimate=SMALL,
    )(me, x)


def regroup_kernel(n_seg, n_pair, me_ref, *refs):
    ins, outs = refs[:n_pair], refs[n_pair:]
    for kz in range(n_seg):
        z = jnp.bitwise_xor(me_ref[0], kz)
        for k in range(n_pair):
            p = jnp.bitwise_xor(me_ref[1], k)
            outs[kz][p] = ins[k % 2 * (n_pair // 2) + k // 2][k % 2, z]


def regroup(me, blocks, n_seg, n_pair):
    shape = (n_pair,) + blocks[0].shape[2:]
    vmem = pl.BlockSpec(memory_space=pltpu.VMEM)
    return pl.pallas_call(
        functools.partial(regroup_kernel, n_seg, n_pair),
        out_shape=[jax.ShapeDtypeStruct(shape, jnp.bfloat16)] * n_seg,
        in_specs=[pl.BlockSpec(memory_space=pltpu.SMEM)] + [vmem] * n_pair,
        out_specs=[vmem] * n_seg,
        name="regroup",
        cost_estimate=SMALL,
    )(me, *blocks)


def stack_kernel(n_seg, n_pair, most, n_specs, me_ref, table_ref, *refs):
    specs, out_refs = refs[:n_specs], refs[n_specs:]
    near = len(out_refs) > 1
    parts = [r.at[g] for r in specs for g in range(r.shape[0])]
    inv = 1.0 / float(n_seg * n_seg)
    for k in range(n_pair):
        owner = jnp.bitwise_xor(me_ref[1], k) if near else k
        count = table_ref[owner, 2 * most]
        out_ref = out_refs[k // 2].at[k % 2] if near else out_refs[0].at[k]

        def one(s, _):
            src = table_ref[owner, 2 * s]
            rcv = table_ref[owner, 2 * s + 1]

            @pl.when(s < count)
            def _():
                lr = li = pr = pi = None
                for g in range(n_seg):
                    a0 = parts[g][src, 0].astype(jnp.float32)
                    a1 = parts[g][src, 1].astype(jnp.float32)
                    b0 = parts[g][rcv, 0].astype(jnp.float32)
                    b1 = parts[g][rcv, 1].astype(jnp.float32)
                    cr = a0 * b0 + a1 * b1
                    ci = a1 * b0 - a0 * b1
                    m = lax.rsqrt(cr * cr + ci * ci + 1.0)
                    if g == 0:
                        lr, li, pr, pi = cr, ci, cr * m, ci * m
                    else:
                        lr, li, pr, pi = lr + cr, li + ci, pr + cr * m, pi + ci * m
                w = (pr * pr + pi * pi) * inv
                out_ref[s, 0] = lr * w
                out_ref[s, 1] = li * w

            @pl.when(s >= count)
            def _():
                out_ref[s] = jnp.zeros(out_ref.shape[1:], jnp.float32)

            return 0

        lax.fori_loop(0, most, one, 0)


def stacks(me, table, specs, near, n_seg, n_pair, most):
    rows = specs[0].shape[3]
    arrays = n_pair // 2 if near else 1
    shape = (n_pair // arrays, most, 2, rows, TILE)
    smem = pl.BlockSpec(memory_space=pltpu.SMEM)
    vmem = pl.BlockSpec(memory_space=pltpu.VMEM)
    return pl.pallas_call(
        functools.partial(stack_kernel, n_seg, n_pair, most, len(specs)),
        out_shape=[jax.ShapeDtypeStruct(shape, jnp.float32)] * arrays,
        in_specs=[smem, smem] + [vmem] * len(specs),
        out_specs=[vmem] * arrays,
        name="stack",
        cost_estimate=LARGE if near else SMALL,
    )(me, table, *specs)


def dft_kernel(n_seg, n_pair, most, n_blocks, me_ref, *refs):
    table_refs, ins = refs[:6], refs[6 : 6 + n_blocks]
    outs = refs[6 + n_blocks : 6 + n_blocks + n_seg]
    held = refs[6 + n_blocks + n_seg : 12 + n_blocks + n_seg]
    s32, shi, slo, y, zhi, zlo, sums, parts, sems = refs[12 + n_blocks + n_seg :]
    whi_ref, wlo_ref, cos_ref, sin_ref, thi_ref, tlo_ref = held
    copies = [
        pltpu.make_async_copy(src, to, sems.at[i])
        for i, (src, to) in enumerate(zip(table_refs, held))
    ]
    for copy in copies:
        copy.start()
    rows = ins[0].shape[3]
    half_h = whi_ref.shape[1] // 2
    wide = most * TILE
    for k in range(n_pair):
        if n_blocks == 1:
            band, src = k, ins[0].at[k]
        else:
            band = jnp.bitwise_xor(me_ref[1], k)
            src = ins[k % 2 * (n_pair // 2) + k // 2].at[k % 2]
        at = pl.ds(pl.multiple_of(band * rows, rows), rows)
        for s in range(most):
            for ri in range(2):
                s32[ri, at, s * TILE : (s + 1) * TILE] = src[s, ri]
    for ri in range(2):
        full = s32[ri]
        hi = full.astype(jnp.bfloat16)
        lo = (full - hi.astype(jnp.float32)).astype(jnp.bfloat16)
        own = slice(ri * wide, (ri + 1) * wide)
        other = slice((1 - ri) * wide, (2 - ri) * wide)
        for to, part in ((shi, hi), (slo, lo)):
            to[:half_h, own] = part
            to[half_h:, other] = part if ri == 0 else -part
    copies[0].wait()
    copies[1].wait()
    for ri in range(2):
        n = slice(ri * wide, (ri + 1) * wide)
        y[ri] = (
            jnp.dot(wlo_ref[...], shi[:, n], preferred_element_type=jnp.float32)
            + jnp.dot(whi_ref[...], slo[:, n], preferred_element_type=jnp.float32)
        ) + jnp.dot(whi_ref[...], shi[:, n], preferred_element_type=jnp.float32)
    copies[2].wait()
    copies[3].wait()
    period = y.shape[1]
    step_rows = 64
    for b in range(period // step_rows):
        at = slice(b * step_rows, (b + 1) * step_rows)
        c = cos_ref[at, :]
        d = sin_ref[at, :]
        for s in range(most):
            lanes = slice(s * TILE, (s + 1) * TILE)
            yr = y[0, at, lanes]
            yi = y[1, at, lanes]
            for ri, z in enumerate((c * yr - d * yi, d * yr + c * yi)):
                to = slice((ri * most + s) * TILE, (ri * most + s + 1) * TILE)
                hi = z.astype(jnp.bfloat16)
                zhi[at, to] = hi
                zlo[at, to] = (z - hi.astype(jnp.float32)).astype(jnp.bfloat16)
    copies[4].wait()
    copies[5].wait()
    sums[...] = (
        jnp.dot(zhi[...], tlo_ref[...], preferred_element_type=jnp.float32)
        + jnp.dot(zlo[...], thi_ref[...], preferred_element_type=jnp.float32)
    ) + jnp.dot(zhi[...], thi_ref[...], preferred_element_type=jnp.float32)
    half = outs[0].shape[0]
    first = lax.broadcasted_iota(jnp.int32, (half, TILE), 1) < TILE // 2
    for dest in range(n_seg):
        lag = dest * 2 * half
        r, l0 = lag // period, lag % period
        col = slice(r // 2 * TILE, (r // 2 + 1) * TILE)
        low = sums[l0 : l0 + half, col]
        high = sums[l0 + half : l0 + 2 * half, col]
        if r % 2 == 0:
            high = pltpu.roll(high, TILE // 2, 1)
        else:
            low = pltpu.roll(low, TILE // 2, 1)
        parts[dest] = jnp.where(first, low, high)
    for k in range(n_seg):
        outs[k][...] = parts[jnp.bitwise_xor(me_ref[0], k)]


def turns_kernel(most, turns, shift, hi_ref, lo_ref):
    shape = (most * TILE, turns * most * CC)
    row = lax.broadcasted_iota(jnp.int32, shape, 0)
    col = lax.broadcasted_iota(jnp.int32, shape, 1)
    same = (row // TILE == col // CC % most) & (row % CC == col % CC)
    eighths = (col // (most * CC) - shift) * (row // CC % GROUPS)
    diagonal = jnp.float32(math.sqrt(0.5))
    for ri in range(2):
        e = jnp.bitwise_and(eighths + 2 * ri, 7)
        size = jnp.where(e % 4 == 2, 0.0, jnp.where(e % 2 == 0, 1.0, diagonal))
        t = jnp.where(same, jnp.where((e > 2) & (e < 6), -size, size), 0.0)
        at = slice(ri * most * TILE, (ri + 1) * most * TILE)
        hi = t.astype(jnp.bfloat16)
        hi_ref[at, :] = hi
        lo_ref[at, :] = (t - hi.astype(jnp.float32)).astype(jnp.bfloat16)


def make_tables(freq, most):
    h = freq // GROUPS
    period = 2 * h
    turns = LAG // period
    angle = np.arange(period)[:, None] * np.arange(h)[None, :] % period
    angle = angle * (2.0 * math.pi / period)
    w = np.concatenate([np.cos(angle), np.sin(angle)], 1).astype(np.float32)
    whi = w.astype(jnp.bfloat16)
    wlo = (w - whi.astype(np.float32)).astype(jnp.bfloat16)
    fb = np.arange(TILE) // CC
    phase = ((np.arange(period)[:, None] * fb[None, :]) % (2 * freq)) * (math.pi / freq)
    scale = 1.0 / math.sqrt(freq)
    cos = (np.cos(phase) * scale).astype(np.float32)
    sin = (np.sin(phase) * scale).astype(np.float32)
    shape = (2 * most * TILE, turns * most * CC)
    pair = pl.pallas_call(
        functools.partial(turns_kernel, most, turns, LAG // 2 // period),
        out_shape=[jax.ShapeDtypeStruct(shape, jnp.bfloat16)] * 2,
        out_specs=[pl.BlockSpec(memory_space=pltpu.VMEM)] * 2,
        name="turns",
        cost_estimate=SMALL,
    )()
    return [jnp.asarray(c) for c in (whi, wlo, cos, sin)], list(pair)


def dft(me, tables, blocks, freq, n_seg, n_pair, most):
    period = 2 * (freq // GROUPS)
    smem = pl.BlockSpec(memory_space=pltpu.SMEM)
    vmem = pl.BlockSpec(memory_space=pltpu.VMEM)
    hbm = pl.BlockSpec(memory_space=pltpu.HBM)
    half = LAG // n_seg // 2
    wide = most * TILE
    return pl.pallas_call(
        functools.partial(dft_kernel, n_seg, n_pair, most, len(blocks)),
        out_shape=[jax.ShapeDtypeStruct((half, TILE), jnp.float32)] * n_seg,
        in_specs=[smem] + [hbm] * 6 + [vmem] * len(blocks),
        out_specs=[vmem] * n_seg,
        scratch_shapes=[pltpu.VMEM(t.shape, t.dtype) for t in tables]
        + [
            pltpu.VMEM((2, period // 2, wide), jnp.float32),
            pltpu.VMEM((period, 2 * wide), jnp.bfloat16),
            pltpu.VMEM((period, 2 * wide), jnp.bfloat16),
            pltpu.VMEM((2, period, wide), jnp.float32),
            pltpu.VMEM((period, 2 * wide), jnp.bfloat16),
            pltpu.VMEM((period, 2 * wide), jnp.bfloat16),
            pltpu.VMEM((period, LAG // period * most * CC), jnp.float32),
            pltpu.VMEM((n_seg, half, TILE), jnp.float32),
            pltpu.SemaphoreType.DMA((6,)),
        ],
        name="dft",
        compiler_params=pltpu.CompilerParams(vmem_limit_bytes=24 << 20),
        cost_estimate=SMALL,
    )(me, *tables, *blocks)


def unpack_kernel(n_seg, chunks, most, me_ref, *refs):
    ins = refs[: n_seg * chunks]
    out_ref, buf = refs[n_seg * chunks :]
    half = ins[0].shape[0]
    for k in range(n_seg):
        z = jnp.bitwise_xor(me_ref[0], k)
        for ch in range(chunks):
            buf[z * chunks + ch] = ins[ch * n_seg + k][...]
    step_rows = 16

    def one(b, _):
        at = pl.multiple_of(b * step_rows, step_rows)
        v = transpose_groups([buf[i, pl.ds(at, step_rows), :] for i in range(GROUPS)])
        for h in range(2):
            for s in range(most):
                out_ref[pl.ds(h * half + at, step_rows), s, :] = v[h * most + s]
        return 0

    lax.fori_loop(0, half // step_rows, one, 0, unroll=4)


def unpack(me, parts, n_seg, chunks, most):
    half = parts[0].shape[0]
    smem = pl.BlockSpec(memory_space=pltpu.SMEM)
    vmem = pl.BlockSpec(memory_space=pltpu.VMEM)
    return pl.pallas_call(
        functools.partial(unpack_kernel, n_seg, chunks, most),
        out_shape=jax.ShapeDtypeStruct((2 * half, most, TILE), jnp.float32),
        in_specs=[smem] + [vmem] * len(parts),
        out_specs=vmem,
        scratch_shapes=[pltpu.VMEM((GROUPS, half, TILE), jnp.float32)],
        name="unpack",
        compiler_params=pltpu.CompilerParams(vmem_limit_bytes=12 << 20),
        cost_estimate=SMALL,
    )(me, *parts)


def exchange(blocks, axis, size):
    return [blocks[0]] + [
        lax.ppermute(blocks[k], axis, [(i, i ^ k) for i in range(size)])
        for k in range(1, size)
    ]


def exchange_plane(blocks, n_pair):
    direct = [blocks[0]] + [
        lax.ppermute(blocks[k], "pair", [(i, i ^ (2 * k)) for i in range(n_pair)])
        for k in range(1, n_pair // 2)
    ]
    swap = [(i, i ^ 1) for i in range(n_pair)]
    return direct + [lax.ppermute(d, "pair", swap) for d in direct]


def body(spectra, pair_lists, pair_counts):
    n_pair = lax.axis_size("pair")
    n_seg = lax.axis_size("seg")
    freq = spectra.shape[2]
    most = pair_lists.shape[0]
    tiles = spectra.shape[3] // TILE
    chunks = GROUPS // n_seg
    rows = freq // n_pair // GROUPS
    me = jnp.stack([lax.axis_index("seg"), lax.axis_index("pair")]).astype(jnp.int32)
    x = spectra.reshape(2, freq, spectra.shape[3])
    lists = jnp.concatenate([pair_lists.reshape(-1), pair_counts])
    first = pack(x, 0, n_seg, n_pair)
    near = [pack_near(me, x, chunk, n_seg, n_pair) for chunk in range(1, chunks)]
    if near:
        lists, near[0] = lax.optimization_barrier((lists, near[0]))
    table = lax.all_gather(lists, "pair", axis=0)
    consts, turns = make_tables(freq, most)
    spec = lax.all_to_all(
        first.reshape(n_seg * n_pair, tiles, 2, rows, TILE),
        ("seg", "pair"),
        split_axis=0,
        concat_axis=0,
        tiled=True,
    ).reshape(n_seg, n_pair * tiles, 2, rows, TILE)
    far = [regroup(me, exchange_plane(n, n_pair), n_seg, n_pair) for n in near]
    spec, table, turns, _ = lax.optimization_barrier((spec, table, turns, far))
    tables = consts + turns
    blocks = stacks(me, table, [spec], False, n_seg, n_pair, most)
    blocks = [
        lax.all_to_all(blocks[0], "pair", split_axis=0, concat_axis=0, tiled=True)
    ]
    done = []
    for f in far:
        got = [
            g.reshape(1, n_pair * tiles, 2, rows, TILE)
            for g in exchange(f, "seg", n_seg)
        ]
        after = stacks(me, table, got, True, n_seg, n_pair, most)
        blocks, _ = lax.optimization_barrier((blocks, after))
        after = exchange_plane(after, n_pair)
        lags = dft(me, tables, blocks, freq, n_seg, n_pair, most)
        done += exchange(lags, "seg", n_seg)
        blocks, _ = lax.optimization_barrier((after, lags))
    lags = dft(me, tables, blocks, freq, n_seg, n_pair, most)
    done += exchange(lags, "seg", n_seg)
    return unpack(me, done, n_seg, chunks, most)


def solution(mesh):
    return jax.shard_map(
        body,
        mesh=mesh,
        in_specs=(P("seg", None, None, "pair"), P("pair", None), P("pair")),
        out_specs=P("seg", "pair", None),
        check_vma=False,
    )
```

```python
import functools
import math

import jax
import jax.numpy as jnp
import numpy as np
from jax import lax
from jax.experimental import pallas as pl
from jax.experimental.pallas import tpu as pltpu
from jax.sharding import PartitionSpec as P

TILE = 128
LAG = 2048
GROUPS = 8
SMALL = pl.CostEstimate(flops=1, bytes_accessed=1, transcendentals=0)
CC = TILE // GROUPS


def lane_groups(shape):
    return lax.broadcasted_iota(jnp.int32, shape, len(shape) - 1) // CC


def shift_groups(x, by):
    return pltpu.roll(x, (by * CC) % TILE, x.ndim - 1)


def transpose_groups(vectors):
    v = list(vectors)
    grp = lane_groups(v[0].shape)
    for bit in (4, 2, 1):
        low = (grp & bit) == 0
        for i in range(GROUPS):
            if i & bit:
                continue
            a, b = v[i], v[i | bit]
            v[i] = jnp.where(low, a, shift_groups(b, bit))
            v[i | bit] = jnp.where(low, shift_groups(a, -bit), b)
    return v


def reduce_groups(vectors):
    v = list(vectors)
    grp = lane_groups(v[0].shape)
    low = (grp & 4) == 0
    v = [
        jnp.where(low, v[i], v[i + 4])
        + shift_groups(jnp.where(low, v[i + 4], v[i]), 4)
        for i in range(4)
    ]
    for bit in (2, 1):
        low = (grp & bit) == 0
        v = [
            jnp.where(low, v[i], v[i + bit])
            + jnp.where(low, shift_groups(v[i], -bit), shift_groups(v[i + bit], bit))
            for i in range(bit)
        ]
    return v[0]


def selection(n_seg, chunk, chans):
    wide = chans // TILE * n_seg * CC
    row = lax.broadcasted_iota(jnp.int32, (chans, wide), 0)
    col = lax.broadcasted_iota(jnp.int32, (chans, wide), 1)
    group = col // CC
    want = (
        group // n_seg * TILE
        + group % n_seg * (TILE // n_seg)
        + chunk * CC
        + col % CC
    )
    return (row == want).astype(jnp.bfloat16)


def pack_kernel(n_seg, n_pair, chunk, x_ref, out_ref, x_buf, buf_ref, sems):
    band = x_ref.shape[1] // n_pair
    copies = []
    for p in range(n_pair):
        at = pl.ds(p * band, band)
        copies.append(
            pltpu.make_async_copy(x_ref.at[:, at], x_buf.at[p], sems.at[p])
        )
        copies[-1].start()
    sel = selection(n_seg, chunk, x_ref.shape[2])
    rows = band // GROUPS
    for p in range(n_pair):
        copies[p].wait()
        for ri in range(2):
            for part in range(sel.shape[1] // TILE):
                lanes = slice(part * TILE, (part + 1) * TILE)
                buf = buf_ref.at[p % 2, ri]
                buf[...] = jnp.dot(
                    x_buf[p, ri], sel[:, lanes], preferred_element_type=jnp.float32
                )
                v = [buf[pl.ds(fb, rows, stride=GROUPS), :] for fb in range(GROUPS)]
                v = transpose_groups(v)
                for g in range(GROUPS):
                    t, z = divmod(part * GROUPS + g, n_seg)
                    out_ref[z, p, t, ri] = v[g].astype(jnp.bfloat16)


def pack(x, chunk, n_seg, n_pair):
    _, freq, chans = x.shape
    band = freq // n_pair
    shape = (n_seg, n_pair, chans // TILE, 2, band // GROUPS, TILE)
    return pl.pallas_call(
        functools.partial(pack_kernel, n_seg, n_pair, chunk),
        out_shape=jax.ShapeDtypeStruct(shape, jnp.bfloat16),
        in_specs=[pl.BlockSpec(memory_space=pltpu.HBM)],
        out_specs=pl.BlockSpec(memory_space=pltpu.VMEM),
        scratch_shapes=[
            pltpu.VMEM((n_pair, 2, band, chans), jnp.bfloat16),
            pltpu.VMEM((2, 2, band, TILE), jnp.float32),
            pltpu.SemaphoreType.DMA((n_pair,)),
        ],
        name="pack",
        cost_estimate=SMALL,
    )(x)


def stack_kernel(n_seg, n_pair, most, n_specs, me_ref, table_ref, *refs):
    specs, out_refs = refs[:n_specs], refs[n_specs:]
    parts = [r.at[g] for r in specs for g in range(r.shape[0])]
    inv = 1.0 / float(n_seg * n_seg)
    for k in range(n_pair):
        owner = jnp.bitwise_xor(me_ref[1], k)
        count = table_ref[owner, 2 * most]
        out_ref = out_refs[k // 2].at[k % 2]

        def one(s, _):
            src = table_ref[owner, 2 * s]
            rcv = table_ref[owner, 2 * s + 1]

            @pl.when(s < count)
            def _():
                lr = li = pr = pi = None
                for g in range(n_seg):
                    a0 = parts[g][src, 0].astype(jnp.float32)
                    a1 = parts[g][src, 1].astype(jnp.float32)
                    b0 = parts[g][rcv, 0].astype(jnp.float32)
                    b1 = parts[g][rcv, 1].astype(jnp.float32)
                    cr = a0 * b0 + a1 * b1
                    ci = a1 * b0 - a0 * b1
                    m = lax.rsqrt(cr * cr + ci * ci + 1.0)
                    if g == 0:
                        lr, li, pr, pi = cr, ci, cr * m, ci * m
                    else:
                        lr, li, pr, pi = lr + cr, li + ci, pr + cr * m, pi + ci * m
                w = (pr * pr + pi * pi) * inv
                out_ref[s, 0] = lr * w
                out_ref[s, 1] = li * w

            @pl.when(s >= count)
            def _():
                out_ref[s] = jnp.zeros(out_ref.shape[1:], jnp.float32)

            return 0

        lax.fori_loop(0, most, one, 0)


def stacks(me, table, specs, cost, n_seg, n_pair, most):
    rows = specs[0].shape[3]
    arrays = n_pair // 2
    shape = (n_pair // arrays, most, 2, rows, TILE)
    smem = pl.BlockSpec(memory_space=pltpu.SMEM)
    vmem = pl.BlockSpec(memory_space=pltpu.VMEM)
    return pl.pallas_call(
        functools.partial(stack_kernel, n_seg, n_pair, most, len(specs)),
        out_shape=[jax.ShapeDtypeStruct(shape, jnp.float32)] * arrays,
        in_specs=[smem, smem] + [vmem] * len(specs),
        out_specs=[vmem] * arrays,
        name="stack",
        compiler_params=pltpu.CompilerParams(vmem_limit_bytes=8 << 20),
        cost_estimate=cost,
    )(me, table, *specs)


def dft_kernel(n_seg, n_pair, most, me_ref, tables_ref, *refs):
    ins, outs = refs[:n_pair], refs[n_pair : n_pair + n_seg]
    held, sems = refs[n_pair + n_seg :][:4], refs[n_pair + n_seg + 4]
    s32, shi, slo, y, zhi, zlo, sums, parts = refs[n_pair + n_seg + 5 :]
    whi_ref, wlo_ref, t_ref, phase_ref = held
    copies = []
    row = 0
    for i, to in enumerate(held):
        src = tables_ref.at[pl.ds(row, to.shape[0])]
        copies.append(pltpu.make_async_copy(src, to, sems.at[i]))
        copies[-1].start()
        row += to.shape[0]
    rows = ins[0].shape[3]
    half_h = whi_ref.shape[1] // 2
    wide = most * TILE
    for k in range(n_pair):
        band = jnp.bitwise_xor(me_ref[1], k)
        src = ins[k % 2 * (n_pair // 2) + k // 2].at[k % 2]
        at = pl.ds(pl.multiple_of(band * rows, rows), rows)
        for s in range(most):
            for ri in range(2):
                s32[ri, at, s * TILE : (s + 1) * TILE] = src[s, ri]
    for ri in range(2):
        full = s32[ri]
        hi = full.astype(jnp.bfloat16)
        lo = (full - hi.astype(jnp.float32)).astype(jnp.bfloat16)
        own = slice(ri * wide, (ri + 1) * wide)
        other = slice((1 - ri) * wide, (2 - ri) * wide)
        for to, part in ((shi, hi), (slo, lo)):
            to[:half_h, own] = part
            to[half_h:, other] = part if ri == 0 else -part
    copies[0].wait()
    copies[1].wait()
    for ri in range(2):
        n = slice(ri * wide, (ri + 1) * wide)
        y[ri] = (
            jnp.dot(wlo_ref[...], shi[:, n], preferred_element_type=jnp.float32)
            + jnp.dot(whi_ref[...], slo[:, n], preferred_element_type=jnp.float32)
        ) + jnp.dot(whi_ref[...], shi[:, n], preferred_element_type=jnp.float32)
    copies[3].wait()
    period = y.shape[1]
    step_rows = 64
    for b in range(period // step_rows):
        at = slice(b * step_rows, (b + 1) * step_rows)
        turn = phase_ref[at, :].astype(jnp.float32)
        c = turn[:, :TILE] + turn[:, TILE : 2 * TILE]
        d = turn[:, 2 * TILE : 3 * TILE] + turn[:, 3 * TILE :]
        for s in range(most):
            lanes = slice(s * TILE, (s + 1) * TILE)
            yr = y[0, at, lanes]
            yi = y[1, at, lanes]
            for ri, z in enumerate((c * yr - d * yi, d * yr + c * yi)):
                to = slice((ri * most + s) * TILE, (ri * most + s + 1) * TILE)
                hi = z.astype(jnp.bfloat16)
                zhi[at, to] = hi
                zlo[at, to] = (z - hi.astype(jnp.float32)).astype(jnp.bfloat16)
    copies[2].wait()
    thi, tlo = t_ref[:, : sums.shape[1]], t_ref[:, sums.shape[1] :]
    sums[...] = (
        jnp.dot(zhi[...], tlo, preferred_element_type=jnp.float32)
        + jnp.dot(zlo[...], thi, preferred_element_type=jnp.float32)
    ) + jnp.dot(zhi[...], thi, preferred_element_type=jnp.float32)
    half = outs[0].shape[0]
    first = lax.broadcasted_iota(jnp.int32, (half, TILE), 1) < TILE // 2
    for dest in range(n_seg):
        lag = dest * 2 * half
        r, l0 = lag // period, lag % period
        col = slice(r // 2 * TILE, (r // 2 + 1) * TILE)
        low = sums[l0 : l0 + half, col]
        high = sums[l0 + half : l0 + 2 * half, col]
        if r % 2 == 0:
            high = pltpu.roll(high, TILE // 2, 1)
        else:
            low = pltpu.roll(low, TILE // 2, 1)
        parts[dest] = jnp.where(first, low, high)
    for k in range(n_seg):
        outs[k][...] = parts[jnp.bitwise_xor(me_ref[0], k)]


def tables_kernel(most, turns, shift, whi_ref, wlo_ref, phase_ref, out_ref, t_ref, sems):
    h = whi_ref.shape[0]
    k = t_ref.shape[0]
    copies = [
        pltpu.make_async_copy(whi_ref, out_ref.at[pl.ds(0, h)], sems.at[0]),
        pltpu.make_async_copy(wlo_ref, out_ref.at[pl.ds(h, h)], sems.at[1]),
        pltpu.make_async_copy(phase_ref, out_ref.at[pl.ds(2 * h + k, h)], sems.at[2]),
        pltpu.make_async_copy(t_ref, out_ref.at[pl.ds(2 * h, k)], sems.at[3]),
    ]
    for copy in copies[:3]:
        copy.start()
    shape = (most * TILE, turns * most * CC)
    row = lax.broadcasted_iota(jnp.int32, shape, 0)
    col = lax.broadcasted_iota(jnp.int32, shape, 1)
    same = (row // TILE == col // CC % most) & (row % CC == col % CC)
    eighths = (col // (most * CC) - shift) * (row // CC % GROUPS)
    diagonal = jnp.float32(math.sqrt(0.5))
    for ri in range(2):
        e = jnp.bitwise_and(eighths + 2 * ri, 7)
        size = jnp.where(e % 4 == 2, 0.0, jnp.where(e % 2 == 0, 1.0, diagonal))
        t = jnp.where(same, jnp.where((e > 2) & (e < 6), -size, size), 0.0)
        at = slice(ri * most * TILE, (ri + 1) * most * TILE)
        hi = t.astype(jnp.bfloat16)
        t_ref[at, : shape[1]] = hi
        t_ref[at, shape[1] :] = (t - hi.astype(jnp.float32)).astype(jnp.bfloat16)
    copies[3].start()
    for copy in copies:
        copy.wait()


def split(x):
    hi = x.astype(np.float32).astype(jnp.bfloat16)
    return hi, (x - hi.astype(np.float64)).astype(np.float32).astype(jnp.bfloat16)


def make_tables(freq, most):
    h = freq // GROUPS
    period = 2 * h
    turns = LAG // period
    angle = np.arange(period)[:, None] * np.arange(h)[None, :] % period
    angle = angle * (2.0 * math.pi / period)
    whi, wlo = split(np.concatenate([np.cos(angle), np.sin(angle)], 1))
    fb = np.arange(TILE) // CC
    phase = ((np.arange(period)[:, None] * fb[None, :]) % (2 * freq)) * (math.pi / freq)
    scale = 1.0 / math.sqrt(freq)
    phase = np.concatenate(split(np.cos(phase) * scale) + split(np.sin(phase) * scale), 1)
    hbm = pl.BlockSpec(memory_space=pltpu.HBM)
    width = period
    return pl.pallas_call(
        functools.partial(tables_kernel, most, turns, LAG // 2 // period),
        out_shape=jax.ShapeDtypeStruct((48 << 10, width), jnp.bfloat16),
        in_specs=[hbm] * 3,
        out_specs=hbm,
        scratch_shapes=[
            pltpu.VMEM((2 * most * TILE, width), jnp.bfloat16),
            pltpu.SemaphoreType.DMA((4,)),
        ],
        name="tables",
        cost_estimate=SMALL,
    )(jnp.asarray(whi), jnp.asarray(wlo), jnp.asarray(phase))


def dft(me, tables, blocks, freq, n_seg, n_pair, most):
    period = 2 * (freq // GROUPS)
    smem = pl.BlockSpec(memory_space=pltpu.SMEM)
    vmem = pl.BlockSpec(memory_space=pltpu.VMEM)
    half = LAG // n_seg // 2
    wide = most * TILE
    return pl.pallas_call(
        functools.partial(dft_kernel, n_seg, n_pair, most),
        out_shape=[jax.ShapeDtypeStruct((half, TILE), jnp.float32)] * n_seg,
        in_specs=[smem, pl.BlockSpec(memory_space=pltpu.HBM)] + [vmem] * len(blocks),
        out_specs=[vmem] * n_seg,
        scratch_shapes=[
            pltpu.VMEM((period, period), jnp.bfloat16),
            pltpu.VMEM((period, period), jnp.bfloat16),
            pltpu.VMEM((2 * wide, period), jnp.bfloat16),
            pltpu.VMEM((period, 4 * TILE), jnp.bfloat16),
            pltpu.SemaphoreType.DMA((4,)),
            pltpu.VMEM((2, period // 2, wide), jnp.float32),
            pltpu.VMEM((period, 2 * wide), jnp.bfloat16),
            pltpu.VMEM((period, 2 * wide), jnp.bfloat16),
            pltpu.VMEM((2, period, wide), jnp.float32),
            pltpu.VMEM((period, 2 * wide), jnp.bfloat16),
            pltpu.VMEM((period, 2 * wide), jnp.bfloat16),
            pltpu.VMEM((period, LAG // period * most * CC), jnp.float32),
            pltpu.VMEM((n_seg, half, TILE), jnp.float32),
        ],
        name="dft",
        compiler_params=pltpu.CompilerParams(vmem_limit_bytes=24 << 20),
        cost_estimate=SMALL,
    )(me, tables, *blocks)


def unpack_kernel(n_seg, chunks, most, me_ref, *refs):
    ins = refs[: n_seg * chunks]
    out_ref, buf = refs[n_seg * chunks :]
    half = ins[0].shape[0]
    for k in range(n_seg):
        z = jnp.bitwise_xor(me_ref[0], k)
        for ch in range(chunks):
            buf[z * chunks + ch] = ins[ch * n_seg + k][...]
    step_rows = 16

    def one(b, _):
        at = pl.multiple_of(b * step_rows, step_rows)
        v = transpose_groups([buf[i, pl.ds(at, step_rows), :] for i in range(GROUPS)])
        for h in range(2):
            for s in range(most):
                out_ref[pl.ds(h * half + at, step_rows), s, :] = v[h * most + s]
        return 0

    lax.fori_loop(0, half // step_rows, one, 0, unroll=4)


def unpack(me, parts, n_seg, chunks, most):
    half = parts[0].shape[0]
    smem = pl.BlockSpec(memory_space=pltpu.SMEM)
    vmem = pl.BlockSpec(memory_space=pltpu.VMEM)
    return pl.pallas_call(
        functools.partial(unpack_kernel, n_seg, chunks, most),
        out_shape=jax.ShapeDtypeStruct((2 * half, most, TILE), jnp.float32),
        in_specs=[smem] + [vmem] * len(parts),
        out_specs=vmem,
        scratch_shapes=[pltpu.VMEM((GROUPS, half, TILE), jnp.float32)],
        name="unpack",
        compiler_params=pltpu.CompilerParams(vmem_limit_bytes=12 << 20),
        cost_estimate=SMALL,
    )(me, *parts)


def exchange(blocks, axis, size):
    return [blocks[0]] + [
        lax.ppermute(blocks[k], axis, [(i, i ^ k) for i in range(size)])
        for k in range(1, size)
    ]


def exchange_plane(blocks, n_pair):
    direct = [blocks[0]] + [
        lax.ppermute(blocks[k], "pair", [(i, i ^ (2 * k)) for i in range(n_pair)])
        for k in range(1, n_pair // 2)
    ]
    swap = [(i, i ^ 1) for i in range(n_pair)]
    return direct + [lax.ppermute(d, "pair", swap) for d in direct]


def body(spectra, pair_lists, pair_counts):
    n_pair = lax.axis_size("pair")
    n_seg = lax.axis_size("seg")
    freq = spectra.shape[2]
    most = pair_lists.shape[0]
    tiles = spectra.shape[3] // TILE
    chunks = GROUPS // n_seg
    rows = freq // n_pair // GROUPS
    me = jnp.stack([lax.axis_index("seg"), lax.axis_index("pair")]).astype(jnp.int32)
    x = spectra.reshape(2, freq, spectra.shape[3])
    lists = jnp.concatenate([pair_lists.reshape(-1), pair_counts])
    tables = make_tables(freq, most)
    packed = [pack(x, chunk, n_seg, n_pair) for chunk in range(chunks)]
    lists, packed[-1] = lax.optimization_barrier((lists, packed[-1]))
    table = lax.all_gather(lists, "pair", axis=0)
    if chunks > 1:
        table, packed[1], _ = lax.optimization_barrier((table, packed[1], tables))
    done = []
    lags = None
    for sent in packed:
        got = lax.all_to_all(
            sent.reshape(n_seg * n_pair, tiles, 2, rows, TILE),
            ("seg", "pair"),
            split_axis=0,
            concat_axis=0,
            tiled=True,
        )
        if lags is not None:
            got, _ = lax.optimization_barrier((got, lags))
        spec = got.reshape(n_seg, n_pair * tiles, 2, rows, TILE)
        blocks = stacks(me, table, [spec], SMALL, n_seg, n_pair, most)
        blocks = exchange_plane(blocks, n_pair)
        lags = dft(me, tables, blocks, freq, n_seg, n_pair, most)
        done += exchange(lags, "seg", n_seg)
    return unpack(me, done, n_seg, chunks, most)


def solution(mesh):
    return jax.shard_map(
        body,
        mesh=mesh,
        in_specs=(P("seg", None, None, "pair"), P("pair", None), P("pair")),
        out_specs=P("seg", "pair", None),
        check_vma=False,
    )
```

```python
import functools
import math

import jax
import jax.numpy as jnp
import numpy as np
from jax import lax
from jax.experimental import pallas as pl
from jax.experimental.pallas import tpu as pltpu
from jax.sharding import PartitionSpec as P

TILE = 128
LAG = 2048
GROUPS = 8
SMALL = pl.CostEstimate(flops=1, bytes_accessed=1, transcendentals=0)
CC = TILE // GROUPS


def lane_groups(shape):
    return lax.broadcasted_iota(jnp.int32, shape, len(shape) - 1) // CC


def shift_groups(x, by):
    return pltpu.roll(x, (by * CC) % TILE, x.ndim - 1)


def transpose_groups(vectors):
    v = list(vectors)
    grp = lane_groups(v[0].shape)
    for bit in (4, 2, 1):
        low = (grp & bit) == 0
        for i in range(GROUPS):
            if i & bit:
                continue
            a, b = v[i], v[i | bit]
            v[i] = jnp.where(low, a, shift_groups(b, bit))
            v[i | bit] = jnp.where(low, shift_groups(a, -bit), b)
    return v


def reduce_groups(vectors):
    v = list(vectors)
    grp = lane_groups(v[0].shape)
    low = (grp & 4) == 0
    v = [
        jnp.where(low, v[i], v[i + 4])
        + shift_groups(jnp.where(low, v[i + 4], v[i]), 4)
        for i in range(4)
    ]
    for bit in (2, 1):
        low = (grp & bit) == 0
        v = [
            jnp.where(low, v[i], v[i + bit])
            + jnp.where(low, shift_groups(v[i], -bit), shift_groups(v[i + bit], bit))
            for i in range(bit)
        ]
    return v[0]


def selection(n_seg, chunk, chans):
    wide = chans // TILE * n_seg * CC
    row = lax.broadcasted_iota(jnp.int32, (chans, wide), 0)
    col = lax.broadcasted_iota(jnp.int32, (chans, wide), 1)
    group = col // CC
    want = (
        group // n_seg * TILE
        + group % n_seg * (TILE // n_seg)
        + chunk * CC
        + col % CC
    )
    return (row == want).astype(jnp.bfloat16)


def pack_kernel(n_seg, n_pair, chunk, x_ref, out_ref, buf_ref):
    band = x_ref.shape[1] // n_pair
    sel = selection(n_seg, chunk, x_ref.shape[2])
    rows = band // GROUPS
    for p in range(n_pair):
        for ri in range(2):
            for part in range(sel.shape[1] // TILE):
                lanes = slice(part * TILE, (part + 1) * TILE)
                buf = buf_ref.at[p % 2, ri]
                buf[...] = jnp.dot(
                    x_ref[ri, p * band : (p + 1) * band, :],
                    sel[:, lanes],
                    preferred_element_type=jnp.float32,
                )
                v = [buf[pl.ds(fb, rows, stride=GROUPS), :] for fb in range(GROUPS)]
                v = transpose_groups(v)
                for g in range(GROUPS):
                    t, z = divmod(part * GROUPS + g, n_seg)
                    out_ref[z, p, t, ri] = v[g].astype(jnp.bfloat16)


def pack(x, chunk, n_seg, n_pair):
    _, freq, chans = x.shape
    band = freq // n_pair
    shape = (n_seg, n_pair, chans // TILE, 2, band // GROUPS, TILE)
    return pl.pallas_call(
        functools.partial(pack_kernel, n_seg, n_pair, chunk),
        out_shape=jax.ShapeDtypeStruct(shape, jnp.bfloat16),
        in_specs=[pl.BlockSpec(memory_space=pltpu.VMEM)],
        out_specs=pl.BlockSpec(memory_space=pltpu.VMEM),
        scratch_shapes=[pltpu.VMEM((2, 2, band, TILE), jnp.float32)],
        name="pack",
        cost_estimate=SMALL,
    )(x)


def stack_kernel(n_seg, n_pair, most, n_specs, me_ref, table_ref, *refs):
    specs, out_refs = refs[:n_specs], refs[n_specs:]
    parts = [r.at[g] for r in specs for g in range(r.shape[0])]
    inv = 1.0 / float(n_seg * n_seg)
    for k in range(n_pair):
        owner = jnp.bitwise_xor(me_ref[1], k)
        count = table_ref[owner, 2 * most]
        out_ref = out_refs[k // 2].at[k % 2]

        def one(s, _):
            src = table_ref[owner, 2 * s]
            rcv = table_ref[owner, 2 * s + 1]

            @pl.when(s < count)
            def _():
                lr = li = pr = pi = None
                for g in range(n_seg):
                    a0 = parts[g][src, 0].astype(jnp.float32)
                    a1 = parts[g][src, 1].astype(jnp.float32)
                    b0 = parts[g][rcv, 0].astype(jnp.float32)
                    b1 = parts[g][rcv, 1].astype(jnp.float32)
                    cr = a0 * b0 + a1 * b1
                    ci = a1 * b0 - a0 * b1
                    m = lax.rsqrt(cr * cr + ci * ci + 1.0)
                    if g == 0:
                        lr, li, pr, pi = cr, ci, cr * m, ci * m
                    else:
                        lr, li, pr, pi = lr + cr, li + ci, pr + cr * m, pi + ci * m
                w = (pr * pr + pi * pi) * inv
                out_ref[s, 0] = lr * w
                out_ref[s, 1] = li * w

            @pl.when(s >= count)
            def _():
                out_ref[s] = jnp.zeros(out_ref.shape[1:], jnp.float32)

            return 0

        lax.fori_loop(0, most, one, 0)


def stacks(me, table, specs, cost, n_seg, n_pair, most):
    rows = specs[0].shape[3]
    arrays = n_pair // 2
    shape = (n_pair // arrays, most, 2, rows, TILE)
    smem = pl.BlockSpec(memory_space=pltpu.SMEM)
    vmem = pl.BlockSpec(memory_space=pltpu.VMEM)
    return pl.pallas_call(
        functools.partial(stack_kernel, n_seg, n_pair, most, len(specs)),
        out_shape=[jax.ShapeDtypeStruct(shape, jnp.float32)] * arrays,
        in_specs=[smem, smem] + [vmem] * len(specs),
        out_specs=[vmem] * arrays,
        name="stack",
        compiler_params=pltpu.CompilerParams(vmem_limit_bytes=8 << 20),
        cost_estimate=cost,
    )(me, table, *specs)


def dft_kernel(n_seg, n_pair, most, me_ref, tables_ref, *refs):
    ins, outs = refs[:n_pair], refs[n_pair : n_pair + n_seg]
    w_ref, phase_ref, t_ref, sems = refs[n_pair + n_seg :][:4]
    whi_ref, wlo_ref, s32, shi, slo, y, zhi, zlo, sums, parts = refs[
        n_pair + n_seg + 4 :
    ]
    copies = []
    row = 0
    for i, to in enumerate((w_ref.at[0], w_ref.at[1], phase_ref, t_ref)):
        src = tables_ref.at[pl.ds(row, to.shape[0])]
        copies.append(pltpu.make_async_copy(src, to, sems.at[i]))
        copies[-1].start()
        row += to.shape[0]
    rows = ins[0].shape[3]
    half_h = whi_ref.shape[1] // 2
    wide = most * TILE
    for k in range(n_pair):
        band = jnp.bitwise_xor(me_ref[1], k)
        src = ins[k % 2 * (n_pair // 2) + k // 2].at[k % 2]
        at = pl.ds(pl.multiple_of(band * rows, rows), rows)
        for s in range(most):
            for ri in range(2):
                s32[ri, at, s * TILE : (s + 1) * TILE] = src[s, ri]
    for ri in range(2):
        full = s32[ri]
        hi = full.astype(jnp.bfloat16)
        lo = (full - hi.astype(jnp.float32)).astype(jnp.bfloat16)
        own = slice(ri * wide, (ri + 1) * wide)
        other = slice((1 - ri) * wide, (2 - ri) * wide)
        for to, part in ((shi, hi), (slo, lo)):
            to[:half_h, own] = part
            to[half_h:, other] = part if ri == 0 else -part
    copies[0].wait()
    copies[1].wait()
    for ri in range(2):
        hi = w_ref[ri].astype(jnp.bfloat16)
        n = slice(ri * half_h, (ri + 1) * half_h)
        whi_ref[:, n] = hi
        wlo_ref[:, n] = (w_ref[ri] - hi.astype(jnp.float32)).astype(jnp.bfloat16)
    for ri in range(2):
        n = slice(ri * wide, (ri + 1) * wide)
        y[ri] = (
            jnp.dot(wlo_ref[...], shi[:, n], preferred_element_type=jnp.float32)
            + jnp.dot(whi_ref[...], slo[:, n], preferred_element_type=jnp.float32)
        ) + jnp.dot(whi_ref[...], shi[:, n], preferred_element_type=jnp.float32)
    copies[2].wait()
    period = y.shape[1]
    step_rows = 64
    for b in range(period // step_rows):
        at = slice(b * step_rows, (b + 1) * step_rows)
        c = phase_ref[at, :TILE]
        d = phase_ref[at, TILE:]
        for s in range(most):
            lanes = slice(s * TILE, (s + 1) * TILE)
            yr = y[0, at, lanes]
            yi = y[1, at, lanes]
            for ri, z in enumerate((c * yr - d * yi, d * yr + c * yi)):
                to = slice((ri * most + s) * TILE, (ri * most + s + 1) * TILE)
                hi = z.astype(jnp.bfloat16)
                zhi[at, to] = hi
                zlo[at, to] = (z - hi.astype(jnp.float32)).astype(jnp.bfloat16)
    copies[3].wait()
    thi = t_ref[...].astype(jnp.bfloat16)
    tlo = (t_ref[...] - thi.astype(jnp.float32)).astype(jnp.bfloat16)
    sums[...] = (
        jnp.dot(zhi[...], tlo, preferred_element_type=jnp.float32)
        + jnp.dot(zlo[...], thi, preferred_element_type=jnp.float32)
    ) + jnp.dot(zhi[...], thi, preferred_element_type=jnp.float32)
    half = outs[0].shape[0]
    first = lax.broadcasted_iota(jnp.int32, (half, TILE), 1) < TILE // 2
    for dest in range(n_seg):
        lag = dest * 2 * half
        r, l0 = lag // period, lag % period
        col = slice(r // 2 * TILE, (r // 2 + 1) * TILE)
        low = sums[l0 : l0 + half, col]
        high = sums[l0 + half : l0 + 2 * half, col]
        if r % 2 == 0:
            high = pltpu.roll(high, TILE // 2, 1)
        else:
            low = pltpu.roll(low, TILE // 2, 1)
        parts[dest] = jnp.where(first, low, high)
    for k in range(n_seg):
        outs[k][...] = parts[jnp.bitwise_xor(me_ref[0], k)]


def tables_kernel(most, turns, shift, fixed_ref, out_ref, t_ref, sems):
    used = fixed_ref.shape[0]
    copies = [
        pltpu.make_async_copy(fixed_ref, out_ref.at[pl.ds(0, used)], sems.at[0]),
        pltpu.make_async_copy(
            t_ref, out_ref.at[pl.ds(used, t_ref.shape[0])], sems.at[1]
        ),
    ]
    copies[0].start()
    shape = (most * TILE, turns * most * CC)
    row = lax.broadcasted_iota(jnp.int32, shape, 0)
    col = lax.broadcasted_iota(jnp.int32, shape, 1)
    same = (row // TILE == col // CC % most) & (row % CC == col % CC)
    eighths = (col // (most * CC) - shift) * (row // CC % GROUPS)
    diagonal = jnp.float32(math.sqrt(0.5))
    for ri in range(2):
        e = jnp.bitwise_and(eighths + 2 * ri, 7)
        size = jnp.where(e % 4 == 2, 0.0, jnp.where(e % 2 == 0, 1.0, diagonal))
        t = jnp.where(same, jnp.where((e > 2) & (e < 6), -size, size), 0.0)
        t_ref[ri * most * TILE : (ri + 1) * most * TILE, :] = t
    copies[1].start()
    for copy in copies:
        copy.wait()


def make_tables(freq, most):
    h = freq // GROUPS
    period = 2 * h
    turns = LAG // period
    width = turns * most * CC
    angle = np.arange(period)[:, None] * np.arange(h)[None, :] % period
    angle = angle * (2.0 * math.pi / period)
    fb = np.arange(TILE) // CC
    phase = ((np.arange(period)[:, None] * fb[None, :]) % (2 * freq)) * (math.pi / freq)
    scale = 1.0 / math.sqrt(freq)
    phase = np.concatenate([np.cos(phase), np.sin(phase)], 1) * scale
    fixed = np.concatenate([np.cos(angle), np.sin(angle), phase]).astype(np.float32)
    return pl.pallas_call(
        functools.partial(tables_kernel, most, turns, LAG // 2 // period),
        out_shape=jax.ShapeDtypeStruct((48 << 10, width), jnp.float32),
        in_specs=[pl.BlockSpec(memory_space=pltpu.VMEM)],
        out_specs=pl.BlockSpec(memory_space=pltpu.HBM),
        scratch_shapes=[
            pltpu.VMEM((2 * most * TILE, width), jnp.float32),
            pltpu.SemaphoreType.DMA((2,)),
        ],
        name="tables",
        cost_estimate=SMALL,
    )(jnp.asarray(fixed))


def dft(me, tables, blocks, freq, n_seg, n_pair, most):
    period = 2 * (freq // GROUPS)
    smem = pl.BlockSpec(memory_space=pltpu.SMEM)
    vmem = pl.BlockSpec(memory_space=pltpu.VMEM)
    half = LAG // n_seg // 2
    wide = most * TILE
    return pl.pallas_call(
        functools.partial(dft_kernel, n_seg, n_pair, most),
        out_shape=[jax.ShapeDtypeStruct((half, TILE), jnp.float32)] * n_seg,
        in_specs=[smem, pl.BlockSpec(memory_space=pltpu.HBM)] + [vmem] * len(blocks),
        out_specs=[vmem] * n_seg,
        scratch_shapes=[
            pltpu.VMEM((2, period, period // 2), jnp.float32),
            pltpu.VMEM((period, 2 * TILE), jnp.float32),
            pltpu.VMEM((2 * wide, LAG // period * most * CC), jnp.float32),
            pltpu.SemaphoreType.DMA((4,)),
            pltpu.VMEM((period, period), jnp.bfloat16),
            pltpu.VMEM((period, period), jnp.bfloat16),
            pltpu.VMEM((2, period // 2, wide), jnp.float32),
            pltpu.VMEM((period, 2 * wide), jnp.bfloat16),
            pltpu.VMEM((period, 2 * wide), jnp.bfloat16),
            pltpu.VMEM((2, period, wide), jnp.float32),
            pltpu.VMEM((period, 2 * wide), jnp.bfloat16),
            pltpu.VMEM((period, 2 * wide), jnp.bfloat16),
            pltpu.VMEM((period, LAG // period * most * CC), jnp.float32),
            pltpu.VMEM((n_seg, half, TILE), jnp.float32),
        ],
        name="dft",
        compiler_params=pltpu.CompilerParams(vmem_limit_bytes=24 << 20),
        cost_estimate=SMALL,
    )(me, tables, *blocks)


def unpack_kernel(n_seg, chunks, most, me_ref, *refs):
    ins = refs[: n_seg * chunks]
    out_ref, buf = refs[n_seg * chunks :]
    half = ins[0].shape[0]
    for k in range(n_seg):
        z = jnp.bitwise_xor(me_ref[0], k)
        for ch in range(chunks):
            buf[z * chunks + ch] = ins[ch * n_seg + k][...]
    step_rows = 16

    def one(b, _):
        at = pl.multiple_of(b * step_rows, step_rows)
        v = transpose_groups([buf[i, pl.ds(at, step_rows), :] for i in range(GROUPS)])
        for h in range(2):
            for s in range(most):
                out_ref[pl.ds(h * half + at, step_rows), s, :] = v[h * most + s]
        return 0

    lax.fori_loop(0, half // step_rows, one, 0, unroll=4)


def unpack(me, parts, n_seg, chunks, most):
    half = parts[0].shape[0]
    smem = pl.BlockSpec(memory_space=pltpu.SMEM)
    vmem = pl.BlockSpec(memory_space=pltpu.VMEM)
    return pl.pallas_call(
        functools.partial(unpack_kernel, n_seg, chunks, most),
        out_shape=jax.ShapeDtypeStruct((2 * half, most, TILE), jnp.float32),
        in_specs=[smem] + [vmem] * len(parts),
        out_specs=vmem,
        scratch_shapes=[pltpu.VMEM((GROUPS, half, TILE), jnp.float32)],
        name="unpack",
        compiler_params=pltpu.CompilerParams(vmem_limit_bytes=12 << 20),
        cost_estimate=SMALL,
    )(me, *parts)


def exchange(blocks, axis, size):
    return [blocks[0]] + [
        lax.ppermute(blocks[k], axis, [(i, i ^ k) for i in range(size)])
        for k in range(1, size)
    ]


def exchange_plane(blocks, n_pair):
    direct = [blocks[0]] + [
        lax.ppermute(blocks[k], "pair", [(i, i ^ (2 * k)) for i in range(n_pair)])
        for k in range(1, n_pair // 2)
    ]
    swap = [(i, i ^ 1) for i in range(n_pair)]
    return direct + [lax.ppermute(d, "pair", swap) for d in direct]


def body(spectra, pair_lists, pair_counts):
    n_pair = lax.axis_size("pair")
    n_seg = lax.axis_size("seg")
    freq = spectra.shape[2]
    most = pair_lists.shape[0]
    tiles = spectra.shape[3] // TILE
    chunks = GROUPS // n_seg
    rows = freq // n_pair // GROUPS
    me = jnp.stack([lax.axis_index("seg"), lax.axis_index("pair")]).astype(jnp.int32)
    x = spectra.reshape(2, freq, spectra.shape[3])
    lists = jnp.concatenate([pair_lists.reshape(-1), pair_counts])
    tables = make_tables(freq, most)
    packed = [pack(x, chunk, n_seg, n_pair) for chunk in range(chunks)]
    lists, packed[-1] = lax.optimization_barrier((lists, packed[-1]))
    table = lax.all_gather(lists, "pair", axis=0)
    if chunks > 1:
        table, packed[1], _ = lax.optimization_barrier((table, packed[1], tables))
    done = []
    lags = None
    for sent in packed:
        got = lax.all_to_all(
            sent.reshape(n_seg * n_pair, tiles, 2, rows, TILE),
            ("seg", "pair"),
            split_axis=0,
            concat_axis=0,
            tiled=True,
        )
        if lags is not None:
            got, _ = lax.optimization_barrier((got, lags))
        spec = got.reshape(n_seg, n_pair * tiles, 2, rows, TILE)
        blocks = stacks(me, table, [spec], SMALL, n_seg, n_pair, most)
        blocks = exchange_plane(blocks, n_pair)
        lags = dft(me, tables, blocks, freq, n_seg, n_pair, most)
        done += exchange(lags, "seg", n_seg)
    return unpack(me, done, n_seg, chunks, most)


def solution(mesh):
    return jax.shard_map(
        body,
        mesh=mesh,
        in_specs=(P("seg", None, None, "pair"), P("pair", None), P("pair")),
        out_specs=P("seg", "pair", None),
        check_vma=False,
    )
```

```python
import functools
import math

import jax
import jax.numpy as jnp
import numpy as np
from jax import lax
from jax.experimental import pallas as pl
from jax.experimental.pallas import tpu as pltpu
from jax.sharding import PartitionSpec as P

TILE = 128
LAG = 2048
GROUPS = 8
SMALL = pl.CostEstimate(flops=1, bytes_accessed=1, transcendentals=0)
CC = TILE // GROUPS


def lane_groups(shape):
    return lax.broadcasted_iota(jnp.int32, shape, len(shape) - 1) // CC


def shift_groups(x, by):
    return pltpu.roll(x, (by * CC) % TILE, x.ndim - 1)


def top_exponent(largest):
    return jnp.maximum(jnp.floor(jnp.log2(jnp.maximum(largest, 1e-36))), -100.0)


def encode(a, b, top):
    m = jnp.maximum(jnp.maximum(jnp.abs(a), jnp.abs(b)), 1e-36)
    e = jnp.floor(jnp.log2(m))
    e = jnp.minimum(jnp.maximum(jnp.maximum(e, top - 63.0), -110.0), top)
    s = jnp.exp2(11.0 - e)
    qa, qb = (
        jnp.clip(jnp.floor(x * s + 0.5), -4095.0, 4095.0).astype(jnp.int32) + 4096
        for x in (a, b)
    )
    field = (e - (top - 63.0)).astype(jnp.int32)
    return (field << 26) | (qa << 13) | qb


ZERO = (4096 << 13) | 4096


def decode(code, top):
    e = ((code >> 26) & 63).astype(jnp.float32) + (top - 63.0)
    s = jnp.exp2(e - 11.0)
    a, b = (((q & 8191) - 4096).astype(jnp.float32) * s for q in (code >> 13, code))
    return a, b


def transpose_groups(vectors):
    v = list(vectors)
    grp = lane_groups(v[0].shape)
    for bit in (4, 2, 1):
        low = (grp & bit) == 0
        for i in range(GROUPS):
            if i & bit:
                continue
            a, b = v[i], v[i | bit]
            v[i] = jnp.where(low, a, shift_groups(b, bit))
            v[i | bit] = jnp.where(low, shift_groups(a, -bit), b)
    return v


def reduce_groups(vectors):
    v = list(vectors)
    grp = lane_groups(v[0].shape)
    low = (grp & 4) == 0
    v = [
        jnp.where(low, v[i], v[i + 4])
        + shift_groups(jnp.where(low, v[i + 4], v[i]), 4)
        for i in range(4)
    ]
    for bit in (2, 1):
        low = (grp & bit) == 0
        v = [
            jnp.where(low, v[i], v[i + bit])
            + jnp.where(low, shift_groups(v[i], -bit), shift_groups(v[i + bit], bit))
            for i in range(bit)
        ]
    return v[0]


def selection(n_seg, chunk, chans):
    wide = chans // TILE * n_seg * CC
    row = lax.broadcasted_iota(jnp.int32, (chans, wide), 0)
    col = lax.broadcasted_iota(jnp.int32, (chans, wide), 1)
    group = col // CC
    want = (
        group // n_seg * TILE
        + group % n_seg * (TILE // n_seg)
        + chunk * CC
        + col % CC
    )
    return (row == want).astype(jnp.bfloat16)


def pack_kernel(n_seg, n_pair, chunk, x_ref, out_ref, buf_ref):
    band = x_ref.shape[1] // n_pair
    sel = selection(n_seg, chunk, x_ref.shape[2])
    rows = band // GROUPS
    for p in range(n_pair):
        for ri in range(2):
            for part in range(sel.shape[1] // TILE):
                lanes = slice(part * TILE, (part + 1) * TILE)
                buf = buf_ref.at[p % 2, ri]
                buf[...] = jnp.dot(
                    x_ref[ri, p * band : (p + 1) * band, :],
                    sel[:, lanes],
                    preferred_element_type=jnp.float32,
                )
                v = [buf[pl.ds(fb, rows, stride=GROUPS), :] for fb in range(GROUPS)]
                v = transpose_groups(v)
                for g in range(GROUPS):
                    t, z = divmod(part * GROUPS + g, n_seg)
                    out_ref[z, p, t, ri] = v[g].astype(jnp.bfloat16)


def pack(x, chunk, n_seg, n_pair):
    _, freq, chans = x.shape
    band = freq // n_pair
    shape = (n_seg, n_pair, chans // TILE, 2, band // GROUPS, TILE)
    return pl.pallas_call(
        functools.partial(pack_kernel, n_seg, n_pair, chunk),
        out_shape=jax.ShapeDtypeStruct(shape, jnp.bfloat16),
        in_specs=[pl.BlockSpec(memory_space=pltpu.VMEM)],
        out_specs=pl.BlockSpec(memory_space=pltpu.VMEM),
        scratch_shapes=[pltpu.VMEM((2, 2, band, TILE), jnp.float32)],
        name="pack",
        cost_estimate=SMALL,
    )(x)


def stack_kernel(n_seg, n_pair, most, me_ref, table_ref, spec_ref, *refs):
    outs, (sum_ref, big_ref) = refs[:-2], refs[-2:]
    rows = spec_ref.shape[3]
    inv = 1.0 / float(n_seg * n_seg)
    big_ref[...] = jnp.zeros_like(big_ref)
    for k in range(n_pair):
        owner = jnp.bitwise_xor(me_ref[1], k)
        count = table_ref[owner, 2 * most]

        def one(s, _):
            src = table_ref[owner, 2 * s]
            rcv = table_ref[owner, 2 * s + 1]
            lr = li = pr = pi = None
            for g in range(n_seg):
                a0 = spec_ref[g, src, 0].astype(jnp.float32)
                a1 = spec_ref[g, src, 1].astype(jnp.float32)
                b0 = spec_ref[g, rcv, 0].astype(jnp.float32)
                b1 = spec_ref[g, rcv, 1].astype(jnp.float32)
                cr = a0 * b0 + a1 * b1
                ci = a1 * b0 - a0 * b1
                m = lax.rsqrt(cr * cr + ci * ci + 1.0)
                if g == 0:
                    lr, li, pr, pi = cr, ci, cr * m, ci * m
                else:
                    lr, li, pr, pi = lr + cr, li + ci, pr + cr * m, pi + ci * m
            w = (pr * pr + pi * pi) * inv
            re, im = lr * w, li * w
            sum_ref[k, s, 0] = re
            sum_ref[k, s, 1] = im
            big = jnp.maximum(jnp.abs(re), jnp.abs(im))
            big_ref[...] = jnp.maximum(big_ref[...], big)
            return 0

        lax.fori_loop(0, count, one, 0)
    top = top_exponent(jnp.max(big_ref[...], keepdims=True))
    for k in range(n_pair):
        owner = jnp.bitwise_xor(me_ref[1], k)
        count = table_ref[owner, 2 * most]
        out_ref = outs[k // 2].at[k % 2]

        def code(s, _):
            at = pl.ds(pl.multiple_of(s * rows, rows), rows)
            out_ref[at, :] = encode(sum_ref[k, s, 0], sum_ref[k, s, 1], top)
            return 0

        def dead(s, _):
            at = pl.ds(pl.multiple_of(s * rows, rows), rows)
            out_ref[at, :] = jnp.full((rows, TILE), ZERO, jnp.int32)
            return 0

        lax.fori_loop(0, count, code, 0)
        lax.fori_loop(count, most, dead, 0)
        out_ref[most * rows :, :] = jnp.broadcast_to(top, (8, TILE)).astype(jnp.int32)


def stacks(me, table, spec, n_seg, n_pair, most):
    rows = spec.shape[3]
    shape = (2, most * rows + 8, TILE)
    smem = pl.BlockSpec(memory_space=pltpu.SMEM)
    vmem = pl.BlockSpec(memory_space=pltpu.VMEM)
    return pl.pallas_call(
        functools.partial(stack_kernel, n_seg, n_pair, most),
        out_shape=[jax.ShapeDtypeStruct(shape, jnp.int32)] * (n_pair // 2),
        in_specs=[smem, smem, vmem],
        out_specs=[vmem] * (n_pair // 2),
        scratch_shapes=[
            pltpu.VMEM((n_pair, most, 2, rows, TILE), jnp.float32),
            pltpu.VMEM((rows, TILE), jnp.float32),
        ],
        name="stack",
        compiler_params=pltpu.CompilerParams(vmem_limit_bytes=12 << 20),
        cost_estimate=SMALL,
    )(me, table, spec)


def dft_kernel(n_seg, n_pair, most, me_ref, tables_ref, *refs):
    ins, outs = refs[:n_pair], refs[n_pair : n_pair + n_seg]
    w_ref, phase_ref, t_ref, sems = refs[n_pair + n_seg :][:4]
    whi_ref, wlo_ref, s32, shi, slo, y, zhi, zlo, sums, parts = refs[
        n_pair + n_seg + 4 :
    ]
    copies = []
    row = 0
    for i, to in enumerate((w_ref.at[0], w_ref.at[1], phase_ref, t_ref)):
        src = tables_ref.at[pl.ds(row, to.shape[0])]
        copies.append(pltpu.make_async_copy(src, to, sems.at[i]))
        copies[-1].start()
        row += to.shape[0]
    rows = (ins[0].shape[1] - 8) // most
    half_h = whi_ref.shape[1] // 2
    wide = most * TILE
    for k in range(n_pair):
        band = jnp.bitwise_xor(me_ref[1], k)
        src = ins[k % 2 * (n_pair // 2) + k // 2].at[k % 2]
        at = pl.ds(pl.multiple_of(band * rows, rows), rows)
        top = src[most * rows : most * rows + 1, :].astype(jnp.float32)
        for s in range(most):
            pair = decode(src[s * rows : (s + 1) * rows, :], top)
            for ri in range(2):
                s32[ri, at, s * TILE : (s + 1) * TILE] = pair[ri]
    for ri in range(2):
        full = s32[ri]
        hi = full.astype(jnp.bfloat16)
        lo = (full - hi.astype(jnp.float32)).astype(jnp.bfloat16)
        own = slice(ri * wide, (ri + 1) * wide)
        other = slice((1 - ri) * wide, (2 - ri) * wide)
        for to, part in ((shi, hi), (slo, lo)):
            to[:half_h, own] = part
            to[half_h:, other] = part if ri == 0 else -part
    copies[0].wait()
    copies[1].wait()
    for ri in range(2):
        hi = w_ref[ri].astype(jnp.bfloat16)
        n = slice(ri * half_h, (ri + 1) * half_h)
        whi_ref[:, n] = hi
        wlo_ref[:, n] = (w_ref[ri] - hi.astype(jnp.float32)).astype(jnp.bfloat16)
    for ri in range(2):
        n = slice(ri * wide, (ri + 1) * wide)
        y[ri] = (
            jnp.dot(wlo_ref[...], shi[:, n], preferred_element_type=jnp.float32)
            + jnp.dot(whi_ref[...], slo[:, n], preferred_element_type=jnp.float32)
        ) + jnp.dot(whi_ref[...], shi[:, n], preferred_element_type=jnp.float32)
    copies[2].wait()
    period = y.shape[1]
    step_rows = 64
    for b in range(period // step_rows):
        at = slice(b * step_rows, (b + 1) * step_rows)
        c = phase_ref[at, :TILE]
        d = phase_ref[at, TILE:]
        for s in range(most):
            lanes = slice(s * TILE, (s + 1) * TILE)
            yr = y[0, at, lanes]
            yi = y[1, at, lanes]
            for ri, z in enumerate((c * yr - d * yi, d * yr + c * yi)):
                to = slice((ri * most + s) * TILE, (ri * most + s + 1) * TILE)
                hi = z.astype(jnp.bfloat16)
                zhi[at, to] = hi
                zlo[at, to] = (z - hi.astype(jnp.float32)).astype(jnp.bfloat16)
    copies[3].wait()
    thi = t_ref[...].astype(jnp.bfloat16)
    tlo = (t_ref[...] - thi.astype(jnp.float32)).astype(jnp.bfloat16)
    sums[...] = (
        jnp.dot(zhi[...], tlo, preferred_element_type=jnp.float32)
        + jnp.dot(zlo[...], thi, preferred_element_type=jnp.float32)
    ) + jnp.dot(zhi[...], thi, preferred_element_type=jnp.float32)
    half = parts.shape[1]
    big = None
    first = lax.broadcasted_iota(jnp.int32, (half, TILE), 1) < TILE // 2
    for dest in range(n_seg):
        lag = dest * 2 * half
        r, l0 = lag // period, lag % period
        col = slice(r // 2 * TILE, (r // 2 + 1) * TILE)
        low = sums[l0 : l0 + half, col]
        high = sums[l0 + half : l0 + 2 * half, col]
        if r % 2 == 0:
            high = pltpu.roll(high, TILE // 2, 1)
        else:
            low = pltpu.roll(low, TILE // 2, 1)
        part = jnp.where(first, low, high)
        parts[dest] = part
        part = jnp.max(jnp.abs(part), axis=0, keepdims=True)
        big = part if big is None else jnp.maximum(big, part)
    top = top_exponent(jnp.max(big, keepdims=True))
    for k in range(n_seg):
        part = parts[jnp.bitwise_xor(me_ref[0], k)]
        outs[k][: half // 2, :] = encode(part[: half // 2], part[half // 2 :], top)
        outs[k][half // 2 :, :] = jnp.broadcast_to(top, (8, TILE)).astype(jnp.int32)


def tables_kernel(most, turns, shift, fixed_ref, out_ref, t_ref, sems):
    used = fixed_ref.shape[0]
    copies = [
        pltpu.make_async_copy(fixed_ref, out_ref.at[pl.ds(0, used)], sems.at[0]),
        pltpu.make_async_copy(
            t_ref, out_ref.at[pl.ds(used, t_ref.shape[0])], sems.at[1]
        ),
    ]
    copies[0].start()
    shape = (most * TILE, turns * most * CC)
    row = lax.broadcasted_iota(jnp.int32, shape, 0)
    col = lax.broadcasted_iota(jnp.int32, shape, 1)
    same = (row // TILE == col // CC % most) & (row % CC == col % CC)
    eighths = (col // (most * CC) - shift) * (row // CC % GROUPS)
    diagonal = jnp.float32(math.sqrt(0.5))
    for ri in range(2):
        e = jnp.bitwise_and(eighths + 2 * ri, 7)
        size = jnp.where(e % 4 == 2, 0.0, jnp.where(e % 2 == 0, 1.0, diagonal))
        t = jnp.where(same, jnp.where((e > 2) & (e < 6), -size, size), 0.0)
        t_ref[ri * most * TILE : (ri + 1) * most * TILE, :] = t
    copies[1].start()
    for copy in copies:
        copy.wait()


def make_tables(freq, most):
    h = freq // GROUPS
    period = 2 * h
    turns = LAG // period
    width = turns * most * CC
    angle = np.arange(period)[:, None] * np.arange(h)[None, :] % period
    angle = angle * (2.0 * math.pi / period)
    fb = np.arange(TILE) // CC
    phase = ((np.arange(period)[:, None] * fb[None, :]) % (2 * freq)) * (math.pi / freq)
    scale = 1.0 / math.sqrt(freq)
    phase = np.concatenate([np.cos(phase), np.sin(phase)], 1) * scale
    fixed = np.concatenate([np.cos(angle), np.sin(angle), phase]).astype(np.float32)
    return pl.pallas_call(
        functools.partial(tables_kernel, most, turns, LAG // 2 // period),
        out_shape=jax.ShapeDtypeStruct((48 << 10, width), jnp.float32),
        in_specs=[pl.BlockSpec(memory_space=pltpu.VMEM)],
        out_specs=pl.BlockSpec(memory_space=pltpu.HBM),
        scratch_shapes=[
            pltpu.VMEM((2 * most * TILE, width), jnp.float32),
            pltpu.SemaphoreType.DMA((2,)),
        ],
        name="tables",
        cost_estimate=SMALL,
    )(jnp.asarray(fixed))


def dft(me, tables, blocks, freq, n_seg, n_pair, most):
    period = 2 * (freq // GROUPS)
    smem = pl.BlockSpec(memory_space=pltpu.SMEM)
    vmem = pl.BlockSpec(memory_space=pltpu.VMEM)
    half = LAG // n_seg // 2
    wide = most * TILE
    return pl.pallas_call(
        functools.partial(dft_kernel, n_seg, n_pair, most),
        out_shape=[jax.ShapeDtypeStruct((half // 2 + 8, TILE), jnp.int32)] * n_seg,
        in_specs=[smem, pl.BlockSpec(memory_space=pltpu.HBM)] + [vmem] * len(blocks),
        out_specs=[vmem] * n_seg,
        scratch_shapes=[
            pltpu.VMEM((2, period, period // 2), jnp.float32),
            pltpu.VMEM((period, 2 * TILE), jnp.float32),
            pltpu.VMEM((2 * wide, LAG // period * most * CC), jnp.float32),
            pltpu.SemaphoreType.DMA((4,)),
            pltpu.VMEM((period, period), jnp.bfloat16),
            pltpu.VMEM((period, period), jnp.bfloat16),
            pltpu.VMEM((2, period // 2, wide), jnp.float32),
            pltpu.VMEM((period, 2 * wide), jnp.bfloat16),
            pltpu.VMEM((period, 2 * wide), jnp.bfloat16),
            pltpu.VMEM((2, period, wide), jnp.float32),
            pltpu.VMEM((period, 2 * wide), jnp.bfloat16),
            pltpu.VMEM((period, 2 * wide), jnp.bfloat16),
            pltpu.VMEM((period, LAG // period * most * CC), jnp.float32),
            pltpu.VMEM((n_seg, half, TILE), jnp.float32),
        ],
        name="dft",
        compiler_params=pltpu.CompilerParams(vmem_limit_bytes=24 << 20),
        cost_estimate=SMALL,
    )(me, tables, *blocks)


def unpack_kernel(n_seg, chunks, most, me_ref, *refs):
    ins = refs[: n_seg * chunks]
    out_ref, buf = refs[n_seg * chunks :]
    half = buf.shape[1]
    for k in range(n_seg):
        z = jnp.bitwise_xor(me_ref[0], k)
        for ch in range(chunks):
            src = ins[ch * n_seg + k]
            top = src[half // 2 : half // 2 + 1, :].astype(jnp.float32)
            low, high = decode(src[: half // 2, :], top)
            buf[z * chunks + ch, : half // 2] = low
            buf[z * chunks + ch, half // 2 :] = high
    step_rows = 16

    def one(b, _):
        at = pl.multiple_of(b * step_rows, step_rows)
        v = transpose_groups([buf[i, pl.ds(at, step_rows), :] for i in range(GROUPS)])
        for h in range(2):
            for s in range(most):
                out_ref[pl.ds(h * half + at, step_rows), s, :] = v[h * most + s]
        return 0

    lax.fori_loop(0, half // step_rows, one, 0, unroll=4)


def unpack(me, parts, n_seg, chunks, most):
    half = 2 * (parts[0].shape[0] - 8)
    smem = pl.BlockSpec(memory_space=pltpu.SMEM)
    vmem = pl.BlockSpec(memory_space=pltpu.VMEM)
    return pl.pallas_call(
        functools.partial(unpack_kernel, n_seg, chunks, most),
        out_shape=jax.ShapeDtypeStruct((2 * half, most, TILE), jnp.float32),
        in_specs=[smem] + [vmem] * len(parts),
        out_specs=vmem,
        scratch_shapes=[pltpu.VMEM((GROUPS, half, TILE), jnp.float32)],
        name="unpack",
        compiler_params=pltpu.CompilerParams(vmem_limit_bytes=12 << 20),
        cost_estimate=SMALL,
    )(me, *parts)


def exchange(blocks, axis, size):
    return [blocks[0]] + [
        lax.ppermute(blocks[k], axis, [(i, i ^ k) for i in range(size)])
        for k in range(1, size)
    ]


def exchange_plane(blocks, n_pair):
    direct = [blocks[0]] + [
        lax.ppermute(blocks[k], "pair", [(i, i ^ (2 * k)) for i in range(n_pair)])
        for k in range(1, n_pair // 2)
    ]
    swap = [(i, i ^ 1) for i in range(n_pair)]
    return direct + [lax.ppermute(d, "pair", swap) for d in direct]


def body(spectra, pair_lists, pair_counts):
    n_pair = lax.axis_size("pair")
    n_seg = lax.axis_size("seg")
    freq = spectra.shape[2]
    most = pair_lists.shape[0]
    tiles = spectra.shape[3] // TILE
    chunks = GROUPS // n_seg
    rows = freq // n_pair // GROUPS
    me = jnp.stack([lax.axis_index("seg"), lax.axis_index("pair")]).astype(jnp.int32)
    x = spectra.reshape(2, freq, spectra.shape[3])
    lists = jnp.concatenate([pair_lists.reshape(-1), pair_counts])
    tables = make_tables(freq, most)
    packed = [pack(x, chunk, n_seg, n_pair) for chunk in range(chunks)]
    lists, packed[-1] = lax.optimization_barrier((lists, packed[-1]))
    table = lax.all_gather(lists, "pair", axis=0)
    if chunks > 1:
        table, packed[1], _ = lax.optimization_barrier((table, packed[1], tables))
    done = []
    lags = None
    for sent in packed:
        got = lax.all_to_all(
            sent.reshape(n_seg * n_pair, tiles, 2, rows, TILE),
            ("seg", "pair"),
            split_axis=0,
            concat_axis=0,
            tiled=True,
        )
        if lags is not None:
            got, _ = lax.optimization_barrier((got, lags))
        spec = got.reshape(n_seg, n_pair * tiles, 2, rows, TILE)
        blocks = stacks(me, table, spec, n_seg, n_pair, most)
        blocks = exchange_plane(blocks, n_pair)
        lags = dft(me, tables, blocks, freq, n_seg, n_pair, most)
        done += exchange(lags, "seg", n_seg)
    return unpack(me, done, n_seg, chunks, most)


def solution(mesh):
    return jax.shard_map(
        body,
        mesh=mesh,
        in_specs=(P("seg", None, None, "pair"), P("pair", None), P("pair")),
        out_specs=P("seg", "pair", None),
        check_vma=False,
    )
```

```python
import functools
import math

import jax
import jax.numpy as jnp
import numpy as np
from jax import lax
from jax.experimental import pallas as pl
from jax.experimental.pallas import tpu as pltpu
from jax.sharding import PartitionSpec as P

TILE = 128
LAG = 2048
GROUPS = 8
SMALL = pl.CostEstimate(flops=1, bytes_accessed=1, transcendentals=0)
CC = TILE // GROUPS


def lane_groups(shape):
    return lax.broadcasted_iota(jnp.int32, shape, len(shape) - 1) // CC


def shift_groups(x, by):
    return pltpu.roll(x, (by * CC) % TILE, x.ndim - 1)


def top_exponent(largest):
    return jnp.maximum(jnp.floor(jnp.log2(jnp.maximum(largest, 1e-36))), -90.0)


def encode(a, b, top):
    m = jnp.maximum(jnp.maximum(jnp.abs(a), jnp.abs(b)), 1e-36)
    e = jnp.minimum(jnp.maximum(jnp.floor(jnp.log2(m)), top - 15.0), top)
    s = jnp.exp2(12.0 - e)
    qa, qb = (
        jnp.clip(jnp.floor(x * s + 0.5), -8191.0, 8191.0).astype(jnp.int32) + 8192
        for x in (a, b)
    )
    return ((e - (top - 15.0)).astype(jnp.int32) << 28) | (qa << 14) | qb


ZERO = (8192 << 14) | 8192


def decode(code, top):
    s = jnp.exp2(((code >> 28) & 15).astype(jnp.float32) + (top - 27.0))
    a, b = (
        ((q & 16383) - 8192).astype(jnp.float32) * s for q in (code >> 14, code)
    )
    return a, b


def transpose_groups(vectors):
    v = list(vectors)
    grp = lane_groups(v[0].shape)
    for bit in (4, 2, 1):
        low = (grp & bit) == 0
        for i in range(GROUPS):
            if i & bit:
                continue
            a, b = v[i], v[i | bit]
            v[i] = jnp.where(low, a, shift_groups(b, bit))
            v[i | bit] = jnp.where(low, shift_groups(a, -bit), b)
    return v


def reduce_groups(vectors):
    v = list(vectors)
    grp = lane_groups(v[0].shape)
    low = (grp & 4) == 0
    v = [
        jnp.where(low, v[i], v[i + 4])
        + shift_groups(jnp.where(low, v[i + 4], v[i]), 4)
        for i in range(4)
    ]
    for bit in (2, 1):
        low = (grp & bit) == 0
        v = [
            jnp.where(low, v[i], v[i + bit])
            + jnp.where(low, shift_groups(v[i], -bit), shift_groups(v[i + bit], bit))
            for i in range(bit)
        ]
    return v[0]


def selection(n_seg, chunk, chans):
    wide = chans // TILE * n_seg * CC
    row = lax.broadcasted_iota(jnp.int32, (chans, wide), 0)
    col = lax.broadcasted_iota(jnp.int32, (chans, wide), 1)
    group = col // CC
    want = (
        group // n_seg * TILE
        + group % n_seg * (TILE // n_seg)
        + chunk * CC
        + col % CC
    )
    return (row == want).astype(jnp.bfloat16)


def pack_kernel(n_seg, n_pair, chunk, x_ref, out_ref, buf_ref):
    band = x_ref.shape[1] // n_pair
    sel = selection(n_seg, chunk, x_ref.shape[2])
    rows = band // GROUPS
    for p in range(n_pair):
        for ri in range(2):
            for part in range(sel.shape[1] // TILE):
                lanes = slice(part * TILE, (part + 1) * TILE)
                buf = buf_ref.at[p % 2, ri]
                buf[...] = jnp.dot(
                    x_ref[ri, p * band : (p + 1) * band, :],
                    sel[:, lanes],
                    preferred_element_type=jnp.float32,
                )
                v = [buf[pl.ds(fb, rows, stride=GROUPS), :] for fb in range(GROUPS)]
                v = transpose_groups(v)
                for g in range(GROUPS):
                    t, z = divmod(part * GROUPS + g, n_seg)
                    out_ref[z, p, t, ri] = v[g].astype(jnp.bfloat16)


def pack(x, chunk, n_seg, n_pair):
    _, freq, chans = x.shape
    band = freq // n_pair
    shape = (n_seg, n_pair, chans // TILE, 2, band // GROUPS, TILE)
    return pl.pallas_call(
        functools.partial(pack_kernel, n_seg, n_pair, chunk),
        out_shape=jax.ShapeDtypeStruct(shape, jnp.bfloat16),
        in_specs=[pl.BlockSpec(memory_space=pltpu.VMEM)],
        out_specs=pl.BlockSpec(memory_space=pltpu.VMEM),
        scratch_shapes=[pltpu.VMEM((2, 2, band, TILE), jnp.float32)],
        name="pack",
        cost_estimate=SMALL,
    )(x)


def stack_kernel(n_seg, n_pair, most, me_ref, table_ref, spec_ref, *refs):
    outs, (sum_ref, big_ref) = refs[:-2], refs[-2:]
    rows = spec_ref.shape[3]
    inv = 1.0 / float(n_seg * n_seg)
    big_ref[...] = jnp.zeros_like(big_ref)
    for k in range(n_pair):
        owner = jnp.bitwise_xor(me_ref[1], k)
        count = table_ref[owner, 2 * most]

        def one(s, _):
            src = table_ref[owner, 2 * s]
            rcv = table_ref[owner, 2 * s + 1]
            lr = li = pr = pi = None
            for g in range(n_seg):
                a0 = spec_ref[g, src, 0].astype(jnp.float32)
                a1 = spec_ref[g, src, 1].astype(jnp.float32)
                b0 = spec_ref[g, rcv, 0].astype(jnp.float32)
                b1 = spec_ref[g, rcv, 1].astype(jnp.float32)
                cr = a0 * b0 + a1 * b1
                ci = a1 * b0 - a0 * b1
                m = lax.rsqrt(cr * cr + ci * ci + 1.0)
                if g == 0:
                    lr, li, pr, pi = cr, ci, cr * m, ci * m
                else:
                    lr, li, pr, pi = lr + cr, li + ci, pr + cr * m, pi + ci * m
            w = (pr * pr + pi * pi) * inv
            re, im = lr * w, li * w
            sum_ref[k, s, 0] = re
            sum_ref[k, s, 1] = im
            big = jnp.maximum(jnp.abs(re), jnp.abs(im))
            big_ref[...] = jnp.maximum(big_ref[...], big)
            return 0

        lax.fori_loop(0, count, one, 0)
    top = top_exponent(jnp.max(big_ref[...], keepdims=True))
    for k in range(n_pair):
        owner = jnp.bitwise_xor(me_ref[1], k)
        count = table_ref[owner, 2 * most]
        out_ref = outs[k // 2].at[k % 2]

        def code(s, _):
            at = pl.ds(pl.multiple_of(s * rows, rows), rows)
            out_ref[at, :] = encode(sum_ref[k, s, 0], sum_ref[k, s, 1], top)
            return 0

        def dead(s, _):
            at = pl.ds(pl.multiple_of(s * rows, rows), rows)
            out_ref[at, :] = jnp.full((rows, TILE), ZERO, jnp.int32)
            return 0

        lax.fori_loop(0, count, code, 0)
        lax.fori_loop(count, most, dead, 0)
        out_ref[most * rows :, :] = jnp.broadcast_to(top, (8, TILE)).astype(jnp.int32)


def stacks(me, table, spec, n_seg, n_pair, most):
    rows = spec.shape[3]
    shape = (2, most * rows + 8, TILE)
    smem = pl.BlockSpec(memory_space=pltpu.SMEM)
    vmem = pl.BlockSpec(memory_space=pltpu.VMEM)
    return pl.pallas_call(
        functools.partial(stack_kernel, n_seg, n_pair, most),
        out_shape=[jax.ShapeDtypeStruct(shape, jnp.int32)] * (n_pair // 2),
        in_specs=[smem, smem, vmem],
        out_specs=[vmem] * (n_pair // 2),
        scratch_shapes=[
            pltpu.VMEM((n_pair, most, 2, rows, TILE), jnp.float32),
            pltpu.VMEM((rows, TILE), jnp.float32),
        ],
        name="stack",
        compiler_params=pltpu.CompilerParams(vmem_limit_bytes=12 << 20),
        cost_estimate=SMALL,
    )(me, table, spec)


def dft_kernel(
    n_seg, n_pair, most, me_ref, whi_ref, wlo_ref, phase_ref, tables_ref, *refs
):
    ins, outs = refs[:n_pair], refs[n_pair : n_pair + n_seg]
    t_ref, sem, s32, shi, slo, y, zhi, zlo, sums, parts = refs[n_pair + n_seg :]
    copy = pltpu.make_async_copy(
        tables_ref.at[pl.ds(0, t_ref.shape[0])], t_ref, sem.at[0]
    )
    copy.start()
    rows = (ins[0].shape[1] - 8) // most
    half_h = whi_ref.shape[1] // 2
    wide = most * TILE
    for k in range(n_pair):
        band = jnp.bitwise_xor(me_ref[1], k)
        src = ins[k % 2 * (n_pair // 2) + k // 2].at[k % 2]
        at = pl.ds(pl.multiple_of(band * rows, rows), rows)
        top = src[most * rows : most * rows + 1, :].astype(jnp.float32)
        for s in range(most):
            pair = decode(src[s * rows : (s + 1) * rows, :], top)
            for ri in range(2):
                s32[ri, at, s * TILE : (s + 1) * TILE] = pair[ri]
    for ri in range(2):
        full = s32[ri]
        hi = full.astype(jnp.bfloat16)
        lo = (full - hi.astype(jnp.float32)).astype(jnp.bfloat16)
        own = slice(ri * wide, (ri + 1) * wide)
        other = slice((1 - ri) * wide, (2 - ri) * wide)
        for to, part in ((shi, hi), (slo, lo)):
            to[:half_h, own] = part
            to[half_h:, other] = part if ri == 0 else -part
    for ri in range(2):
        n = slice(ri * wide, (ri + 1) * wide)
        y[ri] = (
            jnp.dot(wlo_ref[...], shi[:, n], preferred_element_type=jnp.float32)
            + jnp.dot(whi_ref[...], slo[:, n], preferred_element_type=jnp.float32)
        ) + jnp.dot(whi_ref[...], shi[:, n], preferred_element_type=jnp.float32)
    period = y.shape[1]
    step_rows = 64
    for b in range(period // step_rows):
        at = slice(b * step_rows, (b + 1) * step_rows)
        c = phase_ref[at, :TILE]
        d = phase_ref[at, TILE:]
        for s in range(most):
            lanes = slice(s * TILE, (s + 1) * TILE)
            yr = y[0, at, lanes]
            yi = y[1, at, lanes]
            for ri, z in enumerate((c * yr - d * yi, d * yr + c * yi)):
                to = slice((ri * most + s) * TILE, (ri * most + s + 1) * TILE)
                hi = z.astype(jnp.bfloat16)
                zhi[at, to] = hi
                zlo[at, to] = (z - hi.astype(jnp.float32)).astype(jnp.bfloat16)
    copy.wait()
    thi = t_ref[...].astype(jnp.bfloat16)
    tlo = (t_ref[...] - thi.astype(jnp.float32)).astype(jnp.bfloat16)
    sums[...] = (
        jnp.dot(zhi[...], tlo, preferred_element_type=jnp.float32)
        + jnp.dot(zlo[...], thi, preferred_element_type=jnp.float32)
    ) + jnp.dot(zhi[...], thi, preferred_element_type=jnp.float32)
    half = parts.shape[1]
    big = None
    first = lax.broadcasted_iota(jnp.int32, (half, TILE), 1) < TILE // 2
    for dest in range(n_seg):
        lag = dest * 2 * half
        r, l0 = lag // period, lag % period
        col = slice(r // 2 * TILE, (r // 2 + 1) * TILE)
        low = sums[l0 : l0 + half, col]
        high = sums[l0 + half : l0 + 2 * half, col]
        if r % 2 == 0:
            high = pltpu.roll(high, TILE // 2, 1)
        else:
            low = pltpu.roll(low, TILE // 2, 1)
        part = jnp.where(first, low, high)
        parts[dest] = part
        part = jnp.max(jnp.abs(part), axis=0, keepdims=True)
        big = part if big is None else jnp.maximum(big, part)
    top = top_exponent(jnp.max(big, keepdims=True))
    for k in range(n_seg):
        part = parts[jnp.bitwise_xor(me_ref[0], k)]
        outs[k][: half // 2, :] = encode(part[: half // 2], part[half // 2 :], top)
        outs[k][half // 2 :, :] = jnp.broadcast_to(top, (8, TILE)).astype(jnp.int32)


def sums_kernel(most, turns, shift, out_ref, t_ref, sem):
    shape = (most * TILE, turns * most * CC)
    row = lax.broadcasted_iota(jnp.int32, shape, 0)
    col = lax.broadcasted_iota(jnp.int32, shape, 1)
    same = (row // TILE == col // CC % most) & (row % CC == col % CC)
    eighths = (col // (most * CC) - shift) * (row // CC % GROUPS)
    diagonal = jnp.float32(math.sqrt(0.5))
    for ri in range(2):
        e = jnp.bitwise_and(eighths + 2 * ri, 7)
        size = jnp.where(e % 4 == 2, 0.0, jnp.where(e % 2 == 0, 1.0, diagonal))
        t = jnp.where(same, jnp.where((e > 2) & (e < 6), -size, size), 0.0)
        t_ref[ri * most * TILE : (ri + 1) * most * TILE, :] = t
    copy = pltpu.make_async_copy(
        t_ref, out_ref.at[pl.ds(0, t_ref.shape[0])], sem.at[0]
    )
    copy.start()
    copy.wait()


def make_sums(freq, most):
    period = 2 * (freq // GROUPS)
    turns = LAG // period
    width = turns * most * CC
    return pl.pallas_call(
        functools.partial(sums_kernel, most, turns, LAG // 2 // period),
        out_shape=jax.ShapeDtypeStruct((48 << 10, width), jnp.float32),
        out_specs=pl.BlockSpec(memory_space=pltpu.HBM),
        scratch_shapes=[
            pltpu.VMEM((2 * most * TILE, width), jnp.float32),
            pltpu.SemaphoreType.DMA((1,)),
        ],
        name="sums",
        cost_estimate=SMALL,
    )()


def make_tables(freq):
    h = freq // GROUPS
    period = 2 * h
    angle = np.arange(period)[:, None] * np.arange(h)[None, :] % period
    angle = angle * (2.0 * math.pi / period)
    w = np.concatenate([np.cos(angle), np.sin(angle)], 1).astype(np.float32)
    whi = w.astype(jnp.bfloat16)
    wlo = (w - whi.astype(np.float32)).astype(jnp.bfloat16)
    fb = np.arange(TILE) // CC
    phase = ((np.arange(period)[:, None] * fb[None, :]) % (2 * freq)) * (math.pi / freq)
    scale = 1.0 / math.sqrt(freq)
    phase = (np.concatenate([np.cos(phase), np.sin(phase)], 1) * scale).astype(np.float32)
    return [jnp.asarray(c) for c in (whi, wlo, phase)]


def dft(me, tables, blocks, freq, n_seg, n_pair, most):
    period = 2 * (freq // GROUPS)
    smem = pl.BlockSpec(memory_space=pltpu.SMEM)
    vmem = pl.BlockSpec(memory_space=pltpu.VMEM)
    half = LAG // n_seg // 2
    wide = most * TILE
    return pl.pallas_call(
        functools.partial(dft_kernel, n_seg, n_pair, most),
        out_shape=[jax.ShapeDtypeStruct((half // 2 + 8, TILE), jnp.int32)] * n_seg,
        in_specs=[smem, vmem, vmem, vmem, pl.BlockSpec(memory_space=pltpu.HBM)]
        + [vmem] * len(blocks),
        out_specs=[vmem] * n_seg,
        scratch_shapes=[
            pltpu.VMEM((2 * wide, LAG // period * most * CC), jnp.float32),
            pltpu.SemaphoreType.DMA((1,)),
            pltpu.VMEM((2, period // 2, wide), jnp.float32),
            pltpu.VMEM((period, 2 * wide), jnp.bfloat16),
            pltpu.VMEM((period, 2 * wide), jnp.bfloat16),
            pltpu.VMEM((2, period, wide), jnp.float32),
            pltpu.VMEM((period, 2 * wide), jnp.bfloat16),
            pltpu.VMEM((period, 2 * wide), jnp.bfloat16),
            pltpu.VMEM((period, LAG // period * most * CC), jnp.float32),
            pltpu.VMEM((n_seg, half, TILE), jnp.float32),
        ],
        name="dft",
        compiler_params=pltpu.CompilerParams(vmem_limit_bytes=24 << 20),
        cost_estimate=SMALL,
    )(me, *tables, *blocks)


def unpack_kernel(n_seg, chunks, most, me_ref, *refs):
    ins = refs[: n_seg * chunks]
    out_ref, buf = refs[n_seg * chunks :]
    half = buf.shape[1]

    @pl.when(pl.program_id(0) == 0)
    def _():
        for k in range(n_seg):
            z = jnp.bitwise_xor(me_ref[0], k)
            for ch in range(chunks):
                src = ins[ch * n_seg + k]
                top = src[half // 2 : half // 2 + 1, :].astype(jnp.float32)
                low, high = decode(src[: half // 2, :], top)
                buf[z * chunks + ch, : half // 2] = low
                buf[z * chunks + ch, half // 2 :] = high

    step_rows = 16
    block = out_ref.shape[1]
    for b in range(block // step_rows):
        at = pl.multiple_of(pl.program_id(0) * block + b * step_rows, step_rows)
        v = transpose_groups([buf[i, pl.ds(at, step_rows), :] for i in range(GROUPS)])
        for h in range(2):
            for s in range(most):
                out_ref[h, b * step_rows : (b + 1) * step_rows, s, :] = v[h * most + s]


def unpack(me, parts, n_seg, chunks, most):
    half = 2 * (parts[0].shape[0] - 8)
    steps = 4
    smem = pl.BlockSpec(memory_space=pltpu.SMEM)
    whole = pl.BlockSpec(parts[0].shape, lambda b: (0, 0))
    out = pl.pallas_call(
        functools.partial(unpack_kernel, n_seg, chunks, most),
        out_shape=jax.ShapeDtypeStruct((2, half, most, TILE), jnp.float32),
        grid=(steps,),
        in_specs=[smem] + [whole] * len(parts),
        out_specs=pl.BlockSpec((2, half // steps, most, TILE), lambda b: (0, b, 0, 0)),
        scratch_shapes=[pltpu.VMEM((GROUPS, half, TILE), jnp.float32)],
        name="unpack",
        compiler_params=pltpu.CompilerParams(vmem_limit_bytes=12 << 20),
        cost_estimate=SMALL,
    )(me, *parts)
    return out.reshape(2 * half, most, TILE)


def exchange(blocks, axis, size):
    return [blocks[0]] + [
        lax.ppermute(blocks[k], axis, [(i, i ^ k) for i in range(size)])
        for k in range(1, size)
    ]


def exchange_plane(blocks, n_pair):
    direct = [blocks[0]] + [
        lax.ppermute(blocks[k], "pair", [(i, i ^ (2 * k)) for i in range(n_pair)])
        for k in range(1, n_pair // 2)
    ]
    swap = [(i, i ^ 1) for i in range(n_pair)]
    return direct + [lax.ppermute(d, "pair", swap) for d in direct]


def body(spectra, pair_lists, pair_counts):
    n_pair = lax.axis_size("pair")
    n_seg = lax.axis_size("seg")
    freq = spectra.shape[2]
    most = pair_lists.shape[0]
    tiles = spectra.shape[3] // TILE
    chunks = GROUPS // n_seg
    rows = freq // n_pair // GROUPS
    me = jnp.stack([lax.axis_index("seg"), lax.axis_index("pair")]).astype(jnp.int32)
    x = spectra.reshape(2, freq, spectra.shape[3])
    lists = jnp.concatenate([pair_lists.reshape(-1), pair_counts])
    sums = make_sums(freq, most)
    tables = make_tables(freq) + [sums]
    packed = [pack(x, chunk, n_seg, n_pair) for chunk in range(chunks)]
    lists, packed[-1] = lax.optimization_barrier((lists, packed[-1]))
    table = lax.all_gather(lists, "pair", axis=0)
    if chunks > 1:
        table, packed[1], _ = lax.optimization_barrier((table, packed[1], sums))
    done = []
    lags = None
    for sent in packed:
        got = lax.all_to_all(
            sent.reshape(n_seg * n_pair, tiles, 2, rows, TILE),
            ("seg", "pair"),
            split_axis=0,
            concat_axis=0,
            tiled=True,
        )
        if lags is not None:
            got, _ = lax.optimization_barrier((got, lags))
        spec = got.reshape(n_seg, n_pair * tiles, 2, rows, TILE)
        blocks = stacks(me, table, spec, n_seg, n_pair, most)
        blocks = exchange_plane(blocks, n_pair)
        if done:
            blocks, _ = lax.optimization_barrier((blocks, done[2:]))
        lags = dft(me, tables, blocks, freq, n_seg, n_pair, most)
        done += exchange(lags, "seg", n_seg)
    return unpack(me, done, n_seg, chunks, most)


def solution(mesh):
    return jax.shard_map(
        body,
        mesh=mesh,
        in_specs=(P("seg", None, None, "pair"), P("pair", None), P("pair")),
        out_specs=P("seg", "pair", None),
        check_vma=False,
    )
```

```python
import functools
import math

import jax
import jax.numpy as jnp
import numpy as np
from jax import lax
from jax.experimental import pallas as pl
from jax.experimental.pallas import tpu as pltpu
from jax.sharding import PartitionSpec as P

TILE = 128
LAG = 2048
GROUPS = 8
SMALL = pl.CostEstimate(flops=1, bytes_accessed=1, transcendentals=0)
CC = TILE // GROUPS


def lane_groups(shape):
    return lax.broadcasted_iota(jnp.int32, shape, len(shape) - 1) // CC


def shift_groups(x, by):
    return pltpu.roll(x, (by * CC) % TILE, x.ndim - 1)


def top_exponent(largest):
    return jnp.maximum(jnp.floor(jnp.log2(jnp.maximum(largest, 1e-36))), -90.0)


def encode(a, b, top):
    m = jnp.maximum(jnp.maximum(jnp.abs(a), jnp.abs(b)), 1e-36)
    e = jnp.minimum(jnp.maximum(jnp.floor(jnp.log2(m)), top - 15.0), top)
    s = jnp.exp2(12.0 - e)
    qa, qb = (
        jnp.clip(jnp.floor(x * s + 0.5), -8191.0, 8191.0).astype(jnp.int32) + 8192
        for x in (a, b)
    )
    return ((e - (top - 15.0)).astype(jnp.int32) << 28) | (qa << 14) | qb


ZERO = (8192 << 14) | 8192


def decode(code, top):
    s = jnp.exp2(((code >> 28) & 15).astype(jnp.float32) + (top - 27.0))
    a, b = (
        ((q & 16383) - 8192).astype(jnp.float32) * s for q in (code >> 14, code)
    )
    return a, b


def transpose_groups(vectors):
    v = list(vectors)
    grp = lane_groups(v[0].shape)
    for bit in (4, 2, 1):
        low = (grp & bit) == 0
        for i in range(GROUPS):
            if i & bit:
                continue
            a, b = v[i], v[i | bit]
            v[i] = jnp.where(low, a, shift_groups(b, bit))
            v[i | bit] = jnp.where(low, shift_groups(a, -bit), b)
    return v


def reduce_groups(vectors):
    v = list(vectors)
    grp = lane_groups(v[0].shape)
    low = (grp & 4) == 0
    v = [
        jnp.where(low, v[i], v[i + 4])
        + shift_groups(jnp.where(low, v[i + 4], v[i]), 4)
        for i in range(4)
    ]
    for bit in (2, 1):
        low = (grp & bit) == 0
        v = [
            jnp.where(low, v[i], v[i + bit])
            + jnp.where(low, shift_groups(v[i], -bit), shift_groups(v[i + bit], bit))
            for i in range(bit)
        ]
    return v[0]


def selection(n_seg, chunk, chans):
    wide = chans // TILE * n_seg * CC
    row = lax.broadcasted_iota(jnp.int32, (chans, wide), 0)
    col = lax.broadcasted_iota(jnp.int32, (chans, wide), 1)
    group = col // CC
    want = (
        group // n_seg * TILE
        + group % n_seg * (TILE // n_seg)
        + chunk * CC
        + col % CC
    )
    return (row == want).astype(jnp.bfloat16)


def pack_kernel(n_seg, chunk, x_ref, out_ref, buf_ref):
    n_pair = out_ref.shape[1]
    band = x_ref.shape[1] // n_pair
    sel = selection(n_seg, chunk, x_ref.shape[2])
    rows = band // GROUPS
    for p in range(n_pair):
        for ri in range(2):
            for part in range(sel.shape[1] // TILE):
                lanes = slice(part * TILE, (part + 1) * TILE)
                buf = buf_ref.at[p % 2, ri]
                buf[...] = jnp.dot(
                    x_ref[ri, p * band : (p + 1) * band, :],
                    sel[:, lanes],
                    preferred_element_type=jnp.float32,
                )
                v = [buf[pl.ds(fb, rows, stride=GROUPS), :] for fb in range(GROUPS)]
                v = transpose_groups(v)
                for g in range(GROUPS):
                    t, z = divmod(part * GROUPS + g, n_seg)
                    out_ref[z, p, t, ri] = v[g].astype(jnp.bfloat16)


def pack(x, chunk, n_seg, n_pair):
    _, freq, chans = x.shape
    band = freq // n_pair
    shape = (n_seg, n_pair, chans // TILE, 2, band // GROUPS, TILE)
    return pl.pallas_call(
        functools.partial(pack_kernel, n_seg, chunk),
        out_shape=jax.ShapeDtypeStruct(shape, jnp.bfloat16),
        grid=(2,),
        in_specs=[pl.BlockSpec((2, freq // 2, chans), lambda i: (0, i, 0))],
        out_specs=pl.BlockSpec(
            (n_seg, n_pair // 2) + shape[2:], lambda i: (0, i, 0, 0, 0, 0)
        ),
        scratch_shapes=[pltpu.VMEM((2, 2, band, TILE), jnp.float32)],
        name="pack",
        cost_estimate=SMALL,
    )(x)


def stack_kernel(n_seg, n_pair, most, me_ref, table_ref, spec_ref, *refs):
    outs, (sum_ref, big_ref) = refs[:-2], refs[-2:]
    rows = spec_ref.shape[3]
    inv = 1.0 / float(n_seg * n_seg)
    big_ref[...] = jnp.zeros_like(big_ref)
    for k in range(n_pair):
        owner = jnp.bitwise_xor(me_ref[1], k)
        count = table_ref[owner, 2 * most]

        def one(s, _):
            src = table_ref[owner, 2 * s]
            rcv = table_ref[owner, 2 * s + 1]
            lr = li = pr = pi = None
            for g in range(n_seg):
                a0 = spec_ref[g, src, 0].astype(jnp.float32)
                a1 = spec_ref[g, src, 1].astype(jnp.float32)
                b0 = spec_ref[g, rcv, 0].astype(jnp.float32)
                b1 = spec_ref[g, rcv, 1].astype(jnp.float32)
                cr = a0 * b0 + a1 * b1
                ci = a1 * b0 - a0 * b1
                m = lax.rsqrt(cr * cr + ci * ci + 1.0)
                if g == 0:
                    lr, li, pr, pi = cr, ci, cr * m, ci * m
                else:
                    lr, li, pr, pi = lr + cr, li + ci, pr + cr * m, pi + ci * m
            w = (pr * pr + pi * pi) * inv
            re, im = lr * w, li * w
            sum_ref[k, s, 0] = re
            sum_ref[k, s, 1] = im
            big = jnp.maximum(jnp.abs(re), jnp.abs(im))
            big_ref[...] = jnp.maximum(big_ref[...], big)
            return 0

        lax.fori_loop(0, count, one, 0)
    top = top_exponent(jnp.max(big_ref[...], keepdims=True))
    for k in range(n_pair):
        owner = jnp.bitwise_xor(me_ref[1], k)
        count = table_ref[owner, 2 * most]
        out_ref = outs[k // 2].at[k % 2]

        def code(s, _):
            at = pl.ds(pl.multiple_of(s * rows, rows), rows)
            out_ref[at, :] = encode(sum_ref[k, s, 0], sum_ref[k, s, 1], top)
            return 0

        def dead(s, _):
            at = pl.ds(pl.multiple_of(s * rows, rows), rows)
            out_ref[at, :] = jnp.full((rows, TILE), ZERO, jnp.int32)
            return 0

        lax.fori_loop(0, count, code, 0)
        lax.fori_loop(count, most, dead, 0)
        out_ref[most * rows :, :] = jnp.broadcast_to(top, (8, TILE)).astype(jnp.int32)


def stacks(me, table, spec, n_seg, n_pair, most):
    rows = spec.shape[3]
    shape = (2, most * rows + 8, TILE)
    smem = pl.BlockSpec(memory_space=pltpu.SMEM)
    vmem = pl.BlockSpec(memory_space=pltpu.VMEM)
    return pl.pallas_call(
        functools.partial(stack_kernel, n_seg, n_pair, most),
        out_shape=[jax.ShapeDtypeStruct(shape, jnp.int32)] * (n_pair // 2),
        in_specs=[smem, smem, vmem],
        out_specs=[vmem] * (n_pair // 2),
        scratch_shapes=[
            pltpu.VMEM((n_pair, most, 2, rows, TILE), jnp.float32),
            pltpu.VMEM((rows, TILE), jnp.float32),
        ],
        name="stack",
        compiler_params=pltpu.CompilerParams(vmem_limit_bytes=12 << 20),
        cost_estimate=SMALL,
    )(me, table, spec)


def dft_kernel(
    n_seg, n_pair, most, me_ref, whi_ref, wlo_ref, phase_ref, tables_ref, *refs
):
    ins, outs = refs[:n_pair], refs[n_pair : n_pair + n_seg]
    t_ref, sem, s32, shi, slo, y, zhi, zlo, sums, parts = refs[n_pair + n_seg :]
    copy = pltpu.make_async_copy(
        tables_ref.at[pl.ds(0, t_ref.shape[0])], t_ref, sem.at[0]
    )
    copy.start()
    rows = (ins[0].shape[1] - 8) // most
    half_h = whi_ref.shape[1] // 2
    wide = most * TILE
    for k in range(n_pair):
        band = jnp.bitwise_xor(me_ref[1], k)
        src = ins[k % 2 * (n_pair // 2) + k // 2].at[k % 2]
        at = pl.ds(pl.multiple_of(band * rows, rows), rows)
        top = src[most * rows : most * rows + 1, :].astype(jnp.float32)
        for s in range(most):
            pair = decode(src[s * rows : (s + 1) * rows, :], top)
            for ri in range(2):
                s32[ri, at, s * TILE : (s + 1) * TILE] = pair[ri]
    for ri in range(2):
        full = s32[ri]
        hi = full.astype(jnp.bfloat16)
        lo = (full - hi.astype(jnp.float32)).astype(jnp.bfloat16)
        own = slice(ri * wide, (ri + 1) * wide)
        other = slice((1 - ri) * wide, (2 - ri) * wide)
        for to, part in ((shi, hi), (slo, lo)):
            to[:half_h, own] = part
            to[half_h:, other] = part if ri == 0 else -part
    for ri in range(2):
        n = slice(ri * wide, (ri + 1) * wide)
        y[ri] = (
            jnp.dot(wlo_ref[...], shi[:, n], preferred_element_type=jnp.float32)
            + jnp.dot(whi_ref[...], slo[:, n], preferred_element_type=jnp.float32)
        ) + jnp.dot(whi_ref[...], shi[:, n], preferred_element_type=jnp.float32)
    period = y.shape[1]
    step_rows = 64
    for b in range(period // step_rows):
        at = slice(b * step_rows, (b + 1) * step_rows)
        c = phase_ref[at, :TILE]
        d = phase_ref[at, TILE:]
        for s in range(most):
            lanes = slice(s * TILE, (s + 1) * TILE)
            yr = y[0, at, lanes]
            yi = y[1, at, lanes]
            for ri, z in enumerate((c * yr - d * yi, d * yr + c * yi)):
                to = slice((ri * most + s) * TILE, (ri * most + s + 1) * TILE)
                hi = z.astype(jnp.bfloat16)
                zhi[at, to] = hi
                zlo[at, to] = (z - hi.astype(jnp.float32)).astype(jnp.bfloat16)
    copy.wait()
    thi = t_ref[...].astype(jnp.bfloat16)
    tlo = (t_ref[...] - thi.astype(jnp.float32)).astype(jnp.bfloat16)
    sums[...] = (
        jnp.dot(zhi[...], tlo, preferred_element_type=jnp.float32)
        + jnp.dot(zlo[...], thi, preferred_element_type=jnp.float32)
    ) + jnp.dot(zhi[...], thi, preferred_element_type=jnp.float32)
    half = parts.shape[1]
    big = None
    first = lax.broadcasted_iota(jnp.int32, (half, TILE), 1) < TILE // 2
    for dest in range(n_seg):
        lag = dest * 2 * half
        r, l0 = lag // period, lag % period
        col = slice(r // 2 * TILE, (r // 2 + 1) * TILE)
        low = sums[l0 : l0 + half, col]
        high = sums[l0 + half : l0 + 2 * half, col]
        if r % 2 == 0:
            high = pltpu.roll(high, TILE // 2, 1)
        else:
            low = pltpu.roll(low, TILE // 2, 1)
        part = jnp.where(first, low, high)
        parts[dest] = part
        part = jnp.max(jnp.abs(part), axis=0, keepdims=True)
        big = part if big is None else jnp.maximum(big, part)
    top = top_exponent(jnp.max(big, keepdims=True))
    for k in range(n_seg):
        part = parts[jnp.bitwise_xor(me_ref[0], k)]
        outs[k][: half // 2, :] = encode(part[: half // 2], part[half // 2 :], top)
        outs[k][half // 2 :, :] = jnp.broadcast_to(top, (8, TILE)).astype(jnp.int32)


def sums_kernel(most, turns, shift, out_ref, t_ref, sem):
    shape = (most * TILE, turns * most * CC)
    row = lax.broadcasted_iota(jnp.int32, shape, 0)
    col = lax.broadcasted_iota(jnp.int32, shape, 1)
    same = (row // TILE == col // CC % most) & (row % CC == col % CC)
    eighths = (col // (most * CC) - shift) * (row // CC % GROUPS)
    diagonal = jnp.float32(math.sqrt(0.5))
    for ri in range(2):
        e = jnp.bitwise_and(eighths + 2 * ri, 7)
        size = jnp.where(e % 4 == 2, 0.0, jnp.where(e % 2 == 0, 1.0, diagonal))
        t = jnp.where(same, jnp.where((e > 2) & (e < 6), -size, size), 0.0)
        t_ref[ri * most * TILE : (ri + 1) * most * TILE, :] = t
    copy = pltpu.make_async_copy(
        t_ref, out_ref.at[pl.ds(0, t_ref.shape[0])], sem.at[0]
    )
    copy.start()
    copy.wait()


def make_sums(freq, most):
    period = 2 * (freq // GROUPS)
    turns = LAG // period
    width = turns * most * CC
    return pl.pallas_call(
        functools.partial(sums_kernel, most, turns, LAG // 2 // period),
        out_shape=jax.ShapeDtypeStruct((48 << 10, width), jnp.float32),
        out_specs=pl.BlockSpec(memory_space=pltpu.HBM),
        scratch_shapes=[
            pltpu.VMEM((2 * most * TILE, width), jnp.float32),
            pltpu.SemaphoreType.DMA((1,)),
        ],
        name="sums",
        cost_estimate=SMALL,
    )()


def make_tables(freq):
    h = freq // GROUPS
    period = 2 * h
    angle = np.arange(period)[:, None] * np.arange(h)[None, :] % period
    angle = angle * (2.0 * math.pi / period)
    w = np.concatenate([np.cos(angle), np.sin(angle)], 1).astype(np.float32)
    whi = w.astype(jnp.bfloat16)
    wlo = (w - whi.astype(np.float32)).astype(jnp.bfloat16)
    fb = np.arange(TILE) // CC
    phase = ((np.arange(period)[:, None] * fb[None, :]) % (2 * freq)) * (math.pi / freq)
    scale = 1.0 / math.sqrt(freq)
    phase = (np.concatenate([np.cos(phase), np.sin(phase)], 1) * scale).astype(np.float32)
    return [jnp.asarray(c) for c in (whi, wlo, phase)]


def dft(me, tables, blocks, freq, n_seg, n_pair, most):
    period = 2 * (freq // GROUPS)
    smem = pl.BlockSpec(memory_space=pltpu.SMEM)
    vmem = pl.BlockSpec(memory_space=pltpu.VMEM)
    half = LAG // n_seg // 2
    wide = most * TILE
    return pl.pallas_call(
        functools.partial(dft_kernel, n_seg, n_pair, most),
        out_shape=[jax.ShapeDtypeStruct((half // 2 + 8, TILE), jnp.int32)] * n_seg,
        in_specs=[smem, vmem, vmem, vmem, pl.BlockSpec(memory_space=pltpu.HBM)]
        + [vmem] * len(blocks),
        out_specs=[vmem] * n_seg,
        scratch_shapes=[
            pltpu.VMEM((2 * wide, LAG // period * most * CC), jnp.float32),
            pltpu.SemaphoreType.DMA((1,)),
            pltpu.VMEM((2, period // 2, wide), jnp.float32),
            pltpu.VMEM((period, 2 * wide), jnp.bfloat16),
            pltpu.VMEM((period, 2 * wide), jnp.bfloat16),
            pltpu.VMEM((2, period, wide), jnp.float32),
            pltpu.VMEM((period, 2 * wide), jnp.bfloat16),
            pltpu.VMEM((period, 2 * wide), jnp.bfloat16),
            pltpu.VMEM((period, LAG // period * most * CC), jnp.float32),
            pltpu.VMEM((n_seg, half, TILE), jnp.float32),
        ],
        name="dft",
        compiler_params=pltpu.CompilerParams(vmem_limit_bytes=24 << 20),
        cost_estimate=SMALL,
    )(me, *tables, *blocks)


def unpack_kernel(n_seg, chunks, most, me_ref, *refs):
    ins = refs[: n_seg * chunks]
    out_ref, buf = refs[n_seg * chunks :]
    half = buf.shape[1]

    @pl.when(pl.program_id(0) == 0)
    def _():
        for k in range(n_seg):
            z = jnp.bitwise_xor(me_ref[0], k)
            for ch in range(chunks):
                src = ins[ch * n_seg + k]
                top = src[half // 2 : half // 2 + 1, :].astype(jnp.float32)
                low, high = decode(src[: half // 2, :], top)
                buf[z * chunks + ch, : half // 2] = low
                buf[z * chunks + ch, half // 2 :] = high

    step_rows = 16
    block = out_ref.shape[1]
    for b in range(block // step_rows):
        at = pl.multiple_of(pl.program_id(0) * block + b * step_rows, step_rows)
        v = transpose_groups([buf[i, pl.ds(at, step_rows), :] for i in range(GROUPS)])
        for h in range(2):
            for s in range(most):
                out_ref[h, b * step_rows : (b + 1) * step_rows, s, :] = v[h * most + s]


def unpack(me, parts, n_seg, chunks, most):
    half = 2 * (parts[0].shape[0] - 8)
    steps = 4
    smem = pl.BlockSpec(memory_space=pltpu.SMEM)
    whole = pl.BlockSpec(parts[0].shape, lambda b: (0, 0))
    out = pl.pallas_call(
        functools.partial(unpack_kernel, n_seg, chunks, most),
        out_shape=jax.ShapeDtypeStruct((2, half, most, TILE), jnp.float32),
        grid=(steps,),
        in_specs=[smem] + [whole] * len(parts),
        out_specs=pl.BlockSpec((2, half // steps, most, TILE), lambda b: (0, b, 0, 0)),
        scratch_shapes=[pltpu.VMEM((GROUPS, half, TILE), jnp.float32)],
        name="unpack",
        compiler_params=pltpu.CompilerParams(vmem_limit_bytes=12 << 20),
        cost_estimate=SMALL,
    )(me, *parts)
    return out.reshape(2 * half, most, TILE)


def exchange(blocks, axis, size):
    return [blocks[0]] + [
        lax.ppermute(blocks[k], axis, [(i, i ^ k) for i in range(size)])
        for k in range(1, size)
    ]


def exchange_plane(blocks, n_pair, between=None):
    direct = [blocks[0]] + [
        lax.ppermute(blocks[k], "pair", [(i, i ^ (2 * k)) for i in range(n_pair)])
        for k in range(1, n_pair // 2)
    ]
    if between is not None:
        direct, _ = lax.optimization_barrier((direct, between))
    swap = [(i, i ^ 1) for i in range(n_pair)]
    return direct + [lax.ppermute(d, "pair", swap) for d in direct]


def body(spectra, pair_lists, pair_counts):
    n_pair = lax.axis_size("pair")
    n_seg = lax.axis_size("seg")
    freq = spectra.shape[2]
    most = pair_lists.shape[0]
    tiles = spectra.shape[3] // TILE
    chunks = GROUPS // n_seg
    rows = freq // n_pair // GROUPS
    me = jnp.stack([lax.axis_index("seg"), lax.axis_index("pair")]).astype(jnp.int32)
    x = spectra.reshape(2, freq, spectra.shape[3])
    lists = jnp.concatenate([pair_lists.reshape(-1), pair_counts])
    sums = make_sums(freq, most)
    tables = make_tables(freq) + [sums]
    packed = [pack(x, chunk, n_seg, n_pair) for chunk in range(chunks)]
    lists, packed[-1] = lax.optimization_barrier((lists, packed[-1]))
    table = lax.all_gather(lists, "pair", axis=0)
    if chunks > 1:
        table, packed[1], _ = lax.optimization_barrier((table, packed[1], sums))
    done = []
    blocks = lags = None
    for sent in packed:
        got = lax.all_to_all(
            sent.reshape(n_seg * n_pair, tiles, 2, rows, TILE),
            ("seg", "pair"),
            split_axis=0,
            concat_axis=0,
            tiled=True,
        )
        if blocks is not None:
            got, _ = lax.optimization_barrier((got, blocks))
        spec = got.reshape(n_seg, n_pair * tiles, 2, rows, TILE)
        stack = stacks(me, table, spec, n_seg, n_pair, most)
        if blocks is not None:
            blocks, _ = lax.optimization_barrier((blocks, stack))
            lags = dft(me, tables, blocks, freq, n_seg, n_pair, most)
            done += exchange(lags, "seg", n_seg)
        blocks = exchange_plane(stack, n_pair, lags)
    lags = dft(me, tables, blocks, freq, n_seg, n_pair, most)
    done += exchange(lags, "seg", n_seg)
    return unpack(me, done, n_seg, chunks, most)


def solution(mesh):
    return jax.shard_map(
        body,
        mesh=mesh,
        in_specs=(P("seg", None, None, "pair"), P("pair", None), P("pair")),
        out_specs=P("seg", "pair", None),
        check_vma=False,
    )
```

```python
import functools
import math

import jax
import jax.numpy as jnp
import numpy as np
from jax import lax
from jax.experimental import pallas as pl
from jax.experimental.pallas import tpu as pltpu
from jax.sharding import PartitionSpec as P

TILE = 128
LAG = 2048
GROUPS = 8
SMALL = pl.CostEstimate(flops=1, bytes_accessed=1, transcendentals=0)
CC = TILE // GROUPS


def lane_groups(shape):
    return lax.broadcasted_iota(jnp.int32, shape, len(shape) - 1) // CC


def shift_groups(x, by):
    return pltpu.roll(x, (by * CC) % TILE, x.ndim - 1)


def top_exponent(largest):
    return jnp.maximum(jnp.floor(jnp.log2(jnp.maximum(largest, 1e-36))), -90.0)


def encode(a, b, top):
    m = jnp.maximum(jnp.maximum(jnp.abs(a), jnp.abs(b)), 1e-36)
    e = jnp.minimum(jnp.maximum(jnp.floor(jnp.log2(m)), top - 15.0), top)
    s = jnp.exp2(12.0 - e)
    qa, qb = (
        jnp.clip(jnp.floor(x * s + 0.5), -8191.0, 8191.0).astype(jnp.int32) + 8192
        for x in (a, b)
    )
    return ((e - (top - 15.0)).astype(jnp.int32) << 28) | (qa << 14) | qb


ZERO = (8192 << 14) | 8192


def decode(code, top):
    s = jnp.exp2(((code >> 28) & 15).astype(jnp.float32) + (top - 27.0))
    a, b = (
        ((q & 16383) - 8192).astype(jnp.float32) * s for q in (code >> 14, code)
    )
    return a, b


def transpose_groups(vectors):
    v = list(vectors)
    grp = lane_groups(v[0].shape)
    for bit in (4, 2, 1):
        low = (grp & bit) == 0
        for i in range(GROUPS):
            if i & bit:
                continue
            a, b = v[i], v[i | bit]
            v[i] = jnp.where(low, a, shift_groups(b, bit))
            v[i | bit] = jnp.where(low, shift_groups(a, -bit), b)
    return v


def reduce_groups(vectors):
    v = list(vectors)
    grp = lane_groups(v[0].shape)
    low = (grp & 4) == 0
    v = [
        jnp.where(low, v[i], v[i + 4])
        + shift_groups(jnp.where(low, v[i + 4], v[i]), 4)
        for i in range(4)
    ]
    for bit in (2, 1):
        low = (grp & bit) == 0
        v = [
            jnp.where(low, v[i], v[i + bit])
            + jnp.where(low, shift_groups(v[i], -bit), shift_groups(v[i + bit], bit))
            for i in range(bit)
        ]
    return v[0]


def selection(n_seg, chunk, chans):
    wide = chans // TILE * n_seg * CC
    row = lax.broadcasted_iota(jnp.int32, (chans, wide), 0)
    col = lax.broadcasted_iota(jnp.int32, (chans, wide), 1)
    group = col // CC
    want = (
        group // n_seg * TILE
        + group % n_seg * (TILE // n_seg)
        + chunk * CC
        + col % CC
    )
    return (row == want).astype(jnp.bfloat16)


def pack_kernel(n_seg, chunk, x_ref, out_ref, buf_ref):
    n_pair = out_ref.shape[1]
    band = x_ref.shape[1] // n_pair
    sel = selection(n_seg, chunk, x_ref.shape[2])
    rows = band // GROUPS
    for p in range(n_pair):
        for ri in range(2):
            for part in range(sel.shape[1] // TILE):
                lanes = slice(part * TILE, (part + 1) * TILE)
                buf = buf_ref.at[p % 2, ri]
                buf[...] = jnp.dot(
                    x_ref[ri, p * band : (p + 1) * band, :],
                    sel[:, lanes],
                    preferred_element_type=jnp.float32,
                )
                v = [buf[pl.ds(fb, rows, stride=GROUPS), :] for fb in range(GROUPS)]
                v = transpose_groups(v)
                for g in range(GROUPS):
                    t, z = divmod(part * GROUPS + g, n_seg)
                    out_ref[z, p, t, ri] = v[g].astype(jnp.bfloat16)


def pack(x, chunk, n_seg, n_pair):
    _, freq, chans = x.shape
    band = freq // n_pair
    shape = (n_seg, n_pair, chans // TILE, 2, band // GROUPS, TILE)
    return pl.pallas_call(
        functools.partial(pack_kernel, n_seg, chunk),
        out_shape=jax.ShapeDtypeStruct(shape, jnp.bfloat16),
        grid=(2,),
        in_specs=[pl.BlockSpec((2, freq // 2, chans), lambda i: (0, i, 0))],
        out_specs=pl.BlockSpec(
            (n_seg, n_pair // 2) + shape[2:], lambda i: (0, i, 0, 0, 0, 0)
        ),
        scratch_shapes=[pltpu.VMEM((2, 2, band, TILE), jnp.float32)],
        name="pack",
        cost_estimate=SMALL,
    )(x)


def stack_kernel(n_seg, n_pair, most, me_ref, table_ref, spec_ref, *refs):
    outs, (sum_ref, big_ref) = refs[:-2], refs[-2:]
    rows = spec_ref.shape[3]
    inv = 1.0 / float(n_seg * n_seg)
    big_ref[...] = jnp.zeros_like(big_ref)
    for k in range(n_pair):
        owner = jnp.bitwise_xor(me_ref[1], k)
        count = table_ref[owner, 2 * most]

        def one(s, _):
            src = table_ref[owner, 2 * s]
            rcv = table_ref[owner, 2 * s + 1]
            lr = li = pr = pi = None
            for g in range(n_seg):
                a0 = spec_ref[g, src, 0].astype(jnp.float32)
                a1 = spec_ref[g, src, 1].astype(jnp.float32)
                b0 = spec_ref[g, rcv, 0].astype(jnp.float32)
                b1 = spec_ref[g, rcv, 1].astype(jnp.float32)
                cr = a0 * b0 + a1 * b1
                ci = a1 * b0 - a0 * b1
                m = lax.rsqrt(cr * cr + ci * ci + 1.0)
                if g == 0:
                    lr, li, pr, pi = cr, ci, cr * m, ci * m
                else:
                    lr, li, pr, pi = lr + cr, li + ci, pr + cr * m, pi + ci * m
            w = (pr * pr + pi * pi) * inv
            re, im = lr * w, li * w
            sum_ref[k, s, 0] = re
            sum_ref[k, s, 1] = im
            big = jnp.maximum(jnp.abs(re), jnp.abs(im))
            big_ref[...] = jnp.maximum(big_ref[...], big)
            return 0

        lax.fori_loop(0, count, one, 0)
    top = top_exponent(jnp.max(big_ref[...], keepdims=True))
    for k in range(n_pair):
        owner = jnp.bitwise_xor(me_ref[1], k)
        count = table_ref[owner, 2 * most]
        out_ref = outs[k // 2].at[k % 2]

        def code(s, _):
            at = pl.ds(pl.multiple_of(s * rows, rows), rows)
            out_ref[at, :] = encode(sum_ref[k, s, 0], sum_ref[k, s, 1], top)
            return 0

        def dead(s, _):
            at = pl.ds(pl.multiple_of(s * rows, rows), rows)
            out_ref[at, :] = jnp.full((rows, TILE), ZERO, jnp.int32)
            return 0

        lax.fori_loop(0, count, code, 0)
        lax.fori_loop(count, most, dead, 0)
        out_ref[most * rows :, :] = jnp.broadcast_to(top, (8, TILE)).astype(jnp.int32)


def stacks(me, table, spec, n_seg, n_pair, most):
    rows = spec.shape[3]
    shape = (2, most * rows + 8, TILE)
    smem = pl.BlockSpec(memory_space=pltpu.SMEM)
    vmem = pl.BlockSpec(memory_space=pltpu.VMEM)
    return pl.pallas_call(
        functools.partial(stack_kernel, n_seg, n_pair, most),
        out_shape=[jax.ShapeDtypeStruct(shape, jnp.int32)] * (n_pair // 2),
        in_specs=[smem, smem, vmem],
        out_specs=[vmem] * (n_pair // 2),
        scratch_shapes=[
            pltpu.VMEM((n_pair, most, 2, rows, TILE), jnp.float32),
            pltpu.VMEM((rows, TILE), jnp.float32),
        ],
        name="stack",
        compiler_params=pltpu.CompilerParams(vmem_limit_bytes=12 << 20),
        cost_estimate=SMALL,
    )(me, table, spec)


def dft_kernel(
    n_seg, n_pair, most, me_ref, w_ref, tables_ref, *refs
):
    ins, outs = refs[:n_pair], refs[n_pair : n_pair + n_seg]
    t_ref, phase_ref, sem, s32, shi, slo, y, zhi, zlo, sums, parts = refs[n_pair + n_seg :]
    copies = [
        pltpu.make_async_copy(
            tables_ref.at[pl.ds(t_ref.shape[0], phase_ref.shape[0])],
            phase_ref,
            sem.at[0],
        ),
        pltpu.make_async_copy(
            tables_ref.at[pl.ds(0, t_ref.shape[0])], t_ref, sem.at[1]
        ),
    ]
    for copy in copies:
        copy.start()
    rows = (ins[0].shape[1] - 8) // most
    half_h = w_ref.shape[1] // 2
    whi_ref, wlo_ref = w_ref.at[: 2 * half_h], w_ref.at[2 * half_h :]
    wide = most * TILE
    for k in range(n_pair):
        band = jnp.bitwise_xor(me_ref[1], k)
        src = ins[k % 2 * (n_pair // 2) + k // 2].at[k % 2]
        at = pl.ds(pl.multiple_of(band * rows, rows), rows)
        top = src[most * rows : most * rows + 1, :].astype(jnp.float32)
        for s in range(most):
            pair = decode(src[s * rows : (s + 1) * rows, :], top)
            for ri in range(2):
                s32[ri, at, s * TILE : (s + 1) * TILE] = pair[ri]
    for ri in range(2):
        full = s32[ri]
        hi = full.astype(jnp.bfloat16)
        lo = (full - hi.astype(jnp.float32)).astype(jnp.bfloat16)
        own = slice(ri * wide, (ri + 1) * wide)
        other = slice((1 - ri) * wide, (2 - ri) * wide)
        for to, part in ((shi, hi), (slo, lo)):
            to[:half_h, own] = part
            to[half_h:, other] = part if ri == 0 else -part
    for ri in range(2):
        n = slice(ri * wide, (ri + 1) * wide)
        y[ri] = (
            jnp.dot(wlo_ref[...], shi[:, n], preferred_element_type=jnp.float32)
            + jnp.dot(whi_ref[...], slo[:, n], preferred_element_type=jnp.float32)
        ) + jnp.dot(whi_ref[...], shi[:, n], preferred_element_type=jnp.float32)
    copies[0].wait()
    period = y.shape[1]
    step_rows = 64
    for b in range(period // step_rows):
        at = slice(b * step_rows, (b + 1) * step_rows)
        c = phase_ref[at, :TILE]
        d = phase_ref[at, TILE:]
        for s in range(most):
            lanes = slice(s * TILE, (s + 1) * TILE)
            yr = y[0, at, lanes]
            yi = y[1, at, lanes]
            for ri, z in enumerate((c * yr - d * yi, d * yr + c * yi)):
                to = slice((ri * most + s) * TILE, (ri * most + s + 1) * TILE)
                hi = z.astype(jnp.bfloat16)
                zhi[at, to] = hi
                zlo[at, to] = (z - hi.astype(jnp.float32)).astype(jnp.bfloat16)
    copies[1].wait()
    thi = t_ref[...].astype(jnp.bfloat16)
    tlo = (t_ref[...] - thi.astype(jnp.float32)).astype(jnp.bfloat16)
    sums[...] = (
        jnp.dot(zhi[...], tlo, preferred_element_type=jnp.float32)
        + jnp.dot(zlo[...], thi, preferred_element_type=jnp.float32)
    ) + jnp.dot(zhi[...], thi, preferred_element_type=jnp.float32)
    half = parts.shape[1]
    big = None
    first = lax.broadcasted_iota(jnp.int32, (half, TILE), 1) < TILE // 2
    for dest in range(n_seg):
        lag = dest * 2 * half
        r, l0 = lag // period, lag % period
        col = slice(r // 2 * TILE, (r // 2 + 1) * TILE)
        low = sums[l0 : l0 + half, col]
        high = sums[l0 + half : l0 + 2 * half, col]
        if r % 2 == 0:
            high = pltpu.roll(high, TILE // 2, 1)
        else:
            low = pltpu.roll(low, TILE // 2, 1)
        part = jnp.where(first, low, high)
        parts[dest] = part
        part = jnp.max(jnp.abs(part), axis=0, keepdims=True)
        big = part if big is None else jnp.maximum(big, part)
    top = top_exponent(jnp.max(big, keepdims=True))
    for k in range(n_seg):
        part = parts[jnp.bitwise_xor(me_ref[0], k)]
        outs[k][: half // 2, :] = encode(part[: half // 2], part[half // 2 :], top)
        outs[k][half // 2 :, :] = jnp.broadcast_to(top, (8, TILE)).astype(jnp.int32)


def sums_kernel(most, turns, shift, phase_ref, out_ref, t_ref, sem):
    shape = (most * TILE, turns * most * CC)
    row = lax.broadcasted_iota(jnp.int32, shape, 0)
    col = lax.broadcasted_iota(jnp.int32, shape, 1)
    same = (row // TILE == col // CC % most) & (row % CC == col % CC)
    eighths = (col // (most * CC) - shift) * (row // CC % GROUPS)
    diagonal = jnp.float32(math.sqrt(0.5))
    for ri in range(2):
        e = jnp.bitwise_and(eighths + 2 * ri, 7)
        size = jnp.where(e % 4 == 2, 0.0, jnp.where(e % 2 == 0, 1.0, diagonal))
        t = jnp.where(same, jnp.where((e > 2) & (e < 6), -size, size), 0.0)
        t_ref[ri * most * TILE : (ri + 1) * most * TILE, :] = t
    copies = [
        pltpu.make_async_copy(
            t_ref, out_ref.at[pl.ds(0, t_ref.shape[0])], sem.at[0]
        ),
        pltpu.make_async_copy(
            phase_ref,
            out_ref.at[pl.ds(t_ref.shape[0], phase_ref.shape[0])],
            sem.at[1],
        ),
    ]
    for copy in copies:
        copy.start()
    for copy in copies:
        copy.wait()


def make_sums(phase, freq, most):
    period = 2 * (freq // GROUPS)
    turns = LAG // period
    width = turns * most * CC
    return pl.pallas_call(
        functools.partial(sums_kernel, most, turns, LAG // 2 // period),
        out_shape=jax.ShapeDtypeStruct((48 << 10, width), jnp.float32),
        in_specs=[pl.BlockSpec(memory_space=pltpu.VMEM)],
        out_specs=pl.BlockSpec(memory_space=pltpu.HBM),
        scratch_shapes=[
            pltpu.VMEM((2 * most * TILE, width), jnp.float32),
            pltpu.SemaphoreType.DMA((2,)),
        ],
        name="sums",
        cost_estimate=SMALL,
    )(phase)


def make_tables(freq):
    h = freq // GROUPS
    period = 2 * h
    angle = np.arange(period)[:, None] * np.arange(h)[None, :] % period
    angle = angle * (2.0 * math.pi / period)
    w = np.concatenate([np.cos(angle), np.sin(angle)], 1).astype(np.float32)
    whi = w.astype(jnp.bfloat16)
    wlo = (w - whi.astype(np.float32)).astype(jnp.bfloat16)
    fb = np.arange(TILE) // CC
    phase = ((np.arange(period)[:, None] * fb[None, :]) % (2 * freq)) * (math.pi / freq)
    scale = 1.0 / math.sqrt(freq)
    phase = (np.concatenate([np.cos(phase), np.sin(phase)], 1) * scale).astype(np.float32)
    return [jnp.asarray(c) for c in (np.concatenate([whi, wlo]), phase)]


def dft(me, tables, blocks, freq, n_seg, n_pair, most):
    period = 2 * (freq // GROUPS)
    smem = pl.BlockSpec(memory_space=pltpu.SMEM)
    vmem = pl.BlockSpec(memory_space=pltpu.VMEM)
    half = LAG // n_seg // 2
    wide = most * TILE
    return pl.pallas_call(
        functools.partial(dft_kernel, n_seg, n_pair, most),
        out_shape=[jax.ShapeDtypeStruct((half // 2 + 8, TILE), jnp.int32)] * n_seg,
        in_specs=[smem, vmem, pl.BlockSpec(memory_space=pltpu.HBM)]
        + [vmem] * len(blocks),
        out_specs=[vmem] * n_seg,
        scratch_shapes=[
            pltpu.VMEM((2 * wide, LAG // period * most * CC), jnp.float32),
            pltpu.VMEM((period, 2 * TILE), jnp.float32),
            pltpu.SemaphoreType.DMA((2,)),
            pltpu.VMEM((2, period // 2, wide), jnp.float32),
            pltpu.VMEM((period, 2 * wide), jnp.bfloat16),
            pltpu.VMEM((period, 2 * wide), jnp.bfloat16),
            pltpu.VMEM((2, period, wide), jnp.float32),
            pltpu.VMEM((period, 2 * wide), jnp.bfloat16),
            pltpu.VMEM((period, 2 * wide), jnp.bfloat16),
            pltpu.VMEM((period, LAG // period * most * CC), jnp.float32),
            pltpu.VMEM((n_seg, half, TILE), jnp.float32),
        ],
        name="dft",
        compiler_params=pltpu.CompilerParams(vmem_limit_bytes=24 << 20),
        cost_estimate=SMALL,
    )(me, *tables, *blocks)


def unpack_kernel(n_seg, chunks, most, me_ref, *refs):
    ins = refs[: n_seg * chunks]
    out_ref, buf = refs[n_seg * chunks :]
    half = buf.shape[1]

    @pl.when(pl.program_id(0) == 0)
    def _():
        for k in range(n_seg):
            z = jnp.bitwise_xor(me_ref[0], k)
            for ch in range(chunks):
                src = ins[ch * n_seg + k]
                top = src[half // 2 : half // 2 + 1, :].astype(jnp.float32)
                low, high = decode(src[: half // 2, :], top)
                buf[z * chunks + ch, : half // 2] = low
                buf[z * chunks + ch, half // 2 :] = high

    step_rows = 16
    block = out_ref.shape[1]
    for b in range(block // step_rows):
        at = pl.multiple_of(pl.program_id(0) * block + b * step_rows, step_rows)
        v = transpose_groups([buf[i, pl.ds(at, step_rows), :] for i in range(GROUPS)])
        for h in range(2):
            for s in range(most):
                out_ref[h, b * step_rows : (b + 1) * step_rows, s, :] = v[h * most + s]


def unpack(me, parts, n_seg, chunks, most):
    half = 2 * (parts[0].shape[0] - 8)
    steps = 4
    smem = pl.BlockSpec(memory_space=pltpu.SMEM)
    whole = pl.BlockSpec(parts[0].shape, lambda b: (0, 0))
    out = pl.pallas_call(
        functools.partial(unpack_kernel, n_seg, chunks, most),
        out_shape=jax.ShapeDtypeStruct((2, half, most, TILE), jnp.float32),
        grid=(steps,),
        in_specs=[smem] + [whole] * len(parts),
        out_specs=pl.BlockSpec((2, half // steps, most, TILE), lambda b: (0, b, 0, 0)),
        scratch_shapes=[pltpu.VMEM((GROUPS, half, TILE), jnp.float32)],
        name="unpack",
        compiler_params=pltpu.CompilerParams(vmem_limit_bytes=12 << 20),
        cost_estimate=SMALL,
    )(me, *parts)
    return out.reshape(2 * half, most, TILE)


def exchange(blocks, axis, size):
    return [blocks[0]] + [
        lax.ppermute(blocks[k], axis, [(i, i ^ k) for i in range(size)])
        for k in range(1, size)
    ]


def exchange_plane(blocks, n_pair, between=None):
    direct = [blocks[0]] + [
        lax.ppermute(blocks[k], "pair", [(i, i ^ (2 * k)) for i in range(n_pair)])
        for k in range(1, n_pair // 2)
    ]
    if between is not None:
        direct, _ = lax.optimization_barrier((direct, between))
    swap = [(i, i ^ 1) for i in range(n_pair)]
    return direct + [lax.ppermute(d, "pair", swap) for d in direct]


def body(spectra, pair_lists, pair_counts):
    n_pair = lax.axis_size("pair")
    n_seg = lax.axis_size("seg")
    freq = spectra.shape[2]
    most = pair_lists.shape[0]
    tiles = spectra.shape[3] // TILE
    chunks = GROUPS // n_seg
    rows = freq // n_pair // GROUPS
    me = jnp.stack([lax.axis_index("seg"), lax.axis_index("pair")]).astype(jnp.int32)
    x = spectra.reshape(2, freq, spectra.shape[3])
    lists = jnp.concatenate([pair_lists.reshape(-1), pair_counts])
    tables, phase = make_tables(freq)
    sums = make_sums(phase, freq, most)
    tables = [tables, sums]
    packed = [pack(x, chunk, n_seg, n_pair) for chunk in range(chunks)]
    lists, packed[-1] = lax.optimization_barrier((lists, packed[-1]))
    table = lax.all_gather(lists, "pair", axis=0)
    if chunks > 1:
        table, packed[1], _ = lax.optimization_barrier((table, packed[1], sums))
    done = []
    lags = None
    for sent in packed:
        got = lax.all_to_all(
            sent.reshape(n_seg * n_pair, tiles, 2, rows, TILE),
            ("seg", "pair"),
            split_axis=0,
            concat_axis=0,
            tiled=True,
        )
        if lags is not None:
            got, _ = lax.optimization_barrier((got, lags))
        spec = got.reshape(n_seg, n_pair * tiles, 2, rows, TILE)
        stack = stacks(me, table, spec, n_seg, n_pair, most)
        blocks = exchange_plane(stack, n_pair, done[1:3] or None)
        lags = dft(me, tables, blocks, freq, n_seg, n_pair, most)
        done += exchange(lags, "seg", n_seg)
    return unpack(me, done, n_seg, chunks, most)


def solution(mesh):
    return jax.shard_map(
        body,
        mesh=mesh,
        in_specs=(P("seg", None, None, "pair"), P("pair", None), P("pair")),
        out_specs=P("seg", "pair", None),
        check_vma=False,
    )
```

```python
import functools
import math

import jax
import jax.numpy as jnp
import numpy as np
from jax import lax
from jax.experimental import pallas as pl
from jax.experimental.pallas import tpu as pltpu
from jax.sharding import PartitionSpec as P

TILE = 128
LAG = 2048
GROUPS = 8
SMALL = pl.CostEstimate(flops=1, bytes_accessed=1, transcendentals=0)
CC = TILE // GROUPS


def lane_groups(shape):
    return lax.broadcasted_iota(jnp.int32, shape, len(shape) - 1) // CC


def shift_groups(x, by):
    return pltpu.roll(x, (by * CC) % TILE, x.ndim - 1)


def top_exponent(largest):
    return jnp.maximum(jnp.floor(jnp.log2(jnp.maximum(largest, 1e-36))), -90.0)


def encode(a, b, top):
    m = jnp.maximum(jnp.maximum(jnp.abs(a), jnp.abs(b)), 1e-36)
    e = jnp.minimum(jnp.maximum(jnp.floor(jnp.log2(m)), top - 15.0), top)
    s = jnp.exp2(12.0 - e)
    qa, qb = (
        jnp.clip(jnp.floor(x * s + 0.5), -8191.0, 8191.0).astype(jnp.int32) + 8192
        for x in (a, b)
    )
    return ((e - (top - 15.0)).astype(jnp.int32) << 28) | (qa << 14) | qb


ZERO = (8192 << 14) | 8192


def decode(code, top):
    s = jnp.exp2(((code >> 28) & 15).astype(jnp.float32) + (top - 27.0))
    a, b = (
        ((q & 16383) - 8192).astype(jnp.float32) * s for q in (code >> 14, code)
    )
    return a, b


ODD = 239.0 / 256.0
ODD_DIAGONAL = 169.0 / 256.0


def transpose_groups(vectors):
    v = list(vectors)
    grp = lane_groups(v[0].shape)
    for bit in (4, 2, 1):
        low = (grp & bit) == 0
        for i in range(GROUPS):
            if i & bit:
                continue
            a, b = v[i], v[i | bit]
            v[i] = jnp.where(low, a, shift_groups(b, bit))
            v[i | bit] = jnp.where(low, shift_groups(a, -bit), b)
    return v


def reduce_groups(vectors):
    v = list(vectors)
    grp = lane_groups(v[0].shape)
    low = (grp & 4) == 0
    v = [
        jnp.where(low, v[i], v[i + 4])
        + shift_groups(jnp.where(low, v[i + 4], v[i]), 4)
        for i in range(4)
    ]
    for bit in (2, 1):
        low = (grp & bit) == 0
        v = [
            jnp.where(low, v[i], v[i + bit])
            + jnp.where(low, shift_groups(v[i], -bit), shift_groups(v[i + bit], bit))
            for i in range(bit)
        ]
    return v[0]


def selection(n_seg, chunk, chans):
    wide = chans // TILE * n_seg * CC
    row = lax.broadcasted_iota(jnp.int32, (chans, wide), 0)
    col = lax.broadcasted_iota(jnp.int32, (chans, wide), 1)
    group = col // CC
    want = (
        group // n_seg * TILE
        + group % n_seg * (TILE // n_seg)
        + chunk * CC
        + col % CC
    )
    return (row == want).astype(jnp.bfloat16)


def pack_kernel(n_seg, chunk, x_ref, out_ref, buf_ref):
    n_pair = out_ref.shape[1]
    band = x_ref.shape[1] // n_pair
    sel = selection(n_seg, chunk, x_ref.shape[2])
    rows = band // GROUPS
    for p in range(n_pair):
        for ri in range(2):
            for part in range(sel.shape[1] // TILE):
                lanes = slice(part * TILE, (part + 1) * TILE)
                buf = buf_ref.at[p % 2, ri]
                buf[...] = jnp.dot(
                    x_ref[ri, p * band : (p + 1) * band, :],
                    sel[:, lanes],
                    preferred_element_type=jnp.float32,
                )
                v = [buf[pl.ds(fb, rows, stride=GROUPS), :] for fb in range(GROUPS)]
                v = transpose_groups(v)
                for g in range(GROUPS):
                    t, z = divmod(part * GROUPS + g, n_seg)
                    out_ref[z, p, t, ri] = v[g].astype(jnp.bfloat16)


def pack(x, chunk, n_seg, n_pair):
    _, freq, chans = x.shape
    band = freq // n_pair
    shape = (n_seg, n_pair, chans // TILE, 2, band // GROUPS, TILE)
    return pl.pallas_call(
        functools.partial(pack_kernel, n_seg, chunk),
        out_shape=jax.ShapeDtypeStruct(shape, jnp.bfloat16),
        grid=(2,),
        in_specs=[pl.BlockSpec((2, freq // 2, chans), lambda i: (0, i, 0))],
        out_specs=pl.BlockSpec(
            (n_seg, n_pair // 2) + shape[2:], lambda i: (0, i, 0, 0, 0, 0)
        ),
        scratch_shapes=[pltpu.VMEM((2, 2, band, TILE), jnp.float32)],
        name="pack",
        cost_estimate=SMALL,
    )(x)


def stack_kernel(n_seg, n_pair, most, me_ref, table_ref, spec_ref, *refs):
    outs, (sum_ref, big_ref) = refs[:-2], refs[-2:]
    rows = spec_ref.shape[3]
    inv = 1.0 / float(n_seg * n_seg)
    big_ref[...] = jnp.zeros_like(big_ref)
    for k in range(n_pair):
        owner = jnp.bitwise_xor(me_ref[1], k)
        count = table_ref[owner, 2 * most]

        def one(s, _):
            src = table_ref[owner, 2 * s]
            rcv = table_ref[owner, 2 * s + 1]
            lr = li = pr = pi = None
            for g in range(n_seg):
                a0 = spec_ref[g, src, 0].astype(jnp.float32)
                a1 = spec_ref[g, src, 1].astype(jnp.float32)
                b0 = spec_ref[g, rcv, 0].astype(jnp.float32)
                b1 = spec_ref[g, rcv, 1].astype(jnp.float32)
                cr = a0 * b0 + a1 * b1
                ci = a1 * b0 - a0 * b1
                m = lax.rsqrt(cr * cr + ci * ci + 1.0)
                if g == 0:
                    lr, li, pr, pi = cr, ci, cr * m, ci * m
                else:
                    lr, li, pr, pi = lr + cr, li + ci, pr + cr * m, pi + ci * m
            w = (pr * pr + pi * pi) * inv
            re, im = lr * w, li * w
            sum_ref[k, s, 0] = re
            sum_ref[k, s, 1] = im
            big = jnp.maximum(jnp.abs(re), jnp.abs(im))
            big_ref[...] = jnp.maximum(big_ref[...], big)
            return 0

        lax.fori_loop(0, count, one, 0)
    top = top_exponent(jnp.max(big_ref[...], keepdims=True))
    for k in range(n_pair):
        owner = jnp.bitwise_xor(me_ref[1], k)
        count = table_ref[owner, 2 * most]
        out_ref = outs[k // 2].at[k % 2]

        def code(s, _):
            at = pl.ds(pl.multiple_of(s * rows, rows), rows)
            out_ref[at, :] = encode(sum_ref[k, s, 0], sum_ref[k, s, 1], top)
            return 0

        def dead(s, _):
            at = pl.ds(pl.multiple_of(s * rows, rows), rows)
            out_ref[at, :] = jnp.full((rows, TILE), ZERO, jnp.int32)
            return 0

        lax.fori_loop(0, count, code, 0)
        lax.fori_loop(count, most, dead, 0)
        out_ref[most * rows :, :] = jnp.broadcast_to(top, (8, TILE)).astype(jnp.int32)


def stacks(me, table, spec, n_seg, n_pair, most):
    rows = spec.shape[3]
    shape = (2, most * rows + 8, TILE)
    smem = pl.BlockSpec(memory_space=pltpu.SMEM)
    vmem = pl.BlockSpec(memory_space=pltpu.VMEM)
    return pl.pallas_call(
        functools.partial(stack_kernel, n_seg, n_pair, most),
        out_shape=[jax.ShapeDtypeStruct(shape, jnp.int32)] * (n_pair // 2),
        in_specs=[smem, smem, vmem],
        out_specs=[vmem] * (n_pair // 2),
        scratch_shapes=[
            pltpu.VMEM((n_pair, most, 2, rows, TILE), jnp.float32),
            pltpu.VMEM((rows, TILE), jnp.float32),
        ],
        name="stack",
        compiler_params=pltpu.CompilerParams(vmem_limit_bytes=12 << 20),
        cost_estimate=SMALL,
    )(me, table, spec)


def dft_kernel(
    n_seg, n_pair, most, me_ref, whi_ref, wlo_ref, phase_ref, tables_ref, *refs
):
    ins, outs = refs[:n_pair], refs[n_pair : n_pair + n_seg]
    t_ref, sem, s32, shi, slo, y, zhi, zlo, sums, parts = refs[n_pair + n_seg :]
    copy = pltpu.make_async_copy(
        tables_ref.at[pl.ds(0, t_ref.shape[0])], t_ref, sem.at[0]
    )
    copy.start()
    rows = (ins[0].shape[1] - 8) // most
    half_h = whi_ref.shape[1] // 2
    wide = most * TILE
    for k in range(n_pair):
        band = jnp.bitwise_xor(me_ref[1], k)
        src = ins[k % 2 * (n_pair // 2) + k // 2].at[k % 2]
        at = pl.ds(pl.multiple_of(band * rows, rows), rows)
        top = src[most * rows : most * rows + 1, :].astype(jnp.float32)
        for s in range(most):
            pair = decode(src[s * rows : (s + 1) * rows, :], top)
            for ri in range(2):
                s32[ri, at, s * TILE : (s + 1) * TILE] = pair[ri]
    for ri in range(2):
        full = s32[ri]
        hi = full.astype(jnp.bfloat16)
        lo = (full - hi.astype(jnp.float32)).astype(jnp.bfloat16)
        own = slice(ri * wide, (ri + 1) * wide)
        other = slice((1 - ri) * wide, (2 - ri) * wide)
        for to, part in ((shi, hi), (slo, lo)):
            to[:half_h, own] = part
            to[half_h:, other] = part if ri == 0 else -part
    for ri in range(2):
        n = slice(ri * wide, (ri + 1) * wide)
        y[ri] = (
            jnp.dot(wlo_ref[...], shi[:, n], preferred_element_type=jnp.float32)
            + jnp.dot(whi_ref[...], slo[:, n], preferred_element_type=jnp.float32)
        ) + jnp.dot(whi_ref[...], shi[:, n], preferred_element_type=jnp.float32)
    period = y.shape[1]
    step_rows = 64
    for b in range(period // step_rows):
        at = slice(b * step_rows, (b + 1) * step_rows)
        c = phase_ref[at, :TILE]
        d = phase_ref[at, TILE:]
        for s in range(most):
            lanes = slice(s * TILE, (s + 1) * TILE)
            yr = y[0, at, lanes]
            yi = y[1, at, lanes]
            for ri, z in enumerate((c * yr - d * yi, d * yr + c * yi)):
                to = slice((ri * most + s) * TILE, (ri * most + s + 1) * TILE)
                hi = z.astype(jnp.bfloat16)
                zhi[at, to] = hi
                zlo[at, to] = (z - hi.astype(jnp.float32)).astype(jnp.bfloat16)
    copy.wait()
    t = t_ref[...]
    sums[...] = jnp.dot(zlo[...], t, preferred_element_type=jnp.float32) + jnp.dot(
        zhi[...], t, preferred_element_type=jnp.float32
    )
    half = parts.shape[1]
    big = None
    first = lax.broadcasted_iota(jnp.int32, (half, TILE), 1) < TILE // 2
    for dest in range(n_seg):
        lag = dest * 2 * half
        r, l0 = lag // period, lag % period
        col = slice(r // 2 * TILE, (r // 2 + 1) * TILE)
        low = sums[l0 : l0 + half, col]
        high = sums[l0 + half : l0 + 2 * half, col]
        if r % 2 == 0:
            high = pltpu.roll(high, TILE // 2, 1)
        else:
            low = pltpu.roll(low, TILE // 2, 1)
        part = jnp.where(first, low, high)
        parts[dest] = part
        part = jnp.max(jnp.abs(part), axis=0, keepdims=True)
        big = part if big is None else jnp.maximum(big, part)
    top = top_exponent(jnp.max(big, keepdims=True))
    for k in range(n_seg):
        part = parts[jnp.bitwise_xor(me_ref[0], k)]
        outs[k][: half // 2, :] = encode(part[: half // 2], part[half // 2 :], top)
        outs[k][half // 2 :, :] = jnp.broadcast_to(top, (8, TILE)).astype(jnp.int32)


def sums_kernel(most, turns, shift, out_ref, t_ref, sem):
    shape = (most * TILE, turns * most * CC)
    row = lax.broadcasted_iota(jnp.int32, shape, 0)
    col = lax.broadcasted_iota(jnp.int32, shape, 1)
    same = (row // TILE == col // CC % most) & (row % CC == col % CC)
    fb = row // CC % GROUPS
    eighths = (col // (most * CC) - shift) * fb
    one = jnp.where(fb % 2 == 0, 1.0, ODD)
    for ri in range(2):
        e = jnp.bitwise_and(eighths + 2 * ri, 7)
        size = jnp.where(e % 4 == 2, 0.0, jnp.where(e % 2 == 0, one, ODD_DIAGONAL))
        t = jnp.where(same, jnp.where((e > 2) & (e < 6), -size, size), 0.0)
        t_ref[ri * most * TILE : (ri + 1) * most * TILE, :] = t.astype(jnp.bfloat16)
    copy = pltpu.make_async_copy(
        t_ref, out_ref.at[pl.ds(0, t_ref.shape[0])], sem.at[0]
    )
    copy.start()
    copy.wait()


def make_sums(freq, most):
    period = 2 * (freq // GROUPS)
    turns = LAG // period
    width = turns * most * CC
    return pl.pallas_call(
        functools.partial(sums_kernel, most, turns, LAG // 2 // period),
        out_shape=jax.ShapeDtypeStruct((96 << 10, width), jnp.bfloat16),
        out_specs=pl.BlockSpec(memory_space=pltpu.HBM),
        scratch_shapes=[
            pltpu.VMEM((2 * most * TILE, width), jnp.bfloat16),
            pltpu.SemaphoreType.DMA((1,)),
        ],
        name="sums",
        cost_estimate=SMALL,
    )()


def make_tables(freq):
    h = freq // GROUPS
    period = 2 * h
    angle = np.arange(period)[:, None] * np.arange(h)[None, :] % period
    angle = angle * (2.0 * math.pi / period)
    w = np.concatenate([np.cos(angle), np.sin(angle)], 1).astype(np.float32)
    whi = w.astype(jnp.bfloat16)
    wlo = (w - whi.astype(np.float32)).astype(jnp.bfloat16)
    fb = np.arange(TILE) // CC
    phase = ((np.arange(period)[:, None] * fb[None, :]) % (2 * freq)) * (math.pi / freq)
    scale = np.where(fb % 2 == 0, 1.0, 1.0 / ODD) / math.sqrt(freq)
    scale = np.concatenate([scale, scale])[None, :]
    phase = (np.concatenate([np.cos(phase), np.sin(phase)], 1) * scale).astype(np.float32)
    return [jnp.asarray(c) for c in (whi, wlo, phase)]


def dft(me, tables, blocks, freq, n_seg, n_pair, most):
    period = 2 * (freq // GROUPS)
    smem = pl.BlockSpec(memory_space=pltpu.SMEM)
    vmem = pl.BlockSpec(memory_space=pltpu.VMEM)
    half = LAG // n_seg // 2
    wide = most * TILE
    return pl.pallas_call(
        functools.partial(dft_kernel, n_seg, n_pair, most),
        out_shape=[jax.ShapeDtypeStruct((half // 2 + 8, TILE), jnp.int32)] * n_seg,
        in_specs=[smem, vmem, vmem, vmem, pl.BlockSpec(memory_space=pltpu.HBM)]
        + [vmem] * len(blocks),
        out_specs=[vmem] * n_seg,
        scratch_shapes=[
            pltpu.VMEM((2 * wide, LAG // period * most * CC), jnp.bfloat16),
            pltpu.SemaphoreType.DMA((1,)),
            pltpu.VMEM((2, period // 2, wide), jnp.float32),
            pltpu.VMEM((period, 2 * wide), jnp.bfloat16),
            pltpu.VMEM((period, 2 * wide), jnp.bfloat16),
            pltpu.VMEM((2, period, wide), jnp.float32),
            pltpu.VMEM((period, 2 * wide), jnp.bfloat16),
            pltpu.VMEM((period, 2 * wide), jnp.bfloat16),
            pltpu.VMEM((period, LAG // period * most * CC), jnp.float32),
            pltpu.VMEM((n_seg, half, TILE), jnp.float32),
        ],
        name="dft",
        compiler_params=pltpu.CompilerParams(vmem_limit_bytes=24 << 20),
        cost_estimate=SMALL,
    )(me, *tables, *blocks)


def unpack_kernel(n_seg, chunks, most, me_ref, *refs):
    ins = refs[: n_seg * chunks]
    out_ref, buf = refs[n_seg * chunks :]
    half = buf.shape[1]

    @pl.when(pl.program_id(0) == 0)
    def _():
        for k in range(n_seg):
            z = jnp.bitwise_xor(me_ref[0], k)
            for ch in range(chunks):
                src = ins[ch * n_seg + k]
                top = src[half // 2 : half // 2 + 1, :].astype(jnp.float32)
                low, high = decode(src[: half // 2, :], top)
                buf[z * chunks + ch, : half // 2] = low
                buf[z * chunks + ch, half // 2 :] = high

    step_rows = 16
    block = out_ref.shape[1]
    for b in range(block // step_rows):
        at = pl.multiple_of(pl.program_id(0) * block + b * step_rows, step_rows)
        v = transpose_groups([buf[i, pl.ds(at, step_rows), :] for i in range(GROUPS)])
        for h in range(2):
            for s in range(most):
                out_ref[h, b * step_rows : (b + 1) * step_rows, s, :] = v[h * most + s]


def unpack(me, parts, n_seg, chunks, most):
    half = 2 * (parts[0].shape[0] - 8)
    steps = 4
    smem = pl.BlockSpec(memory_space=pltpu.SMEM)
    whole = pl.BlockSpec(parts[0].shape, lambda b: (0, 0))
    out = pl.pallas_call(
        functools.partial(unpack_kernel, n_seg, chunks, most),
        out_shape=jax.ShapeDtypeStruct((2, half, most, TILE), jnp.float32),
        grid=(steps,),
        in_specs=[smem] + [whole] * len(parts),
        out_specs=pl.BlockSpec((2, half // steps, most, TILE), lambda b: (0, b, 0, 0)),
        scratch_shapes=[pltpu.VMEM((GROUPS, half, TILE), jnp.float32)],
        name="unpack",
        compiler_params=pltpu.CompilerParams(vmem_limit_bytes=12 << 20),
        cost_estimate=SMALL,
    )(me, *parts)
    return out.reshape(2 * half, most, TILE)


def exchange(blocks, axis, size):
    return [blocks[0]] + [
        lax.ppermute(blocks[k], axis, [(i, i ^ k) for i in range(size)])
        for k in range(1, size)
    ]


def exchange_plane(blocks, n_pair, between=None):
    direct = [blocks[0]] + [
        lax.ppermute(blocks[k], "pair", [(i, i ^ (2 * k)) for i in range(n_pair)])
        for k in range(1, n_pair // 2)
    ]
    if between is not None:
        direct, _ = lax.optimization_barrier((direct, between))
    swap = [(i, i ^ 1) for i in range(n_pair)]
    return direct + [lax.ppermute(d, "pair", swap) for d in direct]


def body(spectra, pair_lists, pair_counts):
    n_pair = lax.axis_size("pair")
    n_seg = lax.axis_size("seg")
    freq = spectra.shape[2]
    most = pair_lists.shape[0]
    tiles = spectra.shape[3] // TILE
    chunks = GROUPS // n_seg
    rows = freq // n_pair // GROUPS
    me = jnp.stack([lax.axis_index("seg"), lax.axis_index("pair")]).astype(jnp.int32)
    x = spectra.reshape(2, freq, spectra.shape[3])
    lists = jnp.concatenate([pair_lists.reshape(-1), pair_counts])
    sums = make_sums(freq, most)
    tables = make_tables(freq) + [sums]
    packed = [pack(x, chunk, n_seg, n_pair) for chunk in range(chunks)]
    lists, packed[-1] = lax.optimization_barrier((lists, packed[-1]))
    table = lax.all_gather(lists, "pair", axis=0)
    if chunks > 1:
        table, packed[1], _ = lax.optimization_barrier((table, packed[1], sums))
    done = []
    lags = None
    for sent in packed:
        got = lax.all_to_all(
            sent.reshape(n_seg * n_pair, tiles, 2, rows, TILE),
            ("seg", "pair"),
            split_axis=0,
            concat_axis=0,
            tiled=True,
        )
        if lags is not None:
            got, _ = lax.optimization_barrier((got, lags))
        spec = got.reshape(n_seg, n_pair * tiles, 2, rows, TILE)
        stack = stacks(me, table, spec, n_seg, n_pair, most)
        blocks = exchange_plane(stack, n_pair, done[1:3] or None)
        lags = dft(me, tables, blocks, freq, n_seg, n_pair, most)
        done += exchange(lags, "seg", n_seg)
    return unpack(me, done, n_seg, chunks, most)


def solution(mesh):
    return jax.shard_map(
        body,
        mesh=mesh,
        in_specs=(P("seg", None, None, "pair"), P("pair", None), P("pair")),
        out_specs=P("seg", "pair", None),
        check_vma=False,
    )
```

```python
import functools
import math

import jax
import jax.numpy as jnp
import numpy as np
from jax import lax
from jax.experimental import pallas as pl
from jax.experimental.pallas import tpu as pltpu
from jax.sharding import PartitionSpec as P

TILE = 128
LAG = 2048
GROUPS = 8
SMALL = pl.CostEstimate(flops=1, bytes_accessed=1, transcendentals=0)
CC = TILE // GROUPS


def lane_groups(shape):
    return lax.broadcasted_iota(jnp.int32, shape, len(shape) - 1) // CC


def shift_groups(x, by):
    return pltpu.roll(x, (by * CC) % TILE, x.ndim - 1)


def top_exponent(largest):
    return jnp.maximum(jnp.floor(jnp.log2(jnp.maximum(largest, 1e-36))), -90.0)


def encode(a, b, top):
    m = jnp.maximum(jnp.maximum(jnp.abs(a), jnp.abs(b)), 1e-36)
    e = jnp.minimum(jnp.maximum(jnp.floor(jnp.log2(m)), top - 15.0), top)
    s = jnp.exp2(12.0 - e)
    qa, qb = (
        jnp.clip(jnp.floor(x * s + 0.5), -8191.0, 8191.0).astype(jnp.int32) + 8192
        for x in (a, b)
    )
    return ((e - (top - 15.0)).astype(jnp.int32) << 28) | (qa << 14) | qb


ZERO = (8192 << 14) | 8192


def decode(code, top):
    s = jnp.exp2(((code >> 28) & 15).astype(jnp.float32) + (top - 27.0))
    a, b = (
        ((q & 16383) - 8192).astype(jnp.float32) * s for q in (code >> 14, code)
    )
    return a, b


FINE = 64
ODD = 239.0 / 256.0
ODD_DIAGONAL = 169.0 / 256.0


def transpose_groups(vectors):
    v = list(vectors)
    grp = lane_groups(v[0].shape)
    for bit in (4, 2, 1):
        low = (grp & bit) == 0
        for i in range(GROUPS):
            if i & bit:
                continue
            a, b = v[i], v[i | bit]
            v[i] = jnp.where(low, a, shift_groups(b, bit))
            v[i | bit] = jnp.where(low, shift_groups(a, -bit), b)
    return v


def reduce_groups(vectors):
    v = list(vectors)
    grp = lane_groups(v[0].shape)
    low = (grp & 4) == 0
    v = [
        jnp.where(low, v[i], v[i + 4])
        + shift_groups(jnp.where(low, v[i + 4], v[i]), 4)
        for i in range(4)
    ]
    for bit in (2, 1):
        low = (grp & bit) == 0
        v = [
            jnp.where(low, v[i], v[i + bit])
            + jnp.where(low, shift_groups(v[i], -bit), shift_groups(v[i + bit], bit))
            for i in range(bit)
        ]
    return v[0]


def selection(n_seg, chunk, chans):
    wide = chans // TILE * n_seg * CC
    row = lax.broadcasted_iota(jnp.int32, (chans, wide), 0)
    col = lax.broadcasted_iota(jnp.int32, (chans, wide), 1)
    group = col // CC
    want = (
        group // n_seg * TILE
        + group % n_seg * (TILE // n_seg)
        + chunk * CC
        + col % CC
    )
    return (row == want).astype(jnp.bfloat16)


def pack_kernel(n_seg, chunk, x_ref, out_ref, buf_ref):
    n_pair = out_ref.shape[1]
    band = x_ref.shape[1] // n_pair
    sel = selection(n_seg, chunk, x_ref.shape[2])
    rows = band // GROUPS
    for p in range(n_pair):
        for ri in range(2):
            for part in range(sel.shape[1] // TILE):
                lanes = slice(part * TILE, (part + 1) * TILE)
                buf = buf_ref.at[p % 2, ri]
                buf[...] = jnp.dot(
                    x_ref[ri, p * band : (p + 1) * band, :],
                    sel[:, lanes],
                    preferred_element_type=jnp.float32,
                )
                v = [buf[pl.ds(fb, rows, stride=GROUPS), :] for fb in range(GROUPS)]
                v = transpose_groups(v)
                for g in range(GROUPS):
                    t, z = divmod(part * GROUPS + g, n_seg)
                    out_ref[z, p, t, ri] = v[g].astype(jnp.bfloat16)


def pack(x, chunk, n_seg, n_pair):
    _, freq, chans = x.shape
    band = freq // n_pair
    shape = (n_seg, n_pair, chans // TILE, 2, band // GROUPS, TILE)
    return pl.pallas_call(
        functools.partial(pack_kernel, n_seg, chunk),
        out_shape=jax.ShapeDtypeStruct(shape, jnp.bfloat16),
        grid=(2,),
        in_specs=[pl.BlockSpec((2, freq // 2, chans), lambda i: (0, i, 0))],
        out_specs=pl.BlockSpec(
            (n_seg, n_pair // 2) + shape[2:], lambda i: (0, i, 0, 0, 0, 0)
        ),
        scratch_shapes=[pltpu.VMEM((2, 2, band, TILE), jnp.float32)],
        name="pack",
        cost_estimate=SMALL,
    )(x)


def stack_kernel(n_seg, n_pair, most, me_ref, table_ref, spec_ref, *refs):
    outs, (sum_ref, big_ref) = refs[:-2], refs[-2:]
    rows = spec_ref.shape[3]
    inv = 1.0 / float(n_seg * n_seg)
    big_ref[...] = jnp.zeros_like(big_ref)
    for k in range(n_pair):
        owner = jnp.bitwise_xor(me_ref[1], k)
        count = table_ref[owner, 2 * most]

        def one(s, _):
            src = table_ref[owner, 2 * s]
            rcv = table_ref[owner, 2 * s + 1]
            lr = li = pr = pi = None
            for g in range(n_seg):
                a0 = spec_ref[g, src, 0].astype(jnp.float32)
                a1 = spec_ref[g, src, 1].astype(jnp.float32)
                b0 = spec_ref[g, rcv, 0].astype(jnp.float32)
                b1 = spec_ref[g, rcv, 1].astype(jnp.float32)
                cr = a0 * b0 + a1 * b1
                ci = a1 * b0 - a0 * b1
                m = lax.rsqrt(cr * cr + ci * ci + 1.0)
                if g == 0:
                    lr, li, pr, pi = cr, ci, cr * m, ci * m
                else:
                    lr, li, pr, pi = lr + cr, li + ci, pr + cr * m, pi + ci * m
            w = (pr * pr + pi * pi) * inv
            re, im = lr * w, li * w
            sum_ref[k, s, 0] = re
            sum_ref[k, s, 1] = im
            big = jnp.maximum(jnp.abs(re), jnp.abs(im))
            big_ref[...] = jnp.maximum(big_ref[...], big)
            return 0

        lax.fori_loop(0, count, one, 0)
    top = top_exponent(jnp.max(big_ref[...], keepdims=True))
    for k in range(n_pair):
        owner = jnp.bitwise_xor(me_ref[1], k)
        count = table_ref[owner, 2 * most]
        out_ref = outs[k // 2].at[k % 2]

        def code(s, _):
            at = pl.ds(pl.multiple_of(s * rows, rows), rows)
            out_ref[at, :] = encode(sum_ref[k, s, 0], sum_ref[k, s, 1], top)
            return 0

        def dead(s, _):
            at = pl.ds(pl.multiple_of(s * rows, rows), rows)
            out_ref[at, :] = jnp.full((rows, TILE), ZERO, jnp.int32)
            return 0

        lax.fori_loop(0, count, code, 0)
        lax.fori_loop(count, most, dead, 0)
        out_ref[most * rows :, :] = jnp.broadcast_to(top, (8, TILE)).astype(jnp.int32)


def stacks(me, table, spec, n_seg, n_pair, most):
    rows = spec.shape[3]
    shape = (2, most * rows + 8, TILE)
    smem = pl.BlockSpec(memory_space=pltpu.SMEM)
    vmem = pl.BlockSpec(memory_space=pltpu.VMEM)
    return pl.pallas_call(
        functools.partial(stack_kernel, n_seg, n_pair, most),
        out_shape=[jax.ShapeDtypeStruct(shape, jnp.int32)] * (n_pair // 2),
        in_specs=[smem, smem, vmem],
        out_specs=[vmem] * (n_pair // 2),
        scratch_shapes=[
            pltpu.VMEM((n_pair, most, 2, rows, TILE), jnp.float32),
            pltpu.VMEM((rows, TILE), jnp.float32),
        ],
        name="stack",
        compiler_params=pltpu.CompilerParams(vmem_limit_bytes=12 << 20),
        cost_estimate=SMALL,
    )(me, table, spec)


def dft_kernel(
    n_seg, n_pair, most, me_ref, w_ref, phase_ref, tables_ref, *refs
):
    ins, outs = refs[:n_pair], refs[n_pair : n_pair + n_seg]
    t_ref, sem, s32, shi, slo, y, zhi, zlo, sums, parts = refs[n_pair + n_seg :]
    copy = pltpu.make_async_copy(
        tables_ref.at[pl.ds(0, t_ref.shape[0])], t_ref, sem.at[0]
    )
    copy.start()
    rows = (ins[0].shape[1] - 8) // most
    half_h = w_ref.shape[1] // 2
    whi_ref, wlo_ref = w_ref.at[: 2 * half_h], w_ref.at[2 * half_h :]
    wide = most * TILE
    for k in range(n_pair):
        band = jnp.bitwise_xor(me_ref[1], k)
        src = ins[k % 2 * (n_pair // 2) + k // 2].at[k % 2]
        at = pl.ds(pl.multiple_of(band * rows, rows), rows)
        top = src[most * rows : most * rows + 1, :].astype(jnp.float32)
        for s in range(most):
            pair = decode(src[s * rows : (s + 1) * rows, :], top)
            for ri in range(2):
                s32[ri, at, s * TILE : (s + 1) * TILE] = pair[ri]
    for ri in range(2):
        full = s32[ri]
        hi = full.astype(jnp.bfloat16)
        lo = (full - hi.astype(jnp.float32)).astype(jnp.bfloat16)
        own = slice(ri * wide, (ri + 1) * wide)
        other = slice((1 - ri) * wide, (2 - ri) * wide)
        for to, part in ((shi, hi), (slo, lo)):
            to[:half_h, own] = part
            to[half_h:, other] = part if ri == 0 else -part
    for ri in range(2):
        n = slice(ri * wide, (ri + 1) * wide)
        y[ri] = (
            jnp.dot(wlo_ref[...], shi[:, n], preferred_element_type=jnp.float32)
            + jnp.dot(whi_ref[...], slo[:, n], preferred_element_type=jnp.float32)
        ) + jnp.dot(whi_ref[...], shi[:, n], preferred_element_type=jnp.float32)
    period = y.shape[1]
    step_rows = FINE
    fine_c, fine_d = phase_ref[:FINE, :TILE], phase_ref[:FINE, TILE:]
    for b in range(period // step_rows):
        at = slice(b * step_rows, (b + 1) * step_rows)
        big_c = phase_ref[FINE + b : FINE + b + 1, :TILE]
        big_d = phase_ref[FINE + b : FINE + b + 1, TILE:]
        c = big_c * fine_c - big_d * fine_d
        d = big_d * fine_c + big_c * fine_d
        for s in range(most):
            lanes = slice(s * TILE, (s + 1) * TILE)
            yr = y[0, at, lanes]
            yi = y[1, at, lanes]
            for ri, z in enumerate((c * yr - d * yi, d * yr + c * yi)):
                to = slice((ri * most + s) * TILE, (ri * most + s + 1) * TILE)
                hi = z.astype(jnp.bfloat16)
                zhi[at, to] = hi
                zlo[at, to] = (z - hi.astype(jnp.float32)).astype(jnp.bfloat16)
    copy.wait()
    t = t_ref[...]
    sums[...] = jnp.dot(zlo[...], t, preferred_element_type=jnp.float32) + jnp.dot(
        zhi[...], t, preferred_element_type=jnp.float32
    )
    half = parts.shape[1]
    big = None
    first = lax.broadcasted_iota(jnp.int32, (half, TILE), 1) < TILE // 2
    for dest in range(n_seg):
        lag = dest * 2 * half
        r, l0 = lag // period, lag % period
        col = slice(r // 2 * TILE, (r // 2 + 1) * TILE)
        low = sums[l0 : l0 + half, col]
        high = sums[l0 + half : l0 + 2 * half, col]
        if r % 2 == 0:
            high = pltpu.roll(high, TILE // 2, 1)
        else:
            low = pltpu.roll(low, TILE // 2, 1)
        part = jnp.where(first, low, high)
        parts[dest] = part
        part = jnp.max(jnp.abs(part), axis=0, keepdims=True)
        big = part if big is None else jnp.maximum(big, part)
    top = top_exponent(jnp.max(big, keepdims=True))
    for k in range(n_seg):
        part = parts[jnp.bitwise_xor(me_ref[0], k)]
        outs[k][: half // 2, :] = encode(part[: half // 2], part[half // 2 :], top)
        outs[k][half // 2 :, :] = jnp.broadcast_to(top, (8, TILE)).astype(jnp.int32)


def sums_kernel(most, turns, shift, out_ref, t_ref, sem):
    shape = (most * TILE, turns * most * CC)
    row = lax.broadcasted_iota(jnp.int32, shape, 0)
    col = lax.broadcasted_iota(jnp.int32, shape, 1)
    same = (row // TILE == col // CC % most) & (row % CC == col % CC)
    fb = row // CC % GROUPS
    eighths = (col // (most * CC) - shift) * fb
    one = jnp.where(fb % 2 == 0, 1.0, ODD)
    for ri in range(2):
        e = jnp.bitwise_and(eighths + 2 * ri, 7)
        size = jnp.where(e % 4 == 2, 0.0, jnp.where(e % 2 == 0, one, ODD_DIAGONAL))
        t = jnp.where(same, jnp.where((e > 2) & (e < 6), -size, size), 0.0)
        t_ref[ri * most * TILE : (ri + 1) * most * TILE, :] = t.astype(jnp.bfloat16)
    copy = pltpu.make_async_copy(
        t_ref, out_ref.at[pl.ds(0, t_ref.shape[0])], sem.at[0]
    )
    copy.start()
    copy.wait()


def make_sums(freq, most):
    period = 2 * (freq // GROUPS)
    turns = LAG // period
    width = turns * most * CC
    return pl.pallas_call(
        functools.partial(sums_kernel, most, turns, LAG // 2 // period),
        out_shape=jax.ShapeDtypeStruct((96 << 10, width), jnp.bfloat16),
        out_specs=pl.BlockSpec(memory_space=pltpu.HBM),
        scratch_shapes=[
            pltpu.VMEM((2 * most * TILE, width), jnp.bfloat16),
            pltpu.SemaphoreType.DMA((1,)),
        ],
        name="sums",
        cost_estimate=SMALL,
    )()


def make_tables(freq):
    h = freq // GROUPS
    period = 2 * h
    angle = np.arange(period)[:, None] * np.arange(h)[None, :] % period
    angle = angle * (2.0 * math.pi / period)
    w = np.concatenate([np.cos(angle), np.sin(angle)], 1).astype(np.float32)
    whi = w.astype(jnp.bfloat16)
    wlo = (w - whi.astype(np.float32)).astype(jnp.bfloat16)
    fb = np.arange(TILE) // CC
    scale = np.where(fb % 2 == 0, 1.0, 1.0 / ODD) / math.sqrt(freq)
    parts = []
    for at, gain in ((np.arange(FINE), scale), (np.arange(0, period, FINE), 1.0)):
        angle = (at[:, None] * fb[None, :] % (2 * freq)) * (math.pi / freq)
        parts.append(np.concatenate([np.cos(angle) * gain, np.sin(angle) * gain], 1))
    phase = np.concatenate(parts).astype(np.float32)
    return [jnp.asarray(c) for c in (np.concatenate([whi, wlo]), phase)]


def dft(me, tables, blocks, freq, n_seg, n_pair, most):
    period = 2 * (freq // GROUPS)
    smem = pl.BlockSpec(memory_space=pltpu.SMEM)
    vmem = pl.BlockSpec(memory_space=pltpu.VMEM)
    half = LAG // n_seg // 2
    wide = most * TILE
    return pl.pallas_call(
        functools.partial(dft_kernel, n_seg, n_pair, most),
        out_shape=[jax.ShapeDtypeStruct((half // 2 + 8, TILE), jnp.int32)] * n_seg,
        in_specs=[smem, vmem, vmem, pl.BlockSpec(memory_space=pltpu.HBM)]
        + [vmem] * len(blocks),
        out_specs=[vmem] * n_seg,
        scratch_shapes=[
            pltpu.VMEM((2 * wide, LAG // period * most * CC), jnp.bfloat16),
            pltpu.SemaphoreType.DMA((1,)),
            pltpu.VMEM((2, period // 2, wide), jnp.float32),
            pltpu.VMEM((period, 2 * wide), jnp.bfloat16),
            pltpu.VMEM((period, 2 * wide), jnp.bfloat16),
            pltpu.VMEM((2, period, wide), jnp.float32),
            pltpu.VMEM((period, 2 * wide), jnp.bfloat16),
            pltpu.VMEM((period, 2 * wide), jnp.bfloat16),
            pltpu.VMEM((period, LAG // period * most * CC), jnp.float32),
            pltpu.VMEM((n_seg, half, TILE), jnp.float32),
        ],
        name="dft",
        compiler_params=pltpu.CompilerParams(vmem_limit_bytes=24 << 20),
        cost_estimate=SMALL,
    )(me, *tables, *blocks)


def unpack_kernel(n_seg, chunks, most, me_ref, *refs):
    ins = refs[: n_seg * chunks]
    out_ref, buf = refs[n_seg * chunks :]
    half = buf.shape[1]

    @pl.when(pl.program_id(0) == 0)
    def _():
        for k in range(n_seg):
            z = jnp.bitwise_xor(me_ref[0], k)
            for ch in range(chunks):
                src = ins[ch * n_seg + k]
                top = src[half // 2 : half // 2 + 1, :].astype(jnp.float32)
                low, high = decode(src[: half // 2, :], top)
                buf[z * chunks + ch, : half // 2] = low
                buf[z * chunks + ch, half // 2 :] = high

    step_rows = 16
    block = out_ref.shape[1]
    for b in range(block // step_rows):
        at = pl.multiple_of(pl.program_id(0) * block + b * step_rows, step_rows)
        v = transpose_groups([buf[i, pl.ds(at, step_rows), :] for i in range(GROUPS)])
        for h in range(2):
            for s in range(most):
                out_ref[h, b * step_rows : (b + 1) * step_rows, s, :] = v[h * most + s]


def unpack(me, parts, n_seg, chunks, most):
    half = 2 * (parts[0].shape[0] - 8)
    steps = 4
    smem = pl.BlockSpec(memory_space=pltpu.SMEM)
    whole = pl.BlockSpec(parts[0].shape, lambda b: (0, 0))
    out = pl.pallas_call(
        functools.partial(unpack_kernel, n_seg, chunks, most),
        out_shape=jax.ShapeDtypeStruct((2, half, most, TILE), jnp.float32),
        grid=(steps,),
        in_specs=[smem] + [whole] * len(parts),
        out_specs=pl.BlockSpec((2, half // steps, most, TILE), lambda b: (0, b, 0, 0)),
        scratch_shapes=[pltpu.VMEM((GROUPS, half, TILE), jnp.float32)],
        name="unpack",
        compiler_params=pltpu.CompilerParams(vmem_limit_bytes=12 << 20),
        cost_estimate=SMALL,
    )(me, *parts)
    return out.reshape(2 * half, most, TILE)


def exchange(blocks, axis, size):
    got = {
        k: lax.ppermute(blocks[k], axis, [(i, i ^ k) for i in range(size)])
        for k in reversed(range(1, size))
    }
    return [blocks[0]] + [got[k] for k in range(1, size)]


def exchange_plane(blocks, n_pair, between=None):
    direct = [blocks[0]] + [
        lax.ppermute(blocks[k], "pair", [(i, i ^ (2 * k)) for i in range(n_pair)])
        for k in range(1, n_pair // 2)
    ]
    if between is not None:
        direct, _ = lax.optimization_barrier((direct, between))
    swap = [(i, i ^ 1) for i in range(n_pair)]
    return direct + [lax.ppermute(d, "pair", swap) for d in direct]


def body(spectra, pair_lists, pair_counts):
    n_pair = lax.axis_size("pair")
    n_seg = lax.axis_size("seg")
    freq = spectra.shape[2]
    most = pair_lists.shape[0]
    tiles = spectra.shape[3] // TILE
    chunks = GROUPS // n_seg
    rows = freq // n_pair // GROUPS
    me = jnp.stack([lax.axis_index("seg"), lax.axis_index("pair")]).astype(jnp.int32)
    x = spectra.reshape(2, freq, spectra.shape[3])
    lists = jnp.concatenate([pair_lists.reshape(-1), pair_counts])
    sums = make_sums(freq, most)
    tables = make_tables(freq) + [sums]
    packed = [pack(x, chunk, n_seg, n_pair) for chunk in range(chunks)]
    lists, packed[-1] = lax.optimization_barrier((lists, packed[-1]))
    table = lax.all_gather(lists, "pair", axis=0)
    if chunks > 1:
        table, packed[1], _ = lax.optimization_barrier((table, packed[1], sums))
    done = []
    lags = None
    for sent in packed:
        got = lax.all_to_all(
            sent.reshape(n_seg * n_pair, tiles, 2, rows, TILE),
            ("seg", "pair"),
            split_axis=0,
            concat_axis=0,
            tiled=True,
        )
        if lags is not None:
            got, _ = lax.optimization_barrier((got, lags))
        spec = got.reshape(n_seg, n_pair * tiles, 2, rows, TILE)
        stack = stacks(me, table, spec, n_seg, n_pair, most)
        blocks = exchange_plane(stack, n_pair, done[1:3] or None)
        lags = dft(me, tables, blocks, freq, n_seg, n_pair, most)
        done += exchange(lags, "seg", n_seg)
    return unpack(me, done, n_seg, chunks, most)


def solution(mesh):
    return jax.shard_map(
        body,
        mesh=mesh,
        in_specs=(P("seg", None, None, "pair"), P("pair", None), P("pair")),
        out_specs=P("seg", "pair", None),
        check_vma=False,
    )
```

```python
import functools
import math

import jax
import jax.numpy as jnp
import numpy as np
from jax import lax
from jax.experimental import pallas as pl
from jax.experimental.pallas import tpu as pltpu
from jax.sharding import PartitionSpec as P

TILE = 128
LAG = 2048
GROUPS = 8
SMALL = pl.CostEstimate(flops=1, bytes_accessed=1, transcendentals=0)
CC = TILE // GROUPS


def lane_groups(shape):
    return lax.broadcasted_iota(jnp.int32, shape, len(shape) - 1) // CC


def shift_groups(x, by):
    return pltpu.roll(x, (by * CC) % TILE, x.ndim - 1)


def top_exponent(largest):
    return jnp.maximum(jnp.floor(jnp.log2(jnp.maximum(largest, 1e-36))), -90.0)


def encode(a, b, top):
    m = jnp.maximum(jnp.maximum(jnp.abs(a), jnp.abs(b)), 1e-36)
    e = jnp.minimum(jnp.maximum(jnp.floor(jnp.log2(m)), top - 15.0), top)
    s = jnp.exp2(12.0 - e)
    qa, qb = (
        jnp.clip(jnp.floor(x * s + 0.5), -8191.0, 8191.0).astype(jnp.int32) + 8192
        for x in (a, b)
    )
    return ((e - (top - 15.0)).astype(jnp.int32) << 28) | (qa << 14) | qb


ZERO = (8192 << 14) | 8192


def decode(code, top):
    s = jnp.exp2(((code >> 28) & 15).astype(jnp.float32) + (top - 27.0))
    a, b = (
        ((q & 16383) - 8192).astype(jnp.float32) * s for q in (code >> 14, code)
    )
    return a, b


FINE = 64
ODD = 239.0 / 256.0
ODD_DIAGONAL = 169.0 / 256.0


def transpose_groups(vectors):
    v = list(vectors)
    grp = lane_groups(v[0].shape)
    for bit in (4, 2, 1):
        low = (grp & bit) == 0
        for i in range(GROUPS):
            if i & bit:
                continue
            a, b = v[i], v[i | bit]
            v[i] = jnp.where(low, a, shift_groups(b, bit))
            v[i | bit] = jnp.where(low, shift_groups(a, -bit), b)
    return v


def reduce_groups(vectors):
    v = list(vectors)
    grp = lane_groups(v[0].shape)
    low = (grp & 4) == 0
    v = [
        jnp.where(low, v[i], v[i + 4])
        + shift_groups(jnp.where(low, v[i + 4], v[i]), 4)
        for i in range(4)
    ]
    for bit in (2, 1):
        low = (grp & bit) == 0
        v = [
            jnp.where(low, v[i], v[i + bit])
            + jnp.where(low, shift_groups(v[i], -bit), shift_groups(v[i + bit], bit))
            for i in range(bit)
        ]
    return v[0]


def selection(n_seg, chunk, chans):
    wide = chans // TILE * n_seg * CC
    row = lax.broadcasted_iota(jnp.int32, (chans, wide), 0)
    col = lax.broadcasted_iota(jnp.int32, (chans, wide), 1)
    group = col // CC
    want = (
        group // n_seg * TILE
        + group % n_seg * (TILE // n_seg)
        + chunk * CC
        + col % CC
    )
    return (row == want).astype(jnp.bfloat16)


def pack_kernel(n_seg, chunk, x_ref, out_ref, buf_ref):
    n_pair = out_ref.shape[1]
    band = x_ref.shape[1] // n_pair
    sel = selection(n_seg, chunk, x_ref.shape[2])
    rows = band // GROUPS
    for p in range(n_pair):
        for ri in range(2):
            for part in range(sel.shape[1] // TILE):
                lanes = slice(part * TILE, (part + 1) * TILE)
                buf = buf_ref.at[p % 2, ri]
                buf[...] = jnp.dot(
                    x_ref[ri, p * band : (p + 1) * band, :],
                    sel[:, lanes],
                    preferred_element_type=jnp.float32,
                )
                v = [buf[pl.ds(fb, rows, stride=GROUPS), :] for fb in range(GROUPS)]
                v = transpose_groups(v)
                for g in range(GROUPS):
                    t, z = divmod(part * GROUPS + g, n_seg)
                    out_ref[z, p, t, ri] = v[g].astype(jnp.bfloat16)


def pack(x, chunk, n_seg, n_pair):
    _, freq, chans = x.shape
    band = freq // n_pair
    shape = (n_seg, n_pair, chans // TILE, 2, band // GROUPS, TILE)
    return pl.pallas_call(
        functools.partial(pack_kernel, n_seg, chunk),
        out_shape=jax.ShapeDtypeStruct(shape, jnp.bfloat16),
        grid=(2,),
        in_specs=[pl.BlockSpec((2, freq // 2, chans), lambda i: (0, i, 0))],
        out_specs=pl.BlockSpec(
            (n_seg, n_pair // 2) + shape[2:], lambda i: (0, i, 0, 0, 0, 0)
        ),
        scratch_shapes=[pltpu.VMEM((2, 2, band, TILE), jnp.float32)],
        name="pack",
        cost_estimate=SMALL,
    )(x)


def stack_kernel(n_seg, n_pair, most, me_ref, table_ref, spec_ref, *refs):
    outs, (sum_ref, big_ref) = refs[:-2], refs[-2:]
    rows = spec_ref.shape[3]
    inv = 1.0 / float(n_seg * n_seg)
    big_ref[...] = jnp.zeros_like(big_ref)
    for k in range(n_pair):
        owner = jnp.bitwise_xor(me_ref[1], k)
        count = table_ref[owner, 2 * most]

        def one(s, _):
            src = table_ref[owner, 2 * s]
            rcv = table_ref[owner, 2 * s + 1]
            lr = li = pr = pi = None
            for g in range(n_seg):
                a0 = spec_ref[g, src, 0].astype(jnp.float32)
                a1 = spec_ref[g, src, 1].astype(jnp.float32)
                b0 = spec_ref[g, rcv, 0].astype(jnp.float32)
                b1 = spec_ref[g, rcv, 1].astype(jnp.float32)
                cr = a0 * b0 + a1 * b1
                ci = a1 * b0 - a0 * b1
                m = lax.rsqrt(cr * cr + ci * ci + 1.0)
                if g == 0:
                    lr, li, pr, pi = cr, ci, cr * m, ci * m
                else:
                    lr, li, pr, pi = lr + cr, li + ci, pr + cr * m, pi + ci * m
            w = (pr * pr + pi * pi) * inv
            re, im = lr * w, li * w
            sum_ref[k, s, 0] = re
            sum_ref[k, s, 1] = im
            big = jnp.maximum(jnp.abs(re), jnp.abs(im))
            big_ref[...] = jnp.maximum(big_ref[...], big)
            return 0

        lax.fori_loop(0, count, one, 0)
    top = top_exponent(jnp.max(big_ref[...], keepdims=True))
    for k in range(n_pair):
        owner = jnp.bitwise_xor(me_ref[1], k)
        count = table_ref[owner, 2 * most]
        out_ref = outs[k // 2].at[k % 2]

        def code(s, _):
            at = pl.ds(pl.multiple_of(s * rows, rows), rows)
            out_ref[at, :] = encode(sum_ref[k, s, 0], sum_ref[k, s, 1], top)
            return 0

        def dead(s, _):
            at = pl.ds(pl.multiple_of(s * rows, rows), rows)
            out_ref[at, :] = jnp.full((rows, TILE), ZERO, jnp.int32)
            return 0

        lax.fori_loop(0, count, code, 0)
        lax.fori_loop(count, most, dead, 0)
        out_ref[most * rows :, :] = jnp.broadcast_to(top, (8, TILE)).astype(jnp.int32)


def stacks(me, table, spec, n_seg, n_pair, most):
    rows = spec.shape[3]
    shape = (2, most * rows + 8, TILE)
    smem = pl.BlockSpec(memory_space=pltpu.SMEM)
    vmem = pl.BlockSpec(memory_space=pltpu.VMEM)
    return pl.pallas_call(
        functools.partial(stack_kernel, n_seg, n_pair, most),
        out_shape=[jax.ShapeDtypeStruct(shape, jnp.int32)] * (n_pair // 2),
        in_specs=[smem, smem, vmem],
        out_specs=[vmem] * (n_pair // 2),
        scratch_shapes=[
            pltpu.VMEM((n_pair, most, 2, rows, TILE), jnp.float32),
            pltpu.VMEM((rows, TILE), jnp.float32),
        ],
        name="stack",
        compiler_params=pltpu.CompilerParams(vmem_limit_bytes=12 << 20),
        cost_estimate=SMALL,
    )(me, table, spec)


def dft_kernel(
    n_seg, n_pair, most, me_ref, w_ref, phase_ref, tables_ref, *refs
):
    ins, outs = refs[:n_pair], refs[n_pair : n_pair + n_seg]
    t_ref, sem, s32, shi, slo, y, zhi, zlo, sums, parts = refs[n_pair + n_seg :]
    copy = pltpu.make_async_copy(
        tables_ref.at[pl.ds(0, t_ref.shape[0])], t_ref, sem.at[0]
    )
    copy.start()
    rows = (ins[0].shape[1] - 8) // most
    half_h = w_ref.shape[1] // 2
    whi_ref, wlo_ref = w_ref.at[: 2 * half_h], w_ref.at[2 * half_h :]
    wide = most * TILE
    for k in range(n_pair):
        band = jnp.bitwise_xor(me_ref[1], k)
        src = ins[k % 2 * (n_pair // 2) + k // 2].at[k % 2]
        at = pl.ds(pl.multiple_of(band * rows, rows), rows)
        top = src[most * rows : most * rows + 1, :].astype(jnp.float32)
        for s in range(most):
            pair = decode(src[s * rows : (s + 1) * rows, :], top)
            for ri in range(2):
                s32[ri, at, s * TILE : (s + 1) * TILE] = pair[ri]
    for ri in range(2):
        full = s32[ri]
        hi = full.astype(jnp.bfloat16)
        lo = (full - hi.astype(jnp.float32)).astype(jnp.bfloat16)
        own = slice(ri * wide, (ri + 1) * wide)
        other = slice((1 - ri) * wide, (2 - ri) * wide)
        for to, part in ((shi, hi), (slo, lo)):
            to[:half_h, own] = part
            to[half_h:, other] = part if ri == 0 else -part
    for ri in range(2):
        n = slice(ri * wide, (ri + 1) * wide)
        y[ri] = (
            jnp.dot(wlo_ref[...], shi[:, n], preferred_element_type=jnp.float32)
            + jnp.dot(whi_ref[...], slo[:, n], preferred_element_type=jnp.float32)
        ) + jnp.dot(whi_ref[...], shi[:, n], preferred_element_type=jnp.float32)
    period = y.shape[1]
    step_rows = FINE
    fine_c, fine_d = phase_ref[:FINE, :TILE], phase_ref[:FINE, TILE:]
    for b in range(period // step_rows):
        at = slice(b * step_rows, (b + 1) * step_rows)
        big_c = phase_ref[FINE + b : FINE + b + 1, :TILE]
        big_d = phase_ref[FINE + b : FINE + b + 1, TILE:]
        c = big_c * fine_c - big_d * fine_d
        d = big_d * fine_c + big_c * fine_d
        for s in range(most):
            lanes = slice(s * TILE, (s + 1) * TILE)
            yr = y[0, at, lanes]
            yi = y[1, at, lanes]
            for ri, z in enumerate((c * yr - d * yi, d * yr + c * yi)):
                to = slice((ri * most + s) * TILE, (ri * most + s + 1) * TILE)
                hi = z.astype(jnp.bfloat16)
                zhi[at, to] = hi
                zlo[at, to] = (z - hi.astype(jnp.float32)).astype(jnp.bfloat16)
    copy.wait()
    t = t_ref[...]
    sums[...] = jnp.dot(zlo[...], t, preferred_element_type=jnp.float32) + jnp.dot(
        zhi[...], t, preferred_element_type=jnp.float32
    )
    half = parts.shape[1]
    big = None
    first = lax.broadcasted_iota(jnp.int32, (half, TILE), 1) < TILE // 2
    for dest in range(n_seg):
        lag = dest * 2 * half
        r, l0 = lag // period, lag % period
        col = slice(r // 2 * TILE, (r // 2 + 1) * TILE)
        low = sums[l0 : l0 + half, col]
        high = sums[l0 + half : l0 + 2 * half, col]
        if r % 2 == 0:
            high = pltpu.roll(high, TILE // 2, 1)
        else:
            low = pltpu.roll(low, TILE // 2, 1)
        part = jnp.where(first, low, high)
        parts[dest] = part
        part = jnp.max(jnp.abs(part), axis=0, keepdims=True)
        big = part if big is None else jnp.maximum(big, part)
    top = top_exponent(jnp.max(big, keepdims=True))
    for k in range(n_seg):
        part = parts[jnp.bitwise_xor(me_ref[0], k)]
        outs[k][: half // 2, :] = encode(part[: half // 2], part[half // 2 :], top)
        outs[k][half // 2 :, :] = jnp.broadcast_to(top, (8, TILE)).astype(jnp.int32)


def sums_kernel(most, turns, shift, out_ref, t_ref, sem):
    shape = (most * TILE, turns * most * CC)
    row = lax.broadcasted_iota(jnp.int32, shape, 0)
    col = lax.broadcasted_iota(jnp.int32, shape, 1)
    same = (row // TILE == col // CC % most) & (row % CC == col % CC)
    fb = row // CC % GROUPS
    eighths = (col // (most * CC) - shift) * fb
    one = jnp.where(fb % 2 == 0, 1.0, ODD)
    for ri in range(2):
        e = jnp.bitwise_and(eighths + 2 * ri, 7)
        size = jnp.where(e % 4 == 2, 0.0, jnp.where(e % 2 == 0, one, ODD_DIAGONAL))
        t = jnp.where(same, jnp.where((e > 2) & (e < 6), -size, size), 0.0)
        t_ref[ri * most * TILE : (ri + 1) * most * TILE, :] = t.astype(jnp.bfloat16)
    copy = pltpu.make_async_copy(
        t_ref, out_ref.at[pl.ds(0, t_ref.shape[0])], sem.at[0]
    )
    copy.start()
    copy.wait()


def make_sums(freq, most):
    period = 2 * (freq // GROUPS)
    turns = LAG // period
    width = turns * most * CC
    return pl.pallas_call(
        functools.partial(sums_kernel, most, turns, LAG // 2 // period),
        out_shape=jax.ShapeDtypeStruct((96 << 10, width), jnp.bfloat16),
        out_specs=pl.BlockSpec(memory_space=pltpu.HBM),
        scratch_shapes=[
            pltpu.VMEM((2 * most * TILE, width), jnp.bfloat16),
            pltpu.SemaphoreType.DMA((1,)),
        ],
        name="sums",
        cost_estimate=SMALL,
    )()


def make_tables(freq):
    h = freq // GROUPS
    period = 2 * h
    angle = np.arange(period)[:, None] * np.arange(h)[None, :] % period
    angle = angle * (2.0 * math.pi / period)
    w = np.concatenate([np.cos(angle), np.sin(angle)], 1).astype(np.float32)
    whi = w.astype(jnp.bfloat16)
    wlo = (w - whi.astype(np.float32)).astype(jnp.bfloat16)
    fb = np.arange(TILE) // CC
    scale = np.where(fb % 2 == 0, 1.0, 1.0 / ODD) / math.sqrt(freq)
    parts = []
    for at, gain in ((np.arange(FINE), scale), (np.arange(0, period, FINE), 1.0)):
        angle = (at[:, None] * fb[None, :] % (2 * freq)) * (math.pi / freq)
        parts.append(np.concatenate([np.cos(angle) * gain, np.sin(angle) * gain], 1))
    phase = np.concatenate(parts).astype(np.float32)
    return [jnp.asarray(c) for c in (np.concatenate([whi, wlo]), phase)]


def dft(me, tables, blocks, freq, n_seg, n_pair, most):
    period = 2 * (freq // GROUPS)
    smem = pl.BlockSpec(memory_space=pltpu.SMEM)
    vmem = pl.BlockSpec(memory_space=pltpu.VMEM)
    half = LAG // n_seg // 2
    wide = most * TILE
    return pl.pallas_call(
        functools.partial(dft_kernel, n_seg, n_pair, most),
        out_shape=[jax.ShapeDtypeStruct((half // 2 + 8, TILE), jnp.int32)] * n_seg,
        in_specs=[smem, vmem, vmem, pl.BlockSpec(memory_space=pltpu.HBM)]
        + [vmem] * len(blocks),
        out_specs=[vmem] * n_seg,
        scratch_shapes=[
            pltpu.VMEM((2 * wide, LAG // period * most * CC), jnp.bfloat16),
            pltpu.SemaphoreType.DMA((1,)),
            pltpu.VMEM((2, period // 2, wide), jnp.float32),
            pltpu.VMEM((period, 2 * wide), jnp.bfloat16),
            pltpu.VMEM((period, 2 * wide), jnp.bfloat16),
            pltpu.VMEM((2, period, wide), jnp.float32),
            pltpu.VMEM((period, 2 * wide), jnp.bfloat16),
            pltpu.VMEM((period, 2 * wide), jnp.bfloat16),
            pltpu.VMEM((period, LAG // period * most * CC), jnp.float32),
            pltpu.VMEM((n_seg, half, TILE), jnp.float32),
        ],
        name="dft",
        compiler_params=pltpu.CompilerParams(vmem_limit_bytes=24 << 20),
        cost_estimate=SMALL,
    )(me, *tables, *blocks)


def unpack_kernel(n_seg, chunks, most, me_ref, *refs):
    ins = refs[: n_seg * chunks]
    out_ref, buf = refs[n_seg * chunks :]
    half = buf.shape[1]

    @pl.when(pl.program_id(0) == 0)
    def _():
        for k in range(n_seg):
            z = jnp.bitwise_xor(me_ref[0], k)
            for ch in range(chunks):
                src = ins[ch * n_seg + n_seg - 1 - k]
                top = src[half // 2 : half // 2 + 1, :].astype(jnp.float32)
                low, high = decode(src[: half // 2, :], top)
                buf[z * chunks + ch, : half // 2] = low
                buf[z * chunks + ch, half // 2 :] = high

    step_rows = 16
    block = out_ref.shape[1]
    for b in range(block // step_rows):
        at = pl.multiple_of(pl.program_id(0) * block + b * step_rows, step_rows)
        v = transpose_groups([buf[i, pl.ds(at, step_rows), :] for i in range(GROUPS)])
        for h in range(2):
            for s in range(most):
                out_ref[h, b * step_rows : (b + 1) * step_rows, s, :] = v[h * most + s]


def unpack(me, parts, n_seg, chunks, most):
    half = 2 * (parts[0].shape[0] - 8)
    steps = 4
    smem = pl.BlockSpec(memory_space=pltpu.SMEM)
    whole = pl.BlockSpec(parts[0].shape, lambda b: (0, 0))
    out = pl.pallas_call(
        functools.partial(unpack_kernel, n_seg, chunks, most),
        out_shape=jax.ShapeDtypeStruct((2, half, most, TILE), jnp.float32),
        grid=(steps,),
        in_specs=[smem] + [whole] * len(parts),
        out_specs=pl.BlockSpec((2, half // steps, most, TILE), lambda b: (0, b, 0, 0)),
        scratch_shapes=[pltpu.VMEM((GROUPS, half, TILE), jnp.float32)],
        name="unpack",
        compiler_params=pltpu.CompilerParams(vmem_limit_bytes=12 << 20),
        cost_estimate=SMALL,
    )(me, *parts)
    return out.reshape(2 * half, most, TILE)


def exchange(blocks, axis, size):
    got = {
        k: lax.ppermute(blocks[k], axis, [(i, i ^ k) for i in range(size)])
        for k in reversed(range(1, size))
    }
    return [blocks[0]] + [got[k] for k in range(1, size)]


def exchange_plane(blocks, n_pair, between=None):
    direct = [blocks[0]] + [
        lax.ppermute(blocks[k], "pair", [(i, i ^ (2 * k)) for i in range(n_pair)])
        for k in range(1, n_pair // 2)
    ]
    if between is not None:
        direct, _ = lax.optimization_barrier((direct, between))
    swap = [(i, i ^ 1) for i in range(n_pair)]
    return direct + [lax.ppermute(d, "pair", swap) for d in direct]


def body(spectra, pair_lists, pair_counts):
    n_pair = lax.axis_size("pair")
    n_seg = lax.axis_size("seg")
    freq = spectra.shape[2]
    most = pair_lists.shape[0]
    tiles = spectra.shape[3] // TILE
    chunks = GROUPS // n_seg
    rows = freq // n_pair // GROUPS
    me = jnp.stack([lax.axis_index("seg"), lax.axis_index("pair")]).astype(jnp.int32)
    x = spectra.reshape(2, freq, spectra.shape[3])
    lists = jnp.concatenate([pair_lists.reshape(-1), pair_counts])
    sums = make_sums(freq, most)
    tables = make_tables(freq) + [sums]
    packed = [pack(x, chunk, n_seg, n_pair) for chunk in range(chunks)]
    lists, packed[-1] = lax.optimization_barrier((lists, packed[-1]))
    table = lax.all_gather(lists, "pair", axis=0)
    if chunks > 1:
        table, packed[1], _ = lax.optimization_barrier((table, packed[1], sums))
    done, parts = [], []
    lags = None
    for sent in packed:
        got = lax.all_to_all(
            sent.reshape(n_seg * n_pair, tiles, 2, rows, TILE),
            ("seg", "pair"),
            split_axis=0,
            concat_axis=0,
            tiled=True,
        )
        if lags is not None:
            got, _ = lax.optimization_barrier((got, lags))
        spec = got.reshape(n_seg, n_pair * tiles, 2, rows, TILE)
        stack = stacks(me, table, spec, n_seg, n_pair, most)
        blocks = exchange_plane(stack, n_pair, done[2:0:-1] or None)
        lags = dft(me, tables, blocks, freq, n_seg, n_pair, most)
        done = exchange(lags, "seg", n_seg)
        parts += done[::-1]
    return unpack(me, parts, n_seg, chunks, most)


def solution(mesh):
    return jax.shard_map(
        body,
        mesh=mesh,
        in_specs=(P("seg", None, None, "pair"), P("pair", None), P("pair")),
        out_specs=P("seg", "pair", None),
        check_vma=False,
    )
```

```python
import functools
import math

import jax
import jax.numpy as jnp
import numpy as np
from jax import lax
from jax.experimental import pallas as pl
from jax.experimental.pallas import tpu as pltpu
from jax.sharding import PartitionSpec as P

TILE = 128
LAG = 2048
GROUPS = 8
SMALL = pl.CostEstimate(flops=1, bytes_accessed=1, transcendentals=0)
CC = TILE // GROUPS


def lane_groups(shape):
    return lax.broadcasted_iota(jnp.int32, shape, len(shape) - 1) // CC


def shift_groups(x, by):
    return pltpu.roll(x, (by * CC) % TILE, x.ndim - 1)


def top_exponent(largest):
    return jnp.maximum(jnp.floor(jnp.log2(jnp.maximum(largest, 1e-36))), -90.0)


def encode(a, b, top):
    m = jnp.maximum(jnp.maximum(jnp.abs(a), jnp.abs(b)), 1e-36)
    e = jnp.minimum(jnp.maximum(jnp.floor(jnp.log2(m)), top - 15.0), top)
    s = jnp.exp2(12.0 - e)
    qa, qb = (
        jnp.clip(jnp.floor(x * s + 0.5), -8191.0, 8191.0).astype(jnp.int32) + 8192
        for x in (a, b)
    )
    return ((e - (top - 15.0)).astype(jnp.int32) << 28) | (qa << 14) | qb


ZERO = (8192 << 14) | 8192


def decode(code, top):
    s = jnp.exp2(((code >> 28) & 15).astype(jnp.float32) + (top - 27.0))
    a, b = (
        ((q & 16383) - 8192).astype(jnp.float32) * s for q in (code >> 14, code)
    )
    return a, b


FINE = 64
ODD = 239.0 / 256.0
ODD_DIAGONAL = 169.0 / 256.0


def transpose_groups(vectors):
    v = list(vectors)
    grp = lane_groups(v[0].shape)
    for bit in (4, 2, 1):
        low = (grp & bit) == 0
        for i in range(GROUPS):
            if i & bit:
                continue
            a, b = v[i], v[i | bit]
            v[i] = jnp.where(low, a, shift_groups(b, bit))
            v[i | bit] = jnp.where(low, shift_groups(a, -bit), b)
    return v


def reduce_groups(vectors):
    v = list(vectors)
    grp = lane_groups(v[0].shape)
    low = (grp & 4) == 0
    v = [
        jnp.where(low, v[i], v[i + 4])
        + shift_groups(jnp.where(low, v[i + 4], v[i]), 4)
        for i in range(4)
    ]
    for bit in (2, 1):
        low = (grp & bit) == 0
        v = [
            jnp.where(low, v[i], v[i + bit])
            + jnp.where(low, shift_groups(v[i], -bit), shift_groups(v[i + bit], bit))
            for i in range(bit)
        ]
    return v[0]


def selection(n_seg, chunk, chans):
    wide = chans // TILE * n_seg * CC
    row = lax.broadcasted_iota(jnp.int32, (chans, wide), 0)
    col = lax.broadcasted_iota(jnp.int32, (chans, wide), 1)
    group = col // CC
    want = (
        group // n_seg * TILE
        + group % n_seg * (TILE // n_seg)
        + chunk * CC
        + col % CC
    )
    return (row == want).astype(jnp.bfloat16)


def pack_kernel(n_seg, chunk, x_ref, out_ref, buf_ref):
    n_pair = out_ref.shape[1]
    band = x_ref.shape[1] // n_pair
    sel = selection(n_seg, chunk, x_ref.shape[2])
    rows = band // GROUPS
    for p in range(n_pair):
        for ri in range(2):
            for part in range(sel.shape[1] // TILE):
                lanes = slice(part * TILE, (part + 1) * TILE)
                buf = buf_ref.at[p % 2, ri]
                buf[...] = jnp.dot(
                    x_ref[ri, p * band : (p + 1) * band, :],
                    sel[:, lanes],
                    preferred_element_type=jnp.float32,
                )
                v = [buf[pl.ds(fb, rows, stride=GROUPS), :] for fb in range(GROUPS)]
                v = transpose_groups(v)
                for g in range(GROUPS):
                    t, z = divmod(part * GROUPS + g, n_seg)
                    out_ref[z, p, t, ri] = v[g].astype(jnp.bfloat16)


def pack(x, chunk, n_seg, n_pair):
    _, freq, chans = x.shape
    band = freq // n_pair
    shape = (n_seg, n_pair, chans // TILE, 2, band // GROUPS, TILE)
    return pl.pallas_call(
        functools.partial(pack_kernel, n_seg, chunk),
        out_shape=jax.ShapeDtypeStruct(shape, jnp.bfloat16),
        grid=(2,),
        in_specs=[pl.BlockSpec((2, freq // 2, chans), lambda i: (0, i, 0))],
        out_specs=pl.BlockSpec(
            (n_seg, n_pair // 2) + shape[2:], lambda i: (0, i, 0, 0, 0, 0)
        ),
        scratch_shapes=[pltpu.VMEM((2, 2, band, TILE), jnp.float32)],
        name="pack",
        cost_estimate=SMALL,
    )(x)


def stack_kernel(n_seg, n_pair, most, me_ref, table_ref, spec_ref, *refs):
    outs, (sum_ref, big_ref) = refs[:-2], refs[-2:]
    rows = spec_ref.shape[3]
    inv = 1.0 / float(n_seg * n_seg)
    big_ref[...] = jnp.zeros_like(big_ref)
    for k in range(n_pair):
        owner = jnp.bitwise_xor(me_ref[1], k)
        count = table_ref[owner, 2 * most]

        def one(s, _):
            src = table_ref[owner, 2 * s]
            rcv = table_ref[owner, 2 * s + 1]
            lr = li = pr = pi = None
            for g in range(n_seg):
                a0 = spec_ref[g, src, 0].astype(jnp.float32)
                a1 = spec_ref[g, src, 1].astype(jnp.float32)
                b0 = spec_ref[g, rcv, 0].astype(jnp.float32)
                b1 = spec_ref[g, rcv, 1].astype(jnp.float32)
                cr = a0 * b0 + a1 * b1
                ci = a1 * b0 - a0 * b1
                m = lax.rsqrt(cr * cr + ci * ci + 1.0)
                if g == 0:
                    lr, li, pr, pi = cr, ci, cr * m, ci * m
                else:
                    lr, li, pr, pi = lr + cr, li + ci, pr + cr * m, pi + ci * m
            w = (pr * pr + pi * pi) * inv
            re, im = lr * w, li * w
            sum_ref[k, s, 0] = re
            sum_ref[k, s, 1] = im
            big = jnp.maximum(jnp.abs(re), jnp.abs(im))
            big_ref[...] = jnp.maximum(big_ref[...], big)
            return 0

        lax.fori_loop(0, count, one, 0)
    top = top_exponent(jnp.max(big_ref[...], keepdims=True))
    for k in range(n_pair):
        owner = jnp.bitwise_xor(me_ref[1], k)
        count = table_ref[owner, 2 * most]
        out_ref = outs[k // 2].at[k % 2]

        def code(s, _):
            at = pl.ds(pl.multiple_of(s * rows, rows), rows)
            out_ref[at, :] = encode(sum_ref[k, s, 0], sum_ref[k, s, 1], top)
            return 0

        def dead(s, _):
            at = pl.ds(pl.multiple_of(s * rows, rows), rows)
            out_ref[at, :] = jnp.full((rows, TILE), ZERO, jnp.int32)
            return 0

        lax.fori_loop(0, count, code, 0)
        lax.fori_loop(count, most, dead, 0)
        out_ref[most * rows :, :] = jnp.broadcast_to(top, (8, TILE)).astype(jnp.int32)


def stacks(me, table, spec, n_seg, n_pair, most):
    rows = spec.shape[3]
    shape = (2, most * rows + 8, TILE)
    smem = pl.BlockSpec(memory_space=pltpu.SMEM)
    vmem = pl.BlockSpec(memory_space=pltpu.VMEM)
    return pl.pallas_call(
        functools.partial(stack_kernel, n_seg, n_pair, most),
        out_shape=[jax.ShapeDtypeStruct(shape, jnp.int32)] * (n_pair // 2),
        in_specs=[smem, smem, vmem],
        out_specs=[vmem] * (n_pair // 2),
        scratch_shapes=[
            pltpu.VMEM((n_pair, most, 2, rows, TILE), jnp.float32),
            pltpu.VMEM((rows, TILE), jnp.float32),
        ],
        name="stack",
        compiler_params=pltpu.CompilerParams(vmem_limit_bytes=12 << 20),
        cost_estimate=SMALL,
    )(me, table, spec)


def dft_kernel(
    n_seg, n_pair, most, me_ref, w_ref, phase_ref, tables_ref, *refs
):
    ins, outs = refs[:n_pair], refs[n_pair : n_pair + n_seg]
    t_ref, sem, s32, shi, slo, y, zhi, zlo, sums, parts = refs[n_pair + n_seg :]
    copy = pltpu.make_async_copy(
        tables_ref.at[pl.ds(0, t_ref.shape[0])], t_ref, sem.at[0]
    )
    copy.start()
    rows = (ins[0].shape[1] - 8) // most
    half_h = w_ref.shape[1] // 2
    whi_ref, wlo_ref = w_ref.at[: 2 * half_h], w_ref.at[2 * half_h :]
    wide = most * TILE
    for k in range(n_pair):
        band = jnp.bitwise_xor(me_ref[1], k)
        src = ins[k % 2 * (n_pair // 2) + k // 2].at[k % 2]
        at = pl.ds(pl.multiple_of(band * rows, rows), rows)
        top = src[most * rows : most * rows + 1, :].astype(jnp.float32)
        for s in range(most):
            pair = decode(src[s * rows : (s + 1) * rows, :], top)
            for ri in range(2):
                s32[ri, at, s * TILE : (s + 1) * TILE] = pair[ri]
    for ri in range(2):
        full = s32[ri]
        hi = full.astype(jnp.bfloat16)
        lo = (full - hi.astype(jnp.float32)).astype(jnp.bfloat16)
        own = slice(ri * wide, (ri + 1) * wide)
        other = slice((1 - ri) * wide, (2 - ri) * wide)
        for to, part in ((shi, hi), (slo, lo)):
            to[:half_h, own] = part
            to[half_h:, other] = part if ri == 0 else -part
    for ri in range(2):
        n = slice(ri * wide, (ri + 1) * wide)
        y[ri] = (
            jnp.dot(wlo_ref[...], shi[:, n], preferred_element_type=jnp.float32)
            + jnp.dot(whi_ref[...], slo[:, n], preferred_element_type=jnp.float32)
        ) + jnp.dot(whi_ref[...], shi[:, n], preferred_element_type=jnp.float32)
    period = y.shape[1]
    step_rows = FINE
    fine_c, fine_d = phase_ref[:FINE, :TILE], phase_ref[:FINE, TILE:]
    for b in range(period // step_rows):
        at = slice(b * step_rows, (b + 1) * step_rows)
        big_c = phase_ref[FINE + b : FINE + b + 1, :TILE]
        big_d = phase_ref[FINE + b : FINE + b + 1, TILE:]
        c = big_c * fine_c - big_d * fine_d
        d = big_d * fine_c + big_c * fine_d
        for s in range(most):
            lanes = slice(s * TILE, (s + 1) * TILE)
            yr = y[0, at, lanes]
            yi = y[1, at, lanes]
            for ri, z in enumerate((c * yr - d * yi, d * yr + c * yi)):
                to = slice((ri * most + s) * TILE, (ri * most + s + 1) * TILE)
                hi = z.astype(jnp.bfloat16)
                zhi[at, to] = hi
                zlo[at, to] = (z - hi.astype(jnp.float32)).astype(jnp.bfloat16)
    copy.wait()
    t = t_ref[...]
    sums[...] = jnp.dot(zlo[...], t, preferred_element_type=jnp.float32) + jnp.dot(
        zhi[...], t, preferred_element_type=jnp.float32
    )
    half = parts.shape[1]
    big = None
    first = lax.broadcasted_iota(jnp.int32, (half, TILE), 1) < TILE // 2
    for dest in range(n_seg):
        lag = dest * 2 * half
        r, l0 = lag // period, lag % period
        col = slice(r // 2 * TILE, (r // 2 + 1) * TILE)
        low = sums[l0 : l0 + half, col]
        high = sums[l0 + half : l0 + 2 * half, col]
        if r % 2 == 0:
            high = pltpu.roll(high, TILE // 2, 1)
        else:
            low = pltpu.roll(low, TILE // 2, 1)
        part = jnp.where(first, low, high)
        parts[dest] = part
        part = jnp.max(jnp.abs(part), axis=0, keepdims=True)
        big = part if big is None else jnp.maximum(big, part)
    top = top_exponent(jnp.max(big, keepdims=True))
    for k in range(n_seg):
        part = parts[jnp.bitwise_xor(me_ref[0], k)]
        outs[k][: half // 2, :] = encode(part[: half // 2], part[half // 2 :], top)
        outs[k][half // 2 :, :] = jnp.broadcast_to(top, (8, TILE)).astype(jnp.int32)


def sums_kernel(most, turns, shift, out_ref, t_ref, sem):
    shape = (most * TILE, turns * most * CC)
    row = lax.broadcasted_iota(jnp.int32, shape, 0)
    col = lax.broadcasted_iota(jnp.int32, shape, 1)
    same = (row // TILE == col // CC % most) & (row % CC == col % CC)
    fb = row // CC % GROUPS
    eighths = (col // (most * CC) - shift) * fb
    one = jnp.where(fb % 2 == 0, 1.0, ODD)
    for ri in range(2):
        e = jnp.bitwise_and(eighths + 2 * ri, 7)
        size = jnp.where(e % 4 == 2, 0.0, jnp.where(e % 2 == 0, one, ODD_DIAGONAL))
        t = jnp.where(same, jnp.where((e > 2) & (e < 6), -size, size), 0.0)
        t_ref[ri * most * TILE : (ri + 1) * most * TILE, :] = t.astype(jnp.bfloat16)
    copy = pltpu.make_async_copy(
        t_ref, out_ref.at[pl.ds(0, t_ref.shape[0])], sem.at[0]
    )
    copy.start()
    copy.wait()


def make_sums(freq, most):
    period = 2 * (freq // GROUPS)
    turns = LAG // period
    width = turns * most * CC
    return pl.pallas_call(
        functools.partial(sums_kernel, most, turns, LAG // 2 // period),
        out_shape=jax.ShapeDtypeStruct((96 << 10, width), jnp.bfloat16),
        out_specs=pl.BlockSpec(memory_space=pltpu.HBM),
        scratch_shapes=[
            pltpu.VMEM((2 * most * TILE, width), jnp.bfloat16),
            pltpu.SemaphoreType.DMA((1,)),
        ],
        name="sums",
        cost_estimate=SMALL,
    )()


def make_tables(freq):
    h = freq // GROUPS
    period = 2 * h
    angle = np.arange(period)[:, None] * np.arange(h)[None, :] % period
    angle = angle * (2.0 * math.pi / period)
    w = np.concatenate([np.cos(angle), np.sin(angle)], 1).astype(np.float32)
    whi = w.astype(jnp.bfloat16)
    wlo = (w - whi.astype(np.float32)).astype(jnp.bfloat16)
    fb = np.arange(TILE) // CC
    scale = np.where(fb % 2 == 0, 1.0, 1.0 / ODD) / math.sqrt(freq)
    parts = []
    for at, gain in ((np.arange(FINE), scale), (np.arange(0, period, FINE), 1.0)):
        angle = (at[:, None] * fb[None, :] % (2 * freq)) * (math.pi / freq)
        parts.append(np.concatenate([np.cos(angle) * gain, np.sin(angle) * gain], 1))
    phase = np.concatenate(parts).astype(np.float32)
    return [jnp.asarray(c) for c in (np.concatenate([whi, wlo]), phase)]


def dft(me, tables, blocks, freq, n_seg, n_pair, most):
    period = 2 * (freq // GROUPS)
    smem = pl.BlockSpec(memory_space=pltpu.SMEM)
    vmem = pl.BlockSpec(memory_space=pltpu.VMEM)
    half = LAG // n_seg // 2
    wide = most * TILE
    return pl.pallas_call(
        functools.partial(dft_kernel, n_seg, n_pair, most),
        out_shape=[jax.ShapeDtypeStruct((half // 2 + 8, TILE), jnp.int32)] * n_seg,
        in_specs=[smem, vmem, vmem, pl.BlockSpec(memory_space=pltpu.HBM)]
        + [vmem] * len(blocks),
        out_specs=[vmem] * n_seg,
        scratch_shapes=[
            pltpu.VMEM((2 * wide, LAG // period * most * CC), jnp.bfloat16),
            pltpu.SemaphoreType.DMA((1,)),
            pltpu.VMEM((2, period // 2, wide), jnp.float32),
            pltpu.VMEM((period, 2 * wide), jnp.bfloat16),
            pltpu.VMEM((period, 2 * wide), jnp.bfloat16),
            pltpu.VMEM((2, period, wide), jnp.float32),
            pltpu.VMEM((period, 2 * wide), jnp.bfloat16),
            pltpu.VMEM((period, 2 * wide), jnp.bfloat16),
            pltpu.VMEM((period, LAG // period * most * CC), jnp.float32),
            pltpu.VMEM((n_seg, half, TILE), jnp.float32),
        ],
        name="dft",
        compiler_params=pltpu.CompilerParams(vmem_limit_bytes=24 << 20),
        cost_estimate=SMALL,
    )(me, *tables, *blocks)


def unpack_kernel(n_seg, chunks, most, me_ref, *refs):
    ins = refs[: n_seg * chunks]
    out_ref, buf = refs[n_seg * chunks :]
    half = buf.shape[1]

    @pl.when(pl.program_id(0) == 0)
    def _():
        for k in range(n_seg):
            z = jnp.bitwise_xor(me_ref[0], k)
            for ch in range(chunks):
                src = ins[ch * n_seg + n_seg - 1 - k]
                top = src[half // 2 : half // 2 + 1, :].astype(jnp.float32)
                low, high = decode(src[: half // 2, :], top)
                buf[z * chunks + ch, : half // 2] = low
                buf[z * chunks + ch, half // 2 :] = high

    step_rows = 16
    block = out_ref.shape[1]
    for b in range(block // step_rows):
        at = pl.multiple_of(pl.program_id(0) * block + b * step_rows, step_rows)
        v = transpose_groups([buf[i, pl.ds(at, step_rows), :] for i in range(GROUPS)])
        for h in range(2):
            for s in range(most):
                out_ref[h, b * step_rows : (b + 1) * step_rows, s, :] = v[h * most + s]


def unpack(me, parts, n_seg, chunks, most):
    half = 2 * (parts[0].shape[0] - 8)
    steps = 4
    smem = pl.BlockSpec(memory_space=pltpu.SMEM)
    whole = pl.BlockSpec(parts[0].shape, lambda b: (0, 0))
    out = pl.pallas_call(
        functools.partial(unpack_kernel, n_seg, chunks, most),
        out_shape=jax.ShapeDtypeStruct((2, half, most, TILE), jnp.float32),
        grid=(steps,),
        in_specs=[smem] + [whole] * len(parts),
        out_specs=pl.BlockSpec((2, half // steps, most, TILE), lambda b: (0, b, 0, 0)),
        scratch_shapes=[pltpu.VMEM((GROUPS, half, TILE), jnp.float32)],
        name="unpack",
        compiler_params=pltpu.CompilerParams(vmem_limit_bytes=12 << 20),
        cost_estimate=SMALL,
    )(me, *parts)
    return out.reshape(2 * half, most, TILE)


def exchange(blocks, axis, size):
    got = {
        k: lax.ppermute(blocks[k], axis, [(i, i ^ k) for i in range(size)])
        for k in reversed(range(1, size))
    }
    return [blocks[0]] + [got[k] for k in range(1, size)]


def exchange_plane(blocks, n_pair, between=None):
    direct = [blocks[0]] + [
        lax.ppermute(blocks[k], "pair", [(i, i ^ (2 * k)) for i in range(n_pair)])
        for k in range(1, n_pair // 2)
    ]
    if between is not None:
        direct, _ = lax.optimization_barrier((direct, between))
    swap = [(i, i ^ 1) for i in range(n_pair)]
    return direct + [lax.ppermute(d, "pair", swap) for d in direct]


def body(spectra, pair_lists, pair_counts):
    n_pair = lax.axis_size("pair")
    n_seg = lax.axis_size("seg")
    freq = spectra.shape[2]
    most = pair_lists.shape[0]
    tiles = spectra.shape[3] // TILE
    chunks = GROUPS // n_seg
    rows = freq // n_pair // GROUPS
    me = jnp.stack([lax.axis_index("seg"), lax.axis_index("pair")]).astype(jnp.int32)
    x = spectra.reshape(2, freq, spectra.shape[3])
    lists = jnp.concatenate([pair_lists.reshape(-1), pair_counts])
    sums = make_sums(freq, most)
    tables = make_tables(freq) + [sums]
    packed = [pack(x, chunk, n_seg, n_pair) for chunk in range(chunks)]
    lists, packed[-1] = lax.optimization_barrier((lists, packed[-1]))
    table = lax.all_gather(lists, "pair", axis=0)
    if chunks > 1:
        table, packed[1], _ = lax.optimization_barrier((table, packed[1], sums))
    done, parts = [], []
    lags = None
    for sent in packed:
        got = lax.all_to_all(
            sent.reshape(n_seg * n_pair, tiles, 2, rows, TILE),
            ("seg", "pair"),
            split_axis=0,
            concat_axis=0,
            tiled=True,
        )
        if lags is not None:
            got, _ = lax.optimization_barrier((got, lags))
        spec = got.reshape(n_seg, n_pair * tiles, 2, rows, TILE)
        stack = stacks(me, table, spec, n_seg, n_pair, most)
        blocks = exchange_plane(stack, n_pair, done[:1:-1] or None)
        lags = dft(me, tables, blocks, freq, n_seg, n_pair, most)
        done = exchange(lags, "seg", n_seg)
        parts += done[::-1]
    return unpack(me, parts, n_seg, chunks, most)


def solution(mesh):
    return jax.shard_map(
        body,
        mesh=mesh,
        in_specs=(P("seg", None, None, "pair"), P("pair", None), P("pair")),
        out_specs=P("seg", "pair", None),
        check_vma=False,
    )
```

```python
import functools
import math

import jax
import jax.numpy as jnp
import numpy as np
from jax import lax
from jax.experimental import pallas as pl
from jax.experimental.pallas import tpu as pltpu
from jax.sharding import PartitionSpec as P

TILE = 128
LAG = 2048
GROUPS = 8
SMALL = pl.CostEstimate(flops=1, bytes_accessed=1, transcendentals=0)
CC = TILE // GROUPS


def lane_groups(shape):
    return lax.broadcasted_iota(jnp.int32, shape, len(shape) - 1) // CC


def shift_groups(x, by):
    return pltpu.roll(x, (by * CC) % TILE, x.ndim - 1)


def top_exponent(largest):
    return jnp.maximum(jnp.floor(jnp.log2(jnp.maximum(largest, 1e-36))), -90.0)


def encode(a, b, top):
    m = jnp.maximum(jnp.maximum(jnp.abs(a), jnp.abs(b)), 1e-36)
    e = jnp.minimum(jnp.maximum(jnp.floor(jnp.log2(m)), top - 15.0), top)
    s = jnp.exp2(12.0 - e)
    qa, qb = (
        jnp.clip(jnp.floor(x * s + 0.5), -8191.0, 8191.0).astype(jnp.int32) + 8192
        for x in (a, b)
    )
    return ((e - (top - 15.0)).astype(jnp.int32) << 28) | (qa << 14) | qb


ZERO = (8192 << 14) | 8192


def decode(code, top):
    s = jnp.exp2(((code >> 28) & 15).astype(jnp.float32) + (top - 27.0))
    a, b = (
        ((q & 16383) - 8192).astype(jnp.float32) * s for q in (code >> 14, code)
    )
    return a, b


FINE = 64
ODD = 239.0 / 256.0
ODD_DIAGONAL = 169.0 / 256.0


def transpose_groups(vectors):
    v = list(vectors)
    grp = lane_groups(v[0].shape)
    for bit in (4, 2, 1):
        low = (grp & bit) == 0
        for i in range(GROUPS):
            if i & bit:
                continue
            a, b = v[i], v[i | bit]
            v[i] = jnp.where(low, a, shift_groups(b, bit))
            v[i | bit] = jnp.where(low, shift_groups(a, -bit), b)
    return v


def reduce_groups(vectors):
    v = list(vectors)
    grp = lane_groups(v[0].shape)
    low = (grp & 4) == 0
    v = [
        jnp.where(low, v[i], v[i + 4])
        + shift_groups(jnp.where(low, v[i + 4], v[i]), 4)
        for i in range(4)
    ]
    for bit in (2, 1):
        low = (grp & bit) == 0
        v = [
            jnp.where(low, v[i], v[i + bit])
            + jnp.where(low, shift_groups(v[i], -bit), shift_groups(v[i + bit], bit))
            for i in range(bit)
        ]
    return v[0]


def selection(n_seg, chunk, chans):
    wide = chans // TILE * n_seg * CC
    row = lax.broadcasted_iota(jnp.int32, (chans, wide), 0)
    col = lax.broadcasted_iota(jnp.int32, (chans, wide), 1)
    group = col // CC
    want = (
        group // n_seg * TILE
        + group % n_seg * (TILE // n_seg)
        + chunk * CC
        + col % CC
    )
    return (row == want).astype(jnp.bfloat16)


def pack_kernel(n_seg, chunk, x_ref, out_ref, buf_ref):
    n_pair = out_ref.shape[1]
    band = x_ref.shape[1] // n_pair
    sel = selection(n_seg, chunk, x_ref.shape[2])
    rows = band // GROUPS
    for p in range(n_pair):
        for ri in range(2):
            for part in range(sel.shape[1] // TILE):
                lanes = slice(part * TILE, (part + 1) * TILE)
                buf = buf_ref.at[p % 2, ri]
                buf[...] = jnp.dot(
                    x_ref[ri, p * band : (p + 1) * band, :],
                    sel[:, lanes],
                    preferred_element_type=jnp.float32,
                )
                v = [buf[pl.ds(fb, rows, stride=GROUPS), :] for fb in range(GROUPS)]
                v = transpose_groups(v)
                for g in range(GROUPS):
                    t, z = divmod(part * GROUPS + g, n_seg)
                    out_ref[z, p, t, ri] = v[g].astype(jnp.bfloat16)


def pack(x, chunk, n_seg, n_pair):
    _, freq, chans = x.shape
    band = freq // n_pair
    shape = (n_seg, n_pair, chans // TILE, 2, band // GROUPS, TILE)
    return pl.pallas_call(
        functools.partial(pack_kernel, n_seg, chunk),
        out_shape=jax.ShapeDtypeStruct(shape, jnp.bfloat16),
        grid=(2,),
        in_specs=[pl.BlockSpec((2, freq // 2, chans), lambda i: (0, i, 0))],
        out_specs=pl.BlockSpec(
            (n_seg, n_pair // 2) + shape[2:], lambda i: (0, i, 0, 0, 0, 0)
        ),
        scratch_shapes=[pltpu.VMEM((2, 2, band, TILE), jnp.float32)],
        name="pack",
        cost_estimate=SMALL,
    )(x)


def stack_kernel(n_seg, n_pair, most, me_ref, table_ref, spec_ref, *refs):
    outs, (sum_ref, big_ref) = refs[:-2], refs[-2:]
    rows = spec_ref.shape[3]
    inv = 1.0 / float(n_seg * n_seg)
    big_ref[...] = jnp.zeros_like(big_ref)
    for k in range(n_pair):
        owner = jnp.bitwise_xor(me_ref[1], k)
        count = table_ref[owner, 2 * most]

        def one(s, _):
            src = table_ref[owner, 2 * s]
            rcv = table_ref[owner, 2 * s + 1]
            lr = li = pr = pi = None
            for g in range(n_seg):
                a0 = spec_ref[g, src, 0].astype(jnp.float32)
                a1 = spec_ref[g, src, 1].astype(jnp.float32)
                b0 = spec_ref[g, rcv, 0].astype(jnp.float32)
                b1 = spec_ref[g, rcv, 1].astype(jnp.float32)
                cr = a0 * b0 + a1 * b1
                ci = a1 * b0 - a0 * b1
                m = lax.rsqrt(cr * cr + ci * ci + 1.0)
                if g == 0:
                    lr, li, pr, pi = cr, ci, cr * m, ci * m
                else:
                    lr, li, pr, pi = lr + cr, li + ci, pr + cr * m, pi + ci * m
            w = (pr * pr + pi * pi) * inv
            re, im = lr * w, li * w
            sum_ref[k, s, 0] = re
            sum_ref[k, s, 1] = im
            big = jnp.maximum(jnp.abs(re), jnp.abs(im))
            big_ref[...] = jnp.maximum(big_ref[...], big)
            return 0

        lax.fori_loop(0, count, one, 0)
    top = top_exponent(jnp.max(big_ref[...], keepdims=True))
    for k in range(n_pair):
        owner = jnp.bitwise_xor(me_ref[1], k)
        count = table_ref[owner, 2 * most]
        out_ref = outs[k // 2].at[k % 2]

        def code(s, _):
            at = pl.ds(pl.multiple_of(s * rows, rows), rows)
            out_ref[at, :] = encode(sum_ref[k, s, 0], sum_ref[k, s, 1], top)
            return 0

        def dead(s, _):
            at = pl.ds(pl.multiple_of(s * rows, rows), rows)
            out_ref[at, :] = jnp.full((rows, TILE), ZERO, jnp.int32)
            return 0

        lax.fori_loop(0, count, code, 0)
        lax.fori_loop(count, most, dead, 0)
        out_ref[most * rows :, :] = jnp.broadcast_to(top, (8, TILE)).astype(jnp.int32)


def stacks(me, table, spec, n_seg, n_pair, most):
    rows = spec.shape[3]
    shape = (2, most * rows + 8, TILE)
    smem = pl.BlockSpec(memory_space=pltpu.SMEM)
    vmem = pl.BlockSpec(memory_space=pltpu.VMEM)
    return pl.pallas_call(
        functools.partial(stack_kernel, n_seg, n_pair, most),
        out_shape=[jax.ShapeDtypeStruct(shape, jnp.int32)] * (n_pair // 2),
        in_specs=[smem, smem, vmem],
        out_specs=[vmem] * (n_pair // 2),
        scratch_shapes=[
            pltpu.VMEM((n_pair, most, 2, rows, TILE), jnp.float32),
            pltpu.VMEM((rows, TILE), jnp.float32),
        ],
        name="stack",
        compiler_params=pltpu.CompilerParams(vmem_limit_bytes=12 << 20),
        cost_estimate=SMALL,
    )(me, table, spec)


def dft_kernel(
    n_seg, n_pair, most, me_ref, w_ref, phase_ref, tables_ref, *refs
):
    ins, outs = refs[:n_pair], refs[n_pair : n_pair + n_seg]
    t_ref, sem, s32, shi, slo, y, zhi, zlo, sums, parts = refs[n_pair + n_seg :]
    copy = pltpu.make_async_copy(
        tables_ref.at[pl.ds(0, t_ref.shape[0])], t_ref, sem.at[0]
    )
    copy.start()
    rows = (ins[0].shape[1] - 8) // most
    half_h = w_ref.shape[1] // 2
    whi_ref, wlo_ref = w_ref.at[: 2 * half_h], w_ref.at[2 * half_h :]
    wide = most * TILE
    for k in range(n_pair):
        band = jnp.bitwise_xor(me_ref[1], k)
        src = ins[k % 2 * (n_pair // 2) + k // 2].at[k % 2]
        at = pl.ds(pl.multiple_of(band * rows, rows), rows)
        top = src[most * rows : most * rows + 1, :].astype(jnp.float32)
        for s in range(most):
            pair = decode(src[s * rows : (s + 1) * rows, :], top)
            for ri in range(2):
                s32[ri, at, s * TILE : (s + 1) * TILE] = pair[ri]
    for ri in range(2):
        full = s32[ri]
        hi = full.astype(jnp.bfloat16)
        lo = (full - hi.astype(jnp.float32)).astype(jnp.bfloat16)
        own = slice(ri * wide, (ri + 1) * wide)
        other = slice((1 - ri) * wide, (2 - ri) * wide)
        for to, part in ((shi, hi), (slo, lo)):
            to[:half_h, own] = part
            to[half_h:, other] = part if ri == 0 else -part
    for ri in range(2):
        n = slice(ri * wide, (ri + 1) * wide)
        y[ri] = (
            jnp.dot(wlo_ref[...], shi[:, n], preferred_element_type=jnp.float32)
            + jnp.dot(whi_ref[...], slo[:, n], preferred_element_type=jnp.float32)
        ) + jnp.dot(whi_ref[...], shi[:, n], preferred_element_type=jnp.float32)
    period = y.shape[1]
    step_rows = FINE
    fine_c, fine_d = phase_ref[:FINE, :TILE], phase_ref[:FINE, TILE:]
    for b in range(period // step_rows):
        at = slice(b * step_rows, (b + 1) * step_rows)
        big_c = phase_ref[FINE + b : FINE + b + 1, :TILE]
        big_d = phase_ref[FINE + b : FINE + b + 1, TILE:]
        c = big_c * fine_c - big_d * fine_d
        d = big_d * fine_c + big_c * fine_d
        for s in range(most):
            lanes = slice(s * TILE, (s + 1) * TILE)
            yr = y[0, at, lanes]
            yi = y[1, at, lanes]
            for ri, z in enumerate((c * yr - d * yi, d * yr + c * yi)):
                to = slice((ri * most + s) * TILE, (ri * most + s + 1) * TILE)
                hi = z.astype(jnp.bfloat16)
                zhi[at, to] = hi
                zlo[at, to] = (z - hi.astype(jnp.float32)).astype(jnp.bfloat16)
    copy.wait()
    t = t_ref[...]
    sums[...] = jnp.dot(zlo[...], t, preferred_element_type=jnp.float32) + jnp.dot(
        zhi[...], t, preferred_element_type=jnp.float32
    )
    half = parts.shape[1]
    big = None
    first = lax.broadcasted_iota(jnp.int32, (half, TILE), 1) < TILE // 2
    for dest in range(n_seg):
        lag = dest * 2 * half
        r, l0 = lag // period, lag % period
        col = slice(r // 2 * TILE, (r // 2 + 1) * TILE)
        low = sums[l0 : l0 + half, col]
        high = sums[l0 + half : l0 + 2 * half, col]
        if r % 2 == 0:
            high = pltpu.roll(high, TILE // 2, 1)
        else:
            low = pltpu.roll(low, TILE // 2, 1)
        part = jnp.where(first, low, high)
        parts[dest] = part
        part = jnp.max(jnp.abs(part), axis=0, keepdims=True)
        big = part if big is None else jnp.maximum(big, part)
    top = top_exponent(jnp.max(big, keepdims=True))
    for k in range(n_seg):
        part = parts[jnp.bitwise_xor(me_ref[0], k)]
        outs[k][: half // 2, :] = encode(part[: half // 2], part[half // 2 :], top)
        outs[k][half // 2 :, :] = jnp.broadcast_to(top, (8, TILE)).astype(jnp.int32)


def sums_kernel(most, turns, shift, out_ref, t_ref, sem):
    shape = (most * TILE, turns * most * CC)
    row = lax.broadcasted_iota(jnp.int32, shape, 0)
    col = lax.broadcasted_iota(jnp.int32, shape, 1)
    same = (row // TILE == col // CC % most) & (row % CC == col % CC)
    fb = row // CC % GROUPS
    eighths = (col // (most * CC) - shift) * fb
    one = jnp.where(fb % 2 == 0, 1.0, ODD)
    for ri in range(2):
        e = jnp.bitwise_and(eighths + 2 * ri, 7)
        size = jnp.where(e % 4 == 2, 0.0, jnp.where(e % 2 == 0, one, ODD_DIAGONAL))
        t = jnp.where(same, jnp.where((e > 2) & (e < 6), -size, size), 0.0)
        t_ref[ri * most * TILE : (ri + 1) * most * TILE, :] = t.astype(jnp.bfloat16)
    copy = pltpu.make_async_copy(
        t_ref, out_ref.at[pl.ds(0, t_ref.shape[0])], sem.at[0]
    )
    copy.start()
    copy.wait()


def make_sums(freq, most):
    period = 2 * (freq // GROUPS)
    turns = LAG // period
    width = turns * most * CC
    return pl.pallas_call(
        functools.partial(sums_kernel, most, turns, LAG // 2 // period),
        out_shape=jax.ShapeDtypeStruct((96 << 10, width), jnp.bfloat16),
        out_specs=pl.BlockSpec(memory_space=pltpu.HBM),
        scratch_shapes=[
            pltpu.VMEM((2 * most * TILE, width), jnp.bfloat16),
            pltpu.SemaphoreType.DMA((1,)),
        ],
        name="sums",
        cost_estimate=SMALL,
    )()


def make_tables(freq):
    h = freq // GROUPS
    period = 2 * h
    angle = np.arange(period)[:, None] * np.arange(h)[None, :] % period
    angle = angle * (2.0 * math.pi / period)
    w = np.concatenate([np.cos(angle), np.sin(angle)], 1).astype(np.float32)
    whi = w.astype(jnp.bfloat16)
    wlo = (w - whi.astype(np.float32)).astype(jnp.bfloat16)
    fb = np.arange(TILE) // CC
    scale = np.where(fb % 2 == 0, 1.0, 1.0 / ODD) / math.sqrt(freq)
    parts = []
    for at, gain in ((np.arange(FINE), scale), (np.arange(0, period, FINE), 1.0)):
        angle = (at[:, None] * fb[None, :] % (2 * freq)) * (math.pi / freq)
        parts.append(np.concatenate([np.cos(angle) * gain, np.sin(angle) * gain], 1))
    phase = np.concatenate(parts).astype(np.float32)
    return [jnp.asarray(c) for c in (np.concatenate([whi, wlo]), phase)]


def dft(me, tables, blocks, freq, n_seg, n_pair, most):
    period = 2 * (freq // GROUPS)
    smem = pl.BlockSpec(memory_space=pltpu.SMEM)
    vmem = pl.BlockSpec(memory_space=pltpu.VMEM)
    half = LAG // n_seg // 2
    wide = most * TILE
    return pl.pallas_call(
        functools.partial(dft_kernel, n_seg, n_pair, most),
        out_shape=[jax.ShapeDtypeStruct((half // 2 + 8, TILE), jnp.int32)] * n_seg,
        in_specs=[smem, vmem, vmem, pl.BlockSpec(memory_space=pltpu.HBM)]
        + [vmem] * len(blocks),
        out_specs=[vmem] * n_seg,
        scratch_shapes=[
            pltpu.VMEM((2 * wide, LAG // period * most * CC), jnp.bfloat16),
            pltpu.SemaphoreType.DMA((1,)),
            pltpu.VMEM((2, period // 2, wide), jnp.float32),
            pltpu.VMEM((period, 2 * wide), jnp.bfloat16),
            pltpu.VMEM((period, 2 * wide), jnp.bfloat16),
            pltpu.VMEM((2, period, wide), jnp.float32),
            pltpu.VMEM((period, 2 * wide), jnp.bfloat16),
            pltpu.VMEM((period, 2 * wide), jnp.bfloat16),
            pltpu.VMEM((period, LAG // period * most * CC), jnp.float32),
            pltpu.VMEM((n_seg, half, TILE), jnp.float32),
        ],
        name="dft",
        compiler_params=pltpu.CompilerParams(vmem_limit_bytes=24 << 20),
        cost_estimate=SMALL,
    )(me, *tables, *blocks)


def unpack_kernel(n_seg, chunks, most, me_ref, *refs):
    ins = refs[: n_seg * chunks]
    out_ref, buf = refs[n_seg * chunks :]
    half = buf.shape[1]

    @pl.when(pl.program_id(0) == 0)
    def _():
        for k in range(n_seg):
            z = jnp.bitwise_xor(me_ref[0], k)
            for ch in range(chunks):
                src = ins[ch * n_seg + n_seg - 1 - k]
                top = src[half // 2 : half // 2 + 1, :].astype(jnp.float32)
                low, high = decode(src[: half // 2, :], top)
                buf[z * chunks + ch, : half // 2] = low
                buf[z * chunks + ch, half // 2 :] = high

    step_rows = 16
    block = out_ref.shape[1]
    for b in range(block // step_rows):
        at = pl.multiple_of(pl.program_id(0) * block + b * step_rows, step_rows)
        v = transpose_groups([buf[i, pl.ds(at, step_rows), :] for i in range(GROUPS)])
        for h in range(2):
            for s in range(most):
                out_ref[h, b * step_rows : (b + 1) * step_rows, s, :] = v[h * most + s]


def unpack(me, parts, n_seg, chunks, most):
    half = 2 * (parts[0].shape[0] - 8)
    steps = 4
    smem = pl.BlockSpec(memory_space=pltpu.SMEM)
    whole = pl.BlockSpec(parts[0].shape, lambda b: (0, 0))
    out = pl.pallas_call(
        functools.partial(unpack_kernel, n_seg, chunks, most),
        out_shape=jax.ShapeDtypeStruct((2, half, most, TILE), jnp.float32),
        grid=(steps,),
        in_specs=[smem] + [whole] * len(parts),
        out_specs=pl.BlockSpec((2, half // steps, most, TILE), lambda b: (0, b, 0, 0)),
        scratch_shapes=[pltpu.VMEM((GROUPS, half, TILE), jnp.float32)],
        name="unpack",
        compiler_params=pltpu.CompilerParams(vmem_limit_bytes=12 << 20),
        cost_estimate=SMALL,
    )(me, *parts)
    return out.reshape(2 * half, most, TILE)


def exchange(blocks, axis, size):
    got = {
        k: lax.ppermute(blocks[k], axis, [(i, i ^ k) for i in range(size)])
        for k in reversed(range(1, size))
    }
    return [blocks[0]] + [got[k] for k in range(1, size)]


def exchange_plane(blocks, n_pair, between=None):
    direct = [blocks[0]] + [
        lax.ppermute(blocks[k], "pair", [(i, i ^ (2 * k)) for i in range(n_pair)])
        for k in range(1, n_pair // 2)
    ]
    if between is not None:
        far, _ = lax.optimization_barrier((direct[1:], between))
        direct = [direct[0]] + list(far)
    swap = [(i, i ^ 1) for i in range(n_pair)]
    return direct + [lax.ppermute(d, "pair", swap) for d in direct]


def body(spectra, pair_lists, pair_counts):
    n_pair = lax.axis_size("pair")
    n_seg = lax.axis_size("seg")
    freq = spectra.shape[2]
    most = pair_lists.shape[0]
    tiles = spectra.shape[3] // TILE
    chunks = GROUPS // n_seg
    rows = freq // n_pair // GROUPS
    me = jnp.stack([lax.axis_index("seg"), lax.axis_index("pair")]).astype(jnp.int32)
    x = spectra.reshape(2, freq, spectra.shape[3])
    lists = jnp.concatenate([pair_lists.reshape(-1), pair_counts])
    sums = make_sums(freq, most)
    tables = make_tables(freq) + [sums]
    packed = [pack(x, chunk, n_seg, n_pair) for chunk in range(chunks)]
    lists, packed[-1] = lax.optimization_barrier((lists, packed[-1]))
    table = lax.all_gather(lists, "pair", axis=0)
    if chunks > 1:
        table, packed[1], _ = lax.optimization_barrier((table, packed[1], sums))
    done, parts = [], []
    lags = None
    for sent in packed:
        got = lax.all_to_all(
            sent.reshape(n_seg * n_pair, tiles, 2, rows, TILE),
            ("seg", "pair"),
            split_axis=0,
            concat_axis=0,
            tiled=True,
        )
        if lags is not None:
            got, _ = lax.optimization_barrier((got, lags))
        spec = got.reshape(n_seg, n_pair * tiles, 2, rows, TILE)
        stack = stacks(me, table, spec, n_seg, n_pair, most)
        blocks = exchange_plane(stack, n_pair, done[2:0:-1] or None)
        lags = dft(me, tables, blocks, freq, n_seg, n_pair, most)
        done = exchange(lags, "seg", n_seg)
        parts += done[::-1]
    return unpack(me, parts, n_seg, chunks, most)


def solution(mesh):
    return jax.shard_map(
        body,
        mesh=mesh,
        in_specs=(P("seg", None, None, "pair"), P("pair", None), P("pair")),
        out_specs=P("seg", "pair", None),
        check_vma=False,
    )
```
